128 devices in a mesh: depth: 4 (over y_lo, core), freq: 32 (over y_hi, z, x).
Axes of the slice: x: 4, y: 4 (y_hi: 2, y_lo: 2; y = y_hi * 2 + y_lo), z: 4, core: 2. Of those that a mesh axis runs over, the one named last changes fastest.
Arguments:
- source_top: bfloat16 [2, 32, 2, 512, 512], P(None, 'freq'), may hold values from -6 to 6
- receiver_top: bfloat16 [2, 32, 2, 512, 512], P(None, 'freq'), may hold values from -6 to 6
- slowness_codes: int32 [4, 1024, 1024], P('depth'), may hold values from 0 to 31
- slowness_table: float32 [32], replicated, may hold values from 0.8 to 1.25
- anchors: int32 [2, 2], replicated, may hold values from 0 to 512, as said below
Outputs:
- image: float32 [4, 15, 512, 512], P('depth', None, 'freq')
The draws below stay inside these ranges and needn't reach their ends.
Inputs may be any that keep to these rules, and one draw needn't show every extreme that they name: `anchors`: each of the two coordinates is 0 for some shot and 512 for another.
All inputs are finite; a program needn't handle non-finite values.
Results may differ from the reference program's by a relative error of at most 0.03.
Values may be sent and summed in bfloat16 or wider, within the bound.
A program may use at most 192 MiB of HBM per device.

```python
import math
import jax
import jax.numpy as jnp
from jax import lax

NX = 512
NY = 512
MX = 1024
NCODE = 32
LAG = 7
SHOTS = 2
FREQS = 32
NZ = 4


def draw_anchors(key, part):
    key_base, key_first, key_second = jax.random.split(jax.random.fold_in(key, 7), 3)
    corners = jax.random.randint(key_base, (SHOTS, 2), 0, MX - NX + 1)
    order_first = jax.random.permutation(key_first, SHOTS)
    order_second = jax.random.permutation(key_second, SHOTS)
    corners = corners.at[order_first[0], 0].set(0)
    corners = corners.at[order_first[1], 0].set(MX - NX)
    corners = corners.at[order_second[0], 1].set(0)
    corners = corners.at[order_second[1], 1].set(MX - NX)
    return corners.astype(jnp.int32)


def plant(drawn, own_key, least, top_value):
    longest = drawn.shape.index(max(drawn.shape))
    spots = []
    for shift in (0, 1):
        where = [jax.random.randint(jax.random.fold_in(own_key, axis), (), 0, length) for axis, length in enumerate(drawn.shape)]
        where[longest] = (where[longest] + shift) % drawn.shape[longest]
        spots.append(tuple(where))
    return drawn.at[spots[0]].set(least).at[spots[1]].set(top_value)


def level_of(own_key, extent, shards, least, largest):
    level, own = 1.0, jax.random.fold_in(own_key, 6)
    for dim, shards_of in shards:
        steps = jnp.exp(jax.random.uniform(jax.random.fold_in(own, dim), (shards_of,), jnp.float32, least / len(shards), largest / len(shards)))
        level = level * jnp.repeat(steps, extent[dim] // shards_of).reshape([-1 if axis == dim else 1 for axis in range(len(extent))])
    return level


def scatter_about(stream_key, extent, deviation, bound, cuts=(), kind=jnp.bfloat16):
    level = level_of(stream_key, extent, cuts, -0.22, 0.18) if cuts else 1.0
    drawn = jax.random.normal(stream_key, extent, jnp.float32) * deviation * level
    return jnp.minimum(jnp.maximum(drawn, -bound), bound).astype(kind)


def setup_inputs(seed: int = 0) -> dict:
    arg_keys = jax.random.split(jax.random.key(seed), 6)
    source_top = scatter_about(arg_keys[0], (SHOTS, FREQS, 2, NX, NY), 1.0, 6.0, ((1, 32),))
    receiver_top = scatter_about(arg_keys[1], (SHOTS, FREQS, 2, NX, NY), 1.0, 6.0, ((1, 32),))
    slowness_codes = plant(jax.random.randint(arg_keys[2], (NZ, MX, MX), 0, NCODE), jax.random.fold_in(arg_keys[2], 1), 0, NCODE - 1).astype(jnp.int32)
    slowness_table = jnp.clip(jax.random.uniform(arg_keys[3], (NCODE,), jnp.float32, 0.8, 1.25), 0.8, 1.25)
    anchors = draw_anchors(jax.random.fold_in(arg_keys[5], 71), 0)
    return dict(source_top=source_top, receiver_top=receiver_top, slowness_codes=slowness_codes, slowness_table=slowness_table, anchors=anchors)


def transform_tables(length):
    position = jnp.arange(length, dtype=jnp.int32)
    product = position[:, None] * position[None, :] % length
    angles = product.astype(jnp.float32) * (2.0 * math.pi / length)
    factor = 1.0 / math.sqrt(length)
    return (jnp.cos(angles) * factor, jnp.sin(angles) * factor)

def build_tables(len_x, len_y):
    cos_x, sin_x = transform_tables(len_x)
    cos_y, sin_y = transform_tables(len_y)
    fwd_x = jnp.stack([jnp.stack([cos_x, sin_x]), jnp.stack([-sin_x, cos_x])]).astype(jnp.bfloat16)
    inv_x = jnp.stack([jnp.stack([cos_x, -sin_x]), jnp.stack([sin_x, cos_x])]).astype(jnp.bfloat16)
    fwd_y = jnp.stack([jnp.stack([cos_y, -sin_y], axis=1), jnp.stack([sin_y, cos_y], axis=1)]).astype(jnp.bfloat16)
    inv_y = jnp.stack([jnp.stack([cos_y, sin_y], axis=1), jnp.stack([-sin_y, cos_y], axis=1)]).astype(jnp.bfloat16)
    return (fwd_x, inv_x, fwd_y, inv_y)

def wavenumbers(length):
    position = jnp.arange(length, dtype=jnp.int32)
    signed = jnp.where(position < length // 2, position, position - length)
    return signed.astype(jnp.float32) * (2.0 * math.pi / length)

def aperture_slowness(code_plane, slowness_table, corner, rows_x, rows_y):
    window = lax.dynamic_slice(code_plane, (corner[0].astype(jnp.int32), corner[1].astype(jnp.int32)), (rows_x, rows_y))
    levels = jnp.arange(slowness_table.shape[0], dtype=jnp.int32)
    return lax.optimization_barrier(jnp.sum(jnp.where(window[None] == levels[:, None, None], slowness_table[:, None, None], 0.0), axis=0))

def propagators(slowness, angular, wave_x, wave_y):
    mean_slowness = jnp.mean(slowness)
    vertical = (angular * mean_slowness) ** 2 - wave_x[:, None] ** 2 - wave_y[None, :] ** 2
    travel = jnp.sqrt(jnp.maximum(vertical, 0.0))
    damping = jnp.exp(-jnp.sqrt(jnp.maximum(-vertical, 0.0)))
    screen_angle = angular * (slowness - mean_slowness)
    return (damping * jnp.cos(travel), damping * jnp.sin(travel), jnp.cos(screen_angle), jnp.sin(screen_angle))

def advance(fields, tables, operators):
    fwd_x, inv_x, fwd_y, inv_y = tables
    conjugate = jnp.array([1.0, -1.0], jnp.float32)[None, :, None, None]
    across_x = jnp.einsum('pqxu,gfquy->gfpxy', fwd_x.astype(jnp.float32), fields.astype(jnp.float32)).astype(jnp.bfloat16)
    second = jnp.einsum('gfqxu,qupb->gfxpb', across_x.astype(jnp.float32), fwd_y.astype(jnp.float32))
    real_part = second[:, :, :, 0]
    imag_part = second[:, :, :, 1]
    phase_re = operators[0][:, None]
    phase_im = operators[1][:, None] * conjugate
    shifted = jnp.stack([real_part * phase_re - imag_part * phase_im, real_part * phase_im + imag_part * phase_re], axis=3).astype(jnp.bfloat16)
    back_y = jnp.einsum('gfxqu,qupb->gfxpb', shifted.astype(jnp.float32), inv_y.astype(jnp.float32)).astype(jnp.bfloat16)
    fourth = jnp.einsum('pqxu,gfuqy->gfpxy', inv_x.astype(jnp.float32), back_y.astype(jnp.float32))
    real_part = fourth[:, :, 0]
    imag_part = fourth[:, :, 1]
    turn_re = operators[2][:, None]
    turn_im = operators[3][:, None] * conjugate
    return jnp.stack([real_part * turn_re - imag_part * turn_im, real_part * turn_im + imag_part * turn_re], axis=2).astype(jnp.bfloat16)

def correlate(source, receiver, row_count):
    lag_terms = []
    for offset in range(-LAG, LAG + 1):
        shifted_source = source[:, :, :, LAG - offset:LAG - offset + row_count].astype(jnp.float32)
        shifted_receiver = receiver[:, :, :, LAG + offset:LAG + offset + row_count].astype(jnp.float32)
        lag_terms.append(lax.optimization_barrier(jnp.sum(shifted_source * shifted_receiver, axis=(1, 2))))
    return jnp.stack(lag_terms, axis=1)

def reference(source_top, receiver_top, slowness_codes, slowness_table, anchors):
    tables = build_tables(NX, NY)
    wave_x = wavenumbers(NX)
    wave_y = wavenumbers(NY)
    freq_total = source_top.shape[1]
    factor = 1.0 / math.sqrt(2.0 * SHOTS * freq_total)

    def one_shot(image_sum, shot_index):
        corner = anchors[shot_index]

        def one_freq(image_acc, freq_index):
            angular = math.pi * (0.45 + 0.5 * (freq_index.astype(jnp.float32) + 0.5) / freq_total)
            angular = jnp.reshape(angular, (1, 1, 1))
            fields = jnp.stack([source_top[shot_index, freq_index], receiver_top[shot_index, freq_index]])[None]

            def one_plane(current, code_plane):
                slowness = aperture_slowness(code_plane, slowness_table, corner, NX, NY)
                operators = propagators(slowness, angular, wave_x, wave_y)
                current = advance(current, tables, operators)
                padded = jnp.pad(current[0], ((0, 0), (0, 0), (LAG, LAG), (0, 0)))
                lag_image = correlate(padded[0][None, None], padded[1][None, None], NX)[0]
                return (current, lag_image)
            unused, lag_images = lax.scan(one_plane, fields, slowness_codes)
            return (image_acc + lag_images, None)
        image_sum, unused = lax.scan(one_freq, image_sum, jnp.arange(freq_total, dtype=jnp.int32))
        return (image_sum, None)
    image_sum = jnp.zeros((NZ, 2 * LAG + 1, NX, NY), jnp.float32)
    image_sum, unused = lax.scan(one_shot, image_sum, jnp.arange(SHOTS, dtype=jnp.int32))
    return image_sum * factor
```

```python
import functools
import math

import jax
import jax.numpy as jnp
import numpy as np
from jax import lax
from jax.experimental import pallas as pl
from jax.experimental.pallas import tpu as pltpu
from jax.sharding import PartitionSpec as P

LAG = 7
LAGS = 2 * LAG + 1
N = 512
B = 128
GROUPS = 5
PER = LAGS // GROUPS
MESH = pl.DeviceIdType.MESH
F32 = jnp.float32
BF16 = jnp.bfloat16


def butterfly_matrices():
    j = np.arange(B)[:, None]
    k = np.arange(B)[None, :]
    mats = []
    for wave in (4 * k, 4 * k + 1, 4 * k + 2, -(4 * k + 1)):
        angle = 2.0 * np.pi * ((j * wave) % N) / N
        c = np.cos(angle) / math.sqrt(N)
        s = np.sin(angle) / math.sqrt(N)
        mats.append(np.block([[c, -s], [s, c]]))
    right = np.stack(mats)
    return right, np.swapaxes(right, 1, 2)


def even_poly(first, terms, top, samples=400):
    q = (np.cos(np.pi * (np.arange(samples) + 0.5) / samples) + 1.0) * 0.5 * top
    r = np.sqrt(q)
    want = np.cos(r) if first == 0 else np.sin(r) / r
    fit = np.polynomial.Chebyshev.fit(q, want, terms, domain=[0, top])
    return [float(v) for v in fit.convert(kind=np.polynomial.Polynomial).coef]


COS_Q = even_poly(0, 9, 14.0)
SIN_Q = even_poly(1, 9, 14.0)


def horner(coefs, q):
    value = coefs[-1] * q + coefs[-2]
    for c in coefs[-3::-1]:
        value = value * q + c
    return value


def split4(re, im):
    er, ei, dr, di = re[0] + re[2], im[0] + im[2], re[0] - re[2], im[0] - im[2]
    fr, fi, gr, gi = re[1] + re[3], im[1] + im[3], re[1] - re[3], im[1] - im[3]
    return (er + fr, dr + gi, er - fr, dr - gi), (ei + fi, di - gr, ei - fi, di + gr)


def join4(re, im):
    er, ei, dr, di = re[0] + re[2], im[0] + im[2], re[0] - re[2], im[0] - im[2]
    fr, fi, gr, gi = re[1] + re[3], im[1] + im[3], re[1] - re[3], im[1] - im[3]
    return (er + fr, dr - gi, er - fr, dr + gi), (ei + fi, di + gr, ei - fi, di - gr)


def fields_kernel(
    src, rec, codes, table, right_ref, left_ref, out,
    u, a, cbuf, ph, sc, tsem, csem, osem,
):
    depth = lax.axis_index("depth")
    core = depth % 2
    first_plane = (depth // 2) * 2
    steps = first_plane + 2
    position = lax.axis_index("freq").astype(F32)
    angular = math.pi * (0.45 + 0.5 * (position + 0.5) / 32.0)

    tops = []
    for kind, top in enumerate((src, rec)):
        for q in range(4):
            tops.append(pltpu.make_async_copy(
                top.at[core, 0, :, :, pl.ds(q * B, B)], u.at[kind, :, q], tsem.at[kind, q]))
    for copy in tops:
        copy.start()
    for z in range(4):
        pltpu.make_async_copy(codes.at[z, core], cbuf.at[z], csem.at[z]).start()

    lane = lax.broadcasted_iota(jnp.int32, (8, B), 1)
    levels = jnp.zeros((8, B), F32)
    for k in range(32):
        levels = jnp.where(lane == k, table[k], levels)

    def lookup(values, index):
        return jnp.take_along_axis(jnp.tile(values, (index.shape[0] // 8, 1)), index, axis=1)

    for copy in tops:
        copy.wait()

    def step(z, carry):
        pltpu.make_async_copy(codes.at[z, core], cbuf.at[z], csem.at[z]).wait()

        def add_rows(i, total):
            for q in range(4):
                index = cbuf[z, pl.ds(i * 32, 32), q * B:(q + 1) * B].astype(jnp.int32)
                got = lookup(levels, index)
                total = total + (got[0:8] + got[8:16]) + (got[16:24] + got[24:32])
            return total

        total = lax.fori_loop(0, N // 32, add_rows, jnp.zeros((8, B), F32))
        base = jnp.sum(total) * (1.0 / (N * N))

        def phase_block(n, carry):
            rx, ry = n // 3, n % 3
            kx = lax.broadcasted_iota(jnp.int32, (B, B), 0) * 4 + rx
            ky = lax.broadcasted_iota(jnp.int32, (B, B), 1) * 4 + ry
            kx = jnp.where(kx < N // 2, kx, kx - N).astype(F32) * (2.0 * math.pi / N)
            ky = jnp.where(ky < N // 2, ky, ky - N).astype(F32) * (2.0 * math.pi / N)
            q = (angular * base) ** 2 - kx * kx - ky * ky
            root = jnp.sqrt(jnp.abs(q))
            decay = jnp.exp(-root)
            wave = jnp.maximum(q, 0.0)
            ph[0, rx, ry] = jnp.where(q >= 0.0, horner(COS_Q, wave), decay)
            ph[1, rx, ry] = jnp.where(q >= 0.0, root * horner(SIN_Q, wave), 0.0)
            return carry

        lax.fori_loop(0, 9, phase_block, 0)

        angle = angular * (levels - base)
        squared = angle * angle
        cos_levels = horner(COS_Q, squared)
        sin_levels = angle * horner(SIN_Q, squared)

        def screen_rows(i, carry):
            rows = pl.ds(i * 32, 32)
            for q in range(4):
                index = cbuf[z, rows, q * B:(q + 1) * B].astype(jnp.int32)
                sc[0, q, rows, :] = lookup(cos_levels, index)
                sc[1, q, rows, :] = lookup(sin_levels, index)
            return carry

        lax.fori_loop(0, N // 32, screen_rows, 0)

        def wide(ref, kind, p, half, block):
            rows = slice(block * B, (block + 1) * B)
            return jnp.concatenate([ref[kind, p, half * 2, rows, :], ref[kind, p, half * 2 + 1, rows, :]], axis=1)

        def put_wide(ref, kind, p, half, block, value):
            rows = slice(block * B, (block + 1) * B)
            ref[kind, p, half * 2, rows, :] = value[:, :B]
            ref[kind, p, half * 2 + 1, rows, :] = value[:, B:]

        def forward_x(n, carry):
            kind, half = n // 2, n % 2
            re = [wide(u, kind, 0, half, q) for q in range(4)]
            im = [wide(u, kind, 1, half, q) for q in range(4)]
            sre, sim = split4(re, im)
            for r in range(4):
                got = jnp.dot(left_ref[r], jnp.concatenate([sre[r], sim[r]], axis=0),
                              preferred_element_type=F32).astype(BF16)
                put_wide(a, kind, 0, half, r, got[:B])
                put_wide(a, kind, 1, half, r, got[B:])
            return carry

        lax.fori_loop(0, 4, forward_x, 0)

        def along_y(n, carry):
            kind, rx = n // 4, n % 4
            sign = (1 - 2 * kind).astype(F32)
            px = jnp.where(rx == 3, 1, rx)
            rows = pl.ds(pl.multiple_of(rx * B, B), B)
            re = [a[kind, 0, q, rows, :] for q in range(4)]
            im = [a[kind, 1, q, rows, :] for q in range(4)]
            sre, sim = split4(re, im)
            tre, tim = [], []
            for r in range(4):
                got = jnp.dot(jnp.concatenate([sre[r], sim[r]], axis=1), right_ref[r],
                              preferred_element_type=F32)
                gre, gim = got[:, :B], got[:, B:]
                py = 1 if r == 3 else r
                pre, pim = ph[0, px, py], ph[1, px, py] * sign
                turned = jnp.concatenate(
                    [(gre * pre - gim * pim).astype(BF16), (gre * pim + gim * pre).astype(BF16)], axis=1)
                back = jnp.dot(turned, left_ref[r], preferred_element_type=F32)
                tre.append(back[:, :B])
                tim.append(back[:, B:])
            cre, cim = join4(tre, tim)
            for q in range(4):
                a[kind, 0, q, rows, :] = cre[q].astype(BF16)
                a[kind, 1, q, rows, :] = cim[q].astype(BF16)
            return carry

        lax.fori_loop(0, 8, along_y, 0)

        @pl.when(z > first_plane)
        def _():
            pltpu.make_async_copy(u, out.at[0], osem.at[0]).wait()

        def inverse_x(n, carry):
            kind, half = n // 2, n % 2
            sign = (1 - 2 * kind).astype(F32)
            tre, tim = [], []
            for r in range(4):
                data = jnp.concatenate([wide(a, kind, 0, half, r), wide(a, kind, 1, half, r)], axis=0)
                got = jnp.dot(right_ref[r], data, preferred_element_type=F32)
                tre.append(got[:B])
                tim.append(got[B:])
            xre, xim = join4(tre, tim)
            for q in range(4):
                rows = slice(q * B, (q + 1) * B)
                for part in range(2):
                    cols = slice(part * B, (part + 1) * B)
                    cre = sc[0, half * 2 + part, rows, :]
                    cim = sc[1, half * 2 + part, rows, :] * sign
                    gre, gim = xre[q][:, cols], xim[q][:, cols]
                    u[kind, 0, half * 2 + part, rows, :] = (gre * cre - gim * cim).astype(BF16)
                    u[kind, 1, half * 2 + part, rows, :] = (gre * cim + gim * cre).astype(BF16)
            return carry

        lax.fori_loop(0, 4, inverse_x, 0)

        @pl.when(z == first_plane)
        def _():
            pltpu.make_async_copy(u, out.at[0], osem.at[0]).start()

        @pl.when(z == first_plane + 1)
        def _():
            pltpu.make_async_copy(u, out.at[1], osem.at[1]).start()

        return carry

    lax.fori_loop(0, steps, step, 0)

    def drain(z, carry):
        pltpu.make_async_copy(codes.at[z, core], cbuf.at[z], csem.at[z]).wait()
        return carry

    lax.fori_loop(steps, 4, drain, 0)
    pltpu.make_async_copy(u, out.at[1], osem.at[1]).wait()


def make_fields(src, rec, codes, table, right, left):
    vmem = pl.BlockSpec(memory_space=pltpu.VMEM)
    hbm = pl.BlockSpec(memory_space=pl.ANY)
    return pl.pallas_call(
        fields_kernel,
        out_shape=jax.ShapeDtypeStruct((2, 2, 2, 4, N, B), BF16),
        in_specs=[hbm, hbm, hbm, pl.BlockSpec(memory_space=pltpu.SMEM), vmem, vmem],
        out_specs=hbm,
        scratch_shapes=[
            pltpu.VMEM((2, 2, 4, N, B), BF16),
            pltpu.VMEM((2, 2, 4, N, B), BF16),
            pltpu.VMEM((4, N, N), BF16),
            pltpu.VMEM((2, 3, 3, B, B), F32),
            pltpu.VMEM((2, 4, N, B), F32),
            pltpu.SemaphoreType.DMA((2, 4)),
            pltpu.SemaphoreType.DMA((4,)),
            pltpu.SemaphoreType.DMA((2,)),
        ],
        compiler_params=pltpu.CompilerParams(vmem_limit_bytes=60 * 1024 * 1024),
        name="fields",
    )(src, rec, codes, table, right, left)


def image_kernel(factor, fields, out, own, other, pad, buf, r0, r1, r2, r3, r4,
                 lsem, ssem, rsem, xs, xr):
    depth = lax.axis_index("depth")
    freq = lax.axis_index("freq")
    core = depth % 2
    x, z, yh = freq % 4, (freq // 4) % 4, freq // 16
    base = yh * 16 + z * 4 + x
    sibling = (depth + 1 - 2 * core, freq)
    dims = (
        (depth, base - x + (x + 1 - 2 * (x % 2))),
        (depth, base - x + (3 - x)),
        (depth, base - 4 * z + 4 * (z + 1 - 2 * (z % 2))),
        (depth, base - 4 * z + 4 * (3 - z)),
    )
    across = (depth, base - 16 * yh + 16 * (1 - yh))

    barrier = pltpu.get_barrier_semaphore()
    for who in (sibling, across) + dims:
        pl.semaphore_signal(barrier, inc=1, device_id=who, device_id_type=MESH)
    local = pltpu.make_async_copy(fields.at[core], own, lsem)
    local.start()
    pl.semaphore_wait(barrier, 6)
    swap = pltpu.make_async_remote_copy(
        src_ref=fields.at[1 - core], dst_ref=other, send_sem=xs, recv_sem=xr,
        device_id=sibling, device_id_type=MESH)
    swap.start()

    for s in range(2):
        for k in range(2):
            for p in range(2):
                for i in range(4):
                    pad[s, k, p, i, 0:8, :] = jnp.zeros((8, B), F32)
                    pad[s, k, p, i, N + 8:N + 16, :] = jnp.zeros((8, B), F32)

    def widen(s, ref):
        def body(n, carry):
            k, p, i = n // 8, (n // 4) % 2, n % 4
            for h in range(2):
                pad[s, k, p, i, 8 + h * 256:8 + (h + 1) * 256, :] = ref[k, p, i, h * 256:(h + 1) * 256, :].astype(F32)
            return carry
        lax.fori_loop(0, 16, body, 0)

    local.wait()
    widen(0, own)
    swap.wait()
    widen(1, other)

    def bits(ix, iz):
        return [((ix + 1) // 2) % 2, ix // 2, ((iz + 1) // 2) % 2, iz // 2]

    mine = bits(x, z)

    def produce(g):
        def body(n, carry):
            i, f = n // 32, n % 32
            theirs = bits(f % 4, (f // 4) % 4)
            rel = [(m + t) % 2 for m, t in zip(mine, theirs)]
            ybit = (yh + f // 16) % 2
            slot = ybit
            for t in range(4):
                d = (i + t) % 4
                pick = jnp.where(d == 0, rel[0], jnp.where(d == 1, rel[1], jnp.where(d == 2, rel[2], rel[3])))
                slot = slot + pick * (16 >> t)
            row = f * 16
            for l in range(PER):
                h = g * PER + l - LAG
                total = None
                for s in range(2):
                    for p in range(2):
                        left = pad[s, 0, p, i, pl.ds(row + (8 - h), 16), :]
                        right = pad[s, 1, p, i, pl.ds(row + (8 + h), 16), :]
                        term = left * right
                        total = term if total is None else total + term
                buf[g, i, slot, l] = total.astype(BF16)
            return carry
        lax.fori_loop(0, 128, body, 0)

    recv = (r0, r1, r2, r3, r4)

    def copy(g, i, t):
        half = 16 >> t
        who = across if t == 4 else dims[(i + t) % 4]
        return pltpu.make_async_remote_copy(
            src_ref=buf.at[g, i, pl.ds(half, half)], dst_ref=recv[t].at[g, i],
            send_sem=ssem.at[g, i, t], recv_sem=rsem.at[g, i, t],
            device_id=who, device_id_type=MESH)

    def arrive(g, i, t):
        copy(g, i, t).wait_recv()
        half = 16 >> t

        if t < 4:
            def body(n, carry):
                k = half - 1 - n
                buf[g, i, k] = buf[g, i, k] + recv[t][g, i, k]
                return carry
            lax.fori_loop(0, half, body, 0)
            copy(g, i, t + 1).start()
        else:
            total = buf[g, i, 0].astype(F32) + recv[4][g, i, 0].astype(F32)
            out[g * PER:(g + 1) * PER, :, i * B:(i + 1) * B] = total * factor

    for g in range(GROUPS):
        produce(g)
        for i in range(4):
            copy(g, i, 0).start()
    for w in range(GROUPS + 4):
        for t in range(4, -1, -1):
            g = w - t
            if 0 <= g < GROUPS:
                for i in range(4):
                    arrive(g, i, t)
    for g in range(GROUPS):
        for i in range(4):
            for t in range(5):
                copy(g, i, t).wait_send()


def make_image(fields, factor):
    hbm = pl.BlockSpec(memory_space=pl.ANY)
    strip = (PER, 16, B)
    return pl.pallas_call(
        functools.partial(image_kernel, factor),
        out_shape=jax.ShapeDtypeStruct((LAGS, 16, N), F32),
        in_specs=[hbm],
        out_specs=pl.BlockSpec(memory_space=pltpu.VMEM),
        scratch_shapes=[
            pltpu.VMEM((2, 2, 4, N, B), BF16),
            pltpu.VMEM((2, 2, 4, N, B), BF16),
            pltpu.VMEM((2, 2, 2, 4, N + 16, B), F32),
            pltpu.VMEM((GROUPS, 4, 32) + strip, BF16),
            pltpu.VMEM((GROUPS, 4, 16) + strip, BF16),
            pltpu.VMEM((GROUPS, 4, 8) + strip, BF16),
            pltpu.VMEM((GROUPS, 4, 4) + strip, BF16),
            pltpu.VMEM((GROUPS, 4, 2) + strip, BF16),
            pltpu.VMEM((GROUPS, 4, 1) + strip, BF16),
            pltpu.SemaphoreType.DMA,
            pltpu.SemaphoreType.DMA((GROUPS, 4, 5)),
            pltpu.SemaphoreType.DMA((GROUPS, 4, 5)),
            pltpu.SemaphoreType.DMA,
            pltpu.SemaphoreType.DMA,
        ],
        compiler_params=pltpu.CompilerParams(
            collective_id=1, has_side_effects=True, vmem_limit_bytes=60 * 1024 * 1024),
        name="image",
    )(fields)


def shards(source_top, receiver_top, slowness_codes, slowness_table, anchors):
    right, left = butterfly_matrices()
    right = jnp.asarray(right, BF16)
    left = jnp.asarray(left, BF16)
    windows = jnp.stack([
        lax.dynamic_slice(slowness_codes[0], (anchors[s, 0], anchors[s, 1]), (N, N)) for s in range(2)
    ]).astype(BF16)
    windows = lax.all_gather(windows, "depth")
    fields = make_fields(source_top, receiver_top, windows, slowness_table, right, left)
    image = make_image(fields, 1.0 / math.sqrt(128.0))
    return image[None]


def solution(mesh):
    return jax.shard_map(
        shards,
        mesh=mesh,
        in_specs=(
            P(None, "freq", None, None, None),
            P(None, "freq", None, None, None),
            P("depth", None, None),
            P(),
            P(),
        ),
        out_specs=P("depth", None, "freq", None),
        check_vma=False,
    )
```

```python
import functools
import math

import jax
import jax.numpy as jnp
import numpy as np
from jax import lax
from jax.experimental import pallas as pl
from jax.experimental.pallas import tpu as pltpu
from jax.sharding import PartitionSpec as P

LAG = 7
LAGS = 2 * LAG + 1
N = 512
B = 128
GROUPS = 5
PER = LAGS // GROUPS
MESH = pl.DeviceIdType.MESH
F32 = jnp.float32
BF16 = jnp.bfloat16


def butterfly_matrices():
    j = np.arange(B)[:, None]
    k = np.arange(B)[None, :]
    mats = []
    for wave in (4 * k, 4 * k + 1, 4 * k + 2, -(4 * k + 1)):
        angle = 2.0 * np.pi * ((j * wave) % N) / N
        c = np.cos(angle) / math.sqrt(N)
        s = np.sin(angle) / math.sqrt(N)
        mats.append(np.block([[c, -s], [s, c]]))
    right = np.stack(mats)
    return right, np.swapaxes(right, 1, 2)


def even_poly(first, terms, top, samples=400):
    q = (np.cos(np.pi * (np.arange(samples) + 0.5) / samples) + 1.0) * 0.5 * top
    r = np.sqrt(q)
    want = np.cos(r) if first == 0 else np.sin(r) / r
    fit = np.polynomial.Chebyshev.fit(q, want, terms, domain=[0, top])
    return [float(v) for v in fit.convert(kind=np.polynomial.Polynomial).coef]


COS_Q = even_poly(0, 9, 14.0)
SIN_Q = even_poly(1, 9, 14.0)


def horner(coefs, q):
    value = coefs[-1] * q + coefs[-2]
    for c in coefs[-3::-1]:
        value = value * q + c
    return value


def split4(re, im):
    er, ei, dr, di = re[0] + re[2], im[0] + im[2], re[0] - re[2], im[0] - im[2]
    fr, fi, gr, gi = re[1] + re[3], im[1] + im[3], re[1] - re[3], im[1] - im[3]
    return (er + fr, dr + gi, er - fr, dr - gi), (ei + fi, di - gr, ei - fi, di + gr)


def join4(re, im):
    er, ei, dr, di = re[0] + re[2], im[0] + im[2], re[0] - re[2], im[0] - im[2]
    fr, fi, gr, gi = re[1] + re[3], im[1] + im[3], re[1] - re[3], im[1] - im[3]
    return (er + fr, dr - gi, er - fr, dr + gi), (ei + fi, di + gr, ei - fi, di - gr)


def level_row(table):
    lane = lax.broadcasted_iota(jnp.int32, (8, B), 1)
    levels = jnp.zeros((8, B), F32)
    for k in range(32):
        levels = jnp.where(lane == k, table[k], levels)
    return levels


TAKE = lax.GatherDimensionNumbers(
    offset_dims=(), collapsed_slice_dims=(1,), start_index_map=(1,),
    operand_batching_dims=(0,), start_indices_batching_dims=(0,))


def lookup(values, index):
    return lax.gather(
        jnp.tile(values, (index.shape[0] // 8, 1)), index[..., None], TAKE, (1, 1),
        mode=lax.GatherScatterMode.PROMISE_IN_BOUNDS)


def windows_kernel(codes, table, anchors, out, means, raw, sem):
    def fetch(s, h):
        ox = pl.multiple_of(anchors[s, 0], N)
        oy = pl.multiple_of(anchors[s, 1], N)
        return pltpu.make_async_copy(
            codes.at[0, pl.ds(ox + h * 256, 256), pl.ds(oy, N)], raw.at[s, h], sem.at[s, h])

    for s in range(2):
        for h in range(2):
            fetch(s, h).start()
    levels = level_row(table)
    for s in range(2):
        total = jnp.zeros((8, B), F32)
        for h in range(2):
            fetch(s, h).wait()

            def rows_of(n, total):
                take = pl.ds(pl.multiple_of(n * 32, 32), 32)
                for q in range(4):
                    index = raw[s, h, take, q * B:(q + 1) * B]
                    out[s, pl.ds(pl.multiple_of(h * 256 + n * 32, 32), 32), q * B:(q + 1) * B] = (
                        index.astype(F32).astype(BF16))
                    got = lookup(levels, index)
                    total = total + (got[0:8] + got[8:16]) + (got[16:24] + got[24:32])
                return total

            total = lax.fori_loop(0, 8, rows_of, total)
        means[s] = jnp.full((8, B), jnp.sum(total) * (1.0 / (N * N)), F32)


def make_windows(codes, table, anchors):
    vmem = pl.BlockSpec(memory_space=pltpu.VMEM)
    smem = pl.BlockSpec(memory_space=pltpu.SMEM)
    return pl.pallas_call(
        windows_kernel,
        out_shape=(
            jax.ShapeDtypeStruct((2, N, N), BF16),
            jax.ShapeDtypeStruct((2, 8, B), F32),
        ),
        in_specs=[pl.BlockSpec(memory_space=pl.ANY), smem, smem],
        out_specs=(vmem, vmem),
        scratch_shapes=[pltpu.VMEM((2, 2, 256, N), jnp.int32), pltpu.SemaphoreType.DMA((2, 2))],
        compiler_params=pltpu.CompilerParams(vmem_limit_bytes=32 * 1024 * 1024),
        name="windows",
    )(codes, table, anchors)


def exchange_kernel(win, means, out, outm, lsem, ssem, rsem, msend, mrecv):
    depth = lax.axis_index("depth")
    freq = lax.axis_index("freq")
    core = depth % 2
    section = depth // 2
    flipped = (freq + 16) % 32
    sibling = (depth + 1 - 2 * core, freq)
    half = N // 2
    up = lambda s: (2 * (1 - section) + s, freq)
    down = lambda s: (2 * (1 - section) + s, flipped)

    barrier = pltpu.get_barrier_semaphore()
    for who in (sibling, up(0), up(1), down(0), down(1)):
        pl.semaphore_signal(barrier, inc=1, device_id=who, device_id_type=MESH)
    pl.semaphore_wait(barrier, 5)

    def to_section(s, way):
        rows = pl.ds(way * half, half)
        who = (up(s), down(s))[way]
        return (
            pltpu.make_async_remote_copy(
                src_ref=win.at[s, rows], dst_ref=out.at[core, rows],
                send_sem=ssem.at[s, way], recv_sem=rsem.at[core, way],
                device_id=who, device_id_type=MESH),
        )

    def means_to_section(s):
        return pltpu.make_async_remote_copy(
            src_ref=means.at[s], dst_ref=outm.at[core],
            send_sem=msend.at[s], recv_sem=mrecv.at[core],
            device_id=up(s), device_id_type=MESH)

    @pl.when(section == 0)
    def _():
        for s in range(2):
            means_to_section(s).start()
            for way in range(2):
                for copy in to_section(s, way):
                    copy.start()

    swap = pltpu.make_async_remote_copy(
        src_ref=win.at[1 - core], dst_ref=out.at[depth],
        send_sem=ssem.at[2, 0], recv_sem=rsem.at[2, 0], device_id=sibling, device_id_type=MESH)
    swap.start()
    swap_means = pltpu.make_async_remote_copy(
        src_ref=means.at[1 - core], dst_ref=outm.at[depth],
        send_sem=msend.at[2], recv_sem=mrecv.at[2], device_id=sibling, device_id_type=MESH)
    swap_means.start()
    keep = pltpu.make_async_copy(win.at[core], out.at[depth], lsem)
    keep.start()
    outm[depth] = means[core]
    keep.wait()

    swap.wait()
    swap_means.wait()

    @pl.when(section == 0)
    def _():
        for s in range(2):
            means_to_section(s).wait_send()
            for way in range(2):
                for copy in to_section(s, way):
                    copy.wait_send()

    @pl.when(section == 1)
    def _():
        for plane in range(2):
            pltpu.make_async_copy(outm.at[plane], outm.at[plane], mrecv.at[plane]).wait()
            for way in range(2):
                rows = pl.ds(way * half, half)
                pltpu.make_async_copy(out.at[plane, rows], out.at[plane, rows], rsem.at[plane, way]).wait()


def exchange(win, means):
    vmem = pl.BlockSpec(memory_space=pltpu.VMEM)
    return pl.pallas_call(
        exchange_kernel,
        out_shape=(
            jax.ShapeDtypeStruct((4, N, N), BF16),
            jax.ShapeDtypeStruct((4, 8, B), F32),
        ),
        in_specs=[vmem, vmem],
        out_specs=(vmem, vmem),
        scratch_shapes=[
            pltpu.SemaphoreType.DMA,
            pltpu.SemaphoreType.DMA((3, 2)),
            pltpu.SemaphoreType.DMA((3, 2)),
            pltpu.SemaphoreType.DMA((3,)),
            pltpu.SemaphoreType.DMA((3,)),
        ],
        compiler_params=pltpu.CompilerParams(
            collective_id=2, has_side_effects=True, vmem_limit_bytes=16 * 1024 * 1024),
        name="exchange",
    )(win, means)


def fields_kernel(
    src, rec, codes, sums, table, right_ref, left_ref, out,
    u, a, cbuf, ph, sc, tsem, csem, osem,
):
    depth = lax.axis_index("depth")
    core = depth % 2
    first_plane = (depth // 2) * 2
    steps = first_plane + 2
    position = lax.axis_index("freq").astype(F32)
    angular = math.pi * (0.45 + 0.5 * (position + 0.5) / 32.0)

    tops = []
    for kind, top in enumerate((src, rec)):
        for q in range(4):
            tops.append(pltpu.make_async_copy(
                top.at[core, 0, :, :, pl.ds(q * B, B)], u.at[kind, :, q], tsem.at[kind, q]))
    for copy in tops:
        copy.start()
    for z in range(4):
        pltpu.make_async_copy(codes.at[z], cbuf.at[z], csem.at[z]).start()

    levels = level_row(table)
    angle = angular * levels
    squared = angle * angle
    cos_levels = horner(COS_Q, squared)
    sin_levels = angle * horner(SIN_Q, squared)

    for copy in tops:
        copy.wait()

    def step(z, carry):
        pltpu.make_async_copy(codes.at[z], cbuf.at[z], csem.at[z]).wait()
        base = sums[z, 0:1, :]
        turn = angular * base
        turn_sq = turn * turn
        turn_re = horner(COS_Q, turn_sq)
        turn_im = turn * horner(SIN_Q, turn_sq)

        def operators(n, carry):
            rows = n * 24
            k = rows + lax.broadcasted_iota(jnp.int32, (24, B), 0)
            kx = (k % B) * 4 + k // B
            kx = jnp.where(kx < N // 2, kx, kx - N).astype(F32) * (2.0 * math.pi / N)
            left_q = turn_sq - kx * kx
            for ry in range(3):
                ky = lax.broadcasted_iota(jnp.int32, (1, B), 1) * 4 + ry
                ky = jnp.where(ky < N // 2, ky, ky - N).astype(F32) * (2.0 * math.pi / N)
                q = left_q - ky * ky
                root = jnp.sqrt(jnp.abs(q))
                wave = jnp.maximum(q, 0.0)
                travels = q >= 0.0
                pre = jnp.where(travels, horner(COS_Q, wave), jnp.exp(-root))
                pim = jnp.where(travels, root * horner(SIN_Q, wave), 0.0)
                put = pl.ds(pl.multiple_of(rows, 8), 24)
                ph[0, ry, put, :] = pre * turn_re + pim * turn_im
                ph[1, ry, put, :] = pim * turn_re - pre * turn_im
            take = pl.ds(pl.multiple_of(n * 32, 32), 32)
            for q in range(4):
                index = cbuf[z, take, q * B:(q + 1) * B].astype(jnp.int32)
                sc[0, q, take, :] = lookup(cos_levels, index)
                sc[1, q, take, :] = lookup(sin_levels, index)
            return carry

        lax.fori_loop(0, 16, operators, 0)

        def wide(ref, kind, p, half, block):
            rows = slice(block * B, (block + 1) * B)
            return jnp.concatenate([ref[kind, p, half * 2, rows, :], ref[kind, p, half * 2 + 1, rows, :]], axis=1)

        def put_wide(ref, kind, p, half, block, value):
            rows = slice(block * B, (block + 1) * B)
            ref[kind, p, half * 2, rows, :] = value[:, :B]
            ref[kind, p, half * 2 + 1, rows, :] = value[:, B:]

        def forward_x(n, carry):
            kind, half = n // 2, n % 2
            re = [wide(u, kind, 0, half, q) for q in range(4)]
            im = [wide(u, kind, 1, half, q) for q in range(4)]
            sre, sim = split4(re, im)
            for r in range(4):
                got = jnp.dot(left_ref[r], jnp.concatenate([sre[r], sim[r]], axis=0),
                              preferred_element_type=F32).astype(BF16)
                put_wide(a, kind, 0, half, r, got[:B])
                put_wide(a, kind, 1, half, r, got[B:])
            return carry

        lax.fori_loop(0, 4, forward_x, 0)

        def along_y(n, carry):
            kind, rx = n // 4, n % 4
            sign = (1 - 2 * kind).astype(F32)
            prow = pl.ds(pl.multiple_of(jnp.where(rx == 3, 1, rx) * B, B), B)
            rows = pl.ds(pl.multiple_of(rx * B, B), B)
            re = [a[kind, 0, q, rows, :] for q in range(4)]
            im = [a[kind, 1, q, rows, :] for q in range(4)]
            sre, sim = split4(re, im)
            tre, tim = [], []
            for r in range(4):
                got = jnp.dot(jnp.concatenate([sre[r], sim[r]], axis=1), right_ref[r],
                              preferred_element_type=F32)
                gre, gim = got[:, :B], got[:, B:]
                py = 1 if r == 3 else r
                pre, pim = ph[0, py, prow, :], ph[1, py, prow, :] * sign
                turned = jnp.concatenate(
                    [(gre * pre - gim * pim).astype(BF16), (gre * pim + gim * pre).astype(BF16)], axis=1)
                back = jnp.dot(turned, left_ref[r], preferred_element_type=F32)
                tre.append(back[:, :B])
                tim.append(back[:, B:])
            cre, cim = join4(tre, tim)
            for q in range(4):
                a[kind, 0, q, rows, :] = cre[q].astype(BF16)
                a[kind, 1, q, rows, :] = cim[q].astype(BF16)
            return carry

        lax.fori_loop(0, 8, along_y, 0)

        @pl.when(z > first_plane)
        def _():
            pltpu.make_async_copy(u, out.at[0], osem.at[0]).wait()

        def inverse_x(n, carry):
            kind, half = n // 2, n % 2
            sign = (1 - 2 * kind).astype(F32)
            tre, tim = [], []
            for r in range(4):
                data = jnp.concatenate([wide(a, kind, 0, half, r), wide(a, kind, 1, half, r)], axis=0)
                got = jnp.dot(right_ref[r], data, preferred_element_type=F32)
                tre.append(got[:B])
                tim.append(got[B:])
            xre, xim = join4(tre, tim)
            for q in range(4):
                rows = slice(q * B, (q + 1) * B)
                for part in range(2):
                    cols = slice(part * B, (part + 1) * B)
                    cre = sc[0, half * 2 + part, rows, :]
                    cim = sc[1, half * 2 + part, rows, :] * sign
                    gre, gim = xre[q][:, cols], xim[q][:, cols]
                    u[kind, 0, half * 2 + part, rows, :] = (gre * cre - gim * cim).astype(BF16)
                    u[kind, 1, half * 2 + part, rows, :] = (gre * cim + gim * cre).astype(BF16)
            return carry

        lax.fori_loop(0, 4, inverse_x, 0)

        @pl.when(z == first_plane)
        def _():
            pltpu.make_async_copy(u, out.at[0], osem.at[0]).start()

        @pl.when(z == first_plane + 1)
        def _():
            pltpu.make_async_copy(u, out.at[1], osem.at[1]).start()

        return carry

    lax.fori_loop(0, steps, step, 0)

    def drain(z, carry):
        pltpu.make_async_copy(codes.at[z], cbuf.at[z], csem.at[z]).wait()
        return carry

    lax.fori_loop(steps, 4, drain, 0)
    pltpu.make_async_copy(u, out.at[1], osem.at[1]).wait()


def make_fields(src, rec, codes, sums, table, right, left):
    vmem = pl.BlockSpec(memory_space=pltpu.VMEM)
    hbm = pl.BlockSpec(memory_space=pl.ANY)
    return pl.pallas_call(
        fields_kernel,
        out_shape=jax.ShapeDtypeStruct((2, 2, 2, 4, N, B), BF16),
        in_specs=[hbm, hbm, hbm, vmem, pl.BlockSpec(memory_space=pltpu.SMEM), vmem, vmem],
        out_specs=hbm,
        scratch_shapes=[
            pltpu.VMEM((2, 2, 4, N, B), BF16),
            pltpu.VMEM((2, 2, 4, N, B), BF16),
            pltpu.VMEM((4, N, N), BF16),
            pltpu.VMEM((2, 3, 3 * B, B), F32),
            pltpu.VMEM((2, 4, N, B), F32),
            pltpu.SemaphoreType.DMA((2, 4)),
            pltpu.SemaphoreType.DMA((4,)),
            pltpu.SemaphoreType.DMA((2,)),
        ],
        compiler_params=pltpu.CompilerParams(vmem_limit_bytes=60 * 1024 * 1024),
        name="fields",
    )(src, rec, codes, sums, table, right, left)


def image_kernel(factor, fields, out, own, other, pad, buf, r0, r1, r2, r3, r4,
                 lsem, ssem, rsem, xs, xr):
    depth = lax.axis_index("depth")
    freq = lax.axis_index("freq")
    core = depth % 2
    x, z, yh = freq % 4, (freq // 4) % 4, freq // 16
    base = yh * 16 + z * 4 + x
    sibling = (depth + 1 - 2 * core, freq)
    dims = (
        (depth, base - x + (x + 1 - 2 * (x % 2))),
        (depth, base - x + (3 - x)),
        (depth, base - 4 * z + 4 * (z + 1 - 2 * (z % 2))),
        (depth, base - 4 * z + 4 * (3 - z)),
    )
    across = (depth, base - 16 * yh + 16 * (1 - yh))

    barrier = pltpu.get_barrier_semaphore()
    for who in (sibling, across) + dims:
        pl.semaphore_signal(barrier, inc=1, device_id=who, device_id_type=MESH)
    local = pltpu.make_async_copy(fields.at[core], own, lsem)
    local.start()
    pl.semaphore_wait(barrier, 6)
    swap = pltpu.make_async_remote_copy(
        src_ref=fields.at[1 - core], dst_ref=other, send_sem=xs, recv_sem=xr,
        device_id=sibling, device_id_type=MESH)
    swap.start()

    for s in range(2):
        for k in range(2):
            for p in range(2):
                for i in range(4):
                    pad[s, k, p, i, 0:8, :] = jnp.zeros((8, B), F32)
                    pad[s, k, p, i, N + 8:N + 16, :] = jnp.zeros((8, B), F32)

    def widen(s, ref):
        def body(n, carry):
            k, p, i = n // 8, (n // 4) % 2, n % 4
            for h in range(2):
                pad[s, k, p, i, 8 + h * 256:8 + (h + 1) * 256, :] = ref[k, p, i, h * 256:(h + 1) * 256, :].astype(F32)
            return carry
        lax.fori_loop(0, 16, body, 0)

    local.wait()
    widen(0, own)
    swap.wait()
    widen(1, other)

    def bits(ix, iz):
        return [((ix + 1) // 2) % 2, ix // 2, ((iz + 1) // 2) % 2, iz // 2]

    mine = bits(x, z)

    flip_x = [[(mine[d] + bits(v, 0)[d]) % 2 for d in range(2)] for v in range(4)]
    slot_x = [[sum(flip_x[v][d] * (16 >> ((d - i) % 4)) for d in range(2)) for i in range(4)] for v in range(4)]

    def produce(g):
        def body(n, carry):
            theirs = bits(0, n % 4)
            flip_z = [(mine[d] + theirs[d]) % 2 for d in (2, 3)]
            last = (yh + n // 4) % 2
            slot_z = [last + sum(flip_z[d - 2] * (16 >> ((d - i) % 4)) for d in (2, 3)) for i in range(4)]
            for v in range(4):
                row = pl.multiple_of(n * 64 + v * 16, 16)
                for i in range(4):
                    slot = slot_z[i] + slot_x[v][i]
                    for l in range(PER):
                        h = g * PER + l - LAG
                        total = None
                        for s in range(2):
                            for p in range(2):
                                left = pad[s, 0, p, i, pl.ds(row + (8 - h), 16), :]
                                right = pad[s, 1, p, i, pl.ds(row + (8 + h), 16), :]
                                term = left * right
                                total = term if total is None else total + term
                        buf[g, i, slot, l] = total.astype(BF16)
            return carry
        lax.fori_loop(0, 8, body, 0)

    recv = (r0, r1, r2, r3, r4)

    def copy(g, i, t):
        half = 16 >> t
        who = across if t == 4 else dims[(i + t) % 4]
        return pltpu.make_async_remote_copy(
            src_ref=buf.at[g, i, pl.ds(half, half)], dst_ref=recv[t].at[g, i],
            send_sem=ssem.at[g, i, t], recv_sem=rsem.at[g, i, t],
            device_id=who, device_id_type=MESH)

    def arrive(g, i, t):
        copy(g, i, t).wait_recv()
        half = 16 >> t

        if t < 4:
            def body(n, carry):
                k = half - 1 - n
                buf[g, i, k] = buf[g, i, k] + recv[t][g, i, k]
                return carry
            lax.fori_loop(0, half, body, 0)
            copy(g, i, t + 1).start()
        else:
            total = buf[g, i, 0].astype(F32) + recv[4][g, i, 0].astype(F32)
            out[g * PER:(g + 1) * PER, :, i * B:(i + 1) * B] = total * factor

    for g in range(GROUPS):
        produce(g)
        for i in range(4):
            copy(g, i, 0).start()
    for w in range(GROUPS + 4):
        for t in range(4, -1, -1):
            g = w - t
            if 0 <= g < GROUPS:
                for i in range(4):
                    arrive(g, i, t)
    for g in range(GROUPS):
        for i in range(4):
            for t in range(5):
                copy(g, i, t).wait_send()


def make_image(fields, factor):
    hbm = pl.BlockSpec(memory_space=pl.ANY)
    strip = (PER, 16, B)
    return pl.pallas_call(
        functools.partial(image_kernel, factor),
        out_shape=jax.ShapeDtypeStruct((LAGS, 16, N), F32),
        in_specs=[hbm],
        out_specs=pl.BlockSpec(memory_space=pltpu.VMEM),
        scratch_shapes=[
            pltpu.VMEM((2, 2, 4, N, B), BF16),
            pltpu.VMEM((2, 2, 4, N, B), BF16),
            pltpu.VMEM((2, 2, 2, 4, N + 16, B), F32),
            pltpu.VMEM((GROUPS, 4, 32) + strip, BF16),
            pltpu.VMEM((GROUPS, 4, 16) + strip, BF16),
            pltpu.VMEM((GROUPS, 4, 8) + strip, BF16),
            pltpu.VMEM((GROUPS, 4, 4) + strip, BF16),
            pltpu.VMEM((GROUPS, 4, 2) + strip, BF16),
            pltpu.VMEM((GROUPS, 4, 1) + strip, BF16),
            pltpu.SemaphoreType.DMA,
            pltpu.SemaphoreType.DMA((GROUPS, 4, 5)),
            pltpu.SemaphoreType.DMA((GROUPS, 4, 5)),
            pltpu.SemaphoreType.DMA,
            pltpu.SemaphoreType.DMA,
        ],
        compiler_params=pltpu.CompilerParams(
            collective_id=1, has_side_effects=True, vmem_limit_bytes=60 * 1024 * 1024),
        name="image",
    )(fields)


def shards(source_top, receiver_top, slowness_codes, slowness_table, anchors):
    right, left = butterfly_matrices()
    right = jnp.asarray(right, BF16)
    left = jnp.asarray(left, BF16)
    windows, means = make_windows(slowness_codes, slowness_table, anchors)
    codes, sums = exchange(windows, means)
    fields = make_fields(source_top, receiver_top, codes, sums, slowness_table, right, left)
    image = make_image(fields, 1.0 / math.sqrt(128.0))
    return image[None]


def solution(mesh):
    return jax.shard_map(
        shards,
        mesh=mesh,
        in_specs=(
            P(None, "freq", None, None, None),
            P(None, "freq", None, None, None),
            P("depth", None, None),
            P(),
            P(),
        ),
        out_specs=P("depth", None, "freq", None),
        check_vma=False,
    )
```

```python
import functools
import math

import jax
import jax.numpy as jnp
import numpy as np
from jax import lax
from jax.experimental import pallas as pl
from jax.experimental.pallas import tpu as pltpu
from jax.sharding import PartitionSpec as P

LAG = 7
LAGS = 2 * LAG + 1
N = 512
B = 128
GROUPS = 5
PER = LAGS // GROUPS
MESH = pl.DeviceIdType.MESH
F32 = jnp.float32
BF16 = jnp.bfloat16


def butterfly_matrices():
    j = np.arange(B)[:, None]
    k = np.arange(B)[None, :]
    mats = []
    for wave in (4 * k, 4 * k + 1, 4 * k + 2, -(4 * k + 1)):
        angle = 2.0 * np.pi * ((j * wave) % N) / N
        c = np.cos(angle) / math.sqrt(N)
        s = np.sin(angle) / math.sqrt(N)
        mats.append(np.block([[c, -s], [s, c]]))
    right = np.stack(mats)
    return right, np.swapaxes(right, 1, 2)


def even_poly(first, terms, top, samples=400):
    q = (np.cos(np.pi * (np.arange(samples) + 0.5) / samples) + 1.0) * 0.5 * top
    r = np.sqrt(q)
    want = np.cos(r) if first == 0 else np.sin(r) / r
    fit = np.polynomial.Chebyshev.fit(q, want, terms, domain=[0, top])
    return [float(v) for v in fit.convert(kind=np.polynomial.Polynomial).coef]


COS_Q = even_poly(0, 9, 14.0)
SIN_Q = even_poly(1, 9, 14.0)


def horner(coefs, q):
    value = coefs[-1] * q + coefs[-2]
    for c in coefs[-3::-1]:
        value = value * q + c
    return value


def split4(re, im):
    er, ei, dr, di = re[0] + re[2], im[0] + im[2], re[0] - re[2], im[0] - im[2]
    fr, fi, gr, gi = re[1] + re[3], im[1] + im[3], re[1] - re[3], im[1] - im[3]
    return (er + fr, dr + gi, er - fr, dr - gi), (ei + fi, di - gr, ei - fi, di + gr)


def join4(re, im):
    er, ei, dr, di = re[0] + re[2], im[0] + im[2], re[0] - re[2], im[0] - im[2]
    fr, fi, gr, gi = re[1] + re[3], im[1] + im[3], re[1] - re[3], im[1] - im[3]
    return (er + fr, dr - gi, er - fr, dr + gi), (ei + fi, di + gr, ei - fi, di - gr)


def level_row(table):
    lane = lax.broadcasted_iota(jnp.int32, (8, B), 1)
    levels = jnp.zeros((8, B), F32)
    for k in range(32):
        levels = jnp.where(lane == k, table[k], levels)
    return levels


TAKE = lax.GatherDimensionNumbers(
    offset_dims=(), collapsed_slice_dims=(1,), start_index_map=(1,),
    operand_batching_dims=(0,), start_indices_batching_dims=(0,))


def lookup(values, index):
    return lax.gather(
        jnp.tile(values, (index.shape[0] // 8, 1)), index[..., None], TAKE, (1, 1),
        mode=lax.GatherScatterMode.PROMISE_IN_BOUNDS)


def windows_kernel(codes, table, anchors, out, means, raw, sem):
    def fetch(s, h):
        ox = pl.multiple_of(anchors[s, 0], N)
        oy = pl.multiple_of(anchors[s, 1], N)
        return pltpu.make_async_copy(
            codes.at[0, pl.ds(ox + h * 256, 256), pl.ds(oy, N)], raw.at[s, h], sem.at[s, h])

    for s in range(2):
        for h in range(2):
            fetch(s, h).start()
    levels = level_row(table)
    for s in range(2):
        total = jnp.zeros((8, B), F32)
        for h in range(2):
            fetch(s, h).wait()

            def rows_of(n, total):
                take = pl.ds(pl.multiple_of(n * 32, 32), 32)
                for q in range(4):
                    index = raw[s, h, take, q * B:(q + 1) * B]
                    out[s, pl.ds(pl.multiple_of(h * 256 + n * 32, 32), 32), q * B:(q + 1) * B] = (
                        index.astype(F32).astype(BF16))
                    got = lookup(levels, index)
                    total = total + (got[0:8] + got[8:16]) + (got[16:24] + got[24:32])
                return total

            total = lax.fori_loop(0, 8, rows_of, total)
        means[s] = jnp.full((8, B), jnp.sum(total) * (1.0 / (N * N)), F32)


def make_windows(codes, table, anchors):
    vmem = pl.BlockSpec(memory_space=pltpu.VMEM)
    smem = pl.BlockSpec(memory_space=pltpu.SMEM)
    return pl.pallas_call(
        windows_kernel,
        out_shape=(
            jax.ShapeDtypeStruct((2, N, N), BF16),
            jax.ShapeDtypeStruct((2, 8, B), F32),
        ),
        in_specs=[pl.BlockSpec(memory_space=pl.ANY), smem, smem],
        out_specs=(vmem, vmem),
        scratch_shapes=[pltpu.VMEM((2, 2, 256, N), jnp.int32), pltpu.SemaphoreType.DMA((2, 2))],
        compiler_params=pltpu.CompilerParams(vmem_limit_bytes=60 * 1024 * 1024),
        name="windows",
    )(codes, table, anchors)


def exchange_kernel(win, means, out, outm, lsem, ssem, rsem, msend, mrecv):
    depth = lax.axis_index("depth")
    freq = lax.axis_index("freq")
    core = depth % 2
    section = depth // 2
    flipped = (freq + 16) % 32
    sibling = (depth + 1 - 2 * core, freq)
    half = N // 2
    up = lambda s: (2 * (1 - section) + s, freq)
    down = lambda s: (2 * (1 - section) + s, flipped)

    barrier = pltpu.get_barrier_semaphore()
    for who in (sibling, up(0), up(1), down(0), down(1)):
        pl.semaphore_signal(barrier, inc=1, device_id=who, device_id_type=MESH)
    pl.semaphore_wait(barrier, 5)

    def to_section(s, way):
        rows = pl.ds(way * half, half)
        who = (up(s), down(s))[way]
        return (
            pltpu.make_async_remote_copy(
                src_ref=win.at[s, rows], dst_ref=out.at[core, rows],
                send_sem=ssem.at[s, way], recv_sem=rsem.at[core, way],
                device_id=who, device_id_type=MESH),
        )

    def means_to_section(s):
        return pltpu.make_async_remote_copy(
            src_ref=means.at[s], dst_ref=outm.at[core],
            send_sem=msend.at[s], recv_sem=mrecv.at[core],
            device_id=up(s), device_id_type=MESH)

    @pl.when(section == 0)
    def _():
        for s in range(2):
            means_to_section(s).start()
            for way in range(2):
                for copy in to_section(s, way):
                    copy.start()

    swap = pltpu.make_async_remote_copy(
        src_ref=win.at[1 - core], dst_ref=out.at[depth],
        send_sem=ssem.at[2, 0], recv_sem=rsem.at[2, 0], device_id=sibling, device_id_type=MESH)
    swap.start()
    swap_means = pltpu.make_async_remote_copy(
        src_ref=means.at[1 - core], dst_ref=outm.at[depth],
        send_sem=msend.at[2], recv_sem=mrecv.at[2], device_id=sibling, device_id_type=MESH)
    swap_means.start()
    keep = pltpu.make_async_copy(win.at[core], out.at[depth], lsem)
    keep.start()
    outm[depth] = means[core]
    keep.wait()

    swap.wait()
    swap_means.wait()

    @pl.when(section == 0)
    def _():
        for s in range(2):
            means_to_section(s).wait_send()
            for way in range(2):
                for copy in to_section(s, way):
                    copy.wait_send()

    @pl.when(section == 1)
    def _():
        for plane in range(2):
            pltpu.make_async_copy(outm.at[plane], outm.at[plane], mrecv.at[plane]).wait()
            for way in range(2):
                rows = pl.ds(way * half, half)
                pltpu.make_async_copy(out.at[plane, rows], out.at[plane, rows], rsem.at[plane, way]).wait()


def exchange(win, means):
    vmem = pl.BlockSpec(memory_space=pltpu.VMEM)
    return pl.pallas_call(
        exchange_kernel,
        out_shape=(
            jax.ShapeDtypeStruct((4, N, N), BF16),
            jax.ShapeDtypeStruct((4, 8, B), F32),
        ),
        in_specs=[vmem, vmem],
        out_specs=(vmem, vmem),
        scratch_shapes=[
            pltpu.SemaphoreType.DMA,
            pltpu.SemaphoreType.DMA((3, 2)),
            pltpu.SemaphoreType.DMA((3, 2)),
            pltpu.SemaphoreType.DMA((3,)),
            pltpu.SemaphoreType.DMA((3,)),
        ],
        compiler_params=pltpu.CompilerParams(
            collective_id=2, has_side_effects=True, vmem_limit_bytes=60 * 1024 * 1024),
        name="exchange",
    )(win, means)


def fields_kernel(
    src, rec, codes, sums, table, right_ref, left_ref, out,
    u, a, cbuf, ph, sc, tsem, csem, osem,
):
    depth = lax.axis_index("depth")
    core = depth % 2
    first_plane = (depth // 2) * 2
    steps = first_plane + 2
    position = lax.axis_index("freq").astype(F32)
    angular = math.pi * (0.45 + 0.5 * (position + 0.5) / 32.0)

    tops = []
    for kind, top in enumerate((src, rec)):
        for q in range(4):
            tops.append(pltpu.make_async_copy(
                top.at[core, 0, :, :, pl.ds(q * B, B)], u.at[kind, :, q], tsem.at[kind, q]))
    for copy in tops:
        copy.start()
    for z in range(4):
        pltpu.make_async_copy(codes.at[z], cbuf.at[z], csem.at[z]).start()

    levels = level_row(table)
    angle = angular * levels
    squared = angle * angle
    cos_levels = horner(COS_Q, squared)
    sin_levels = angle * horner(SIN_Q, squared)

    for copy in tops:
        copy.wait()

    def step(z, carry):
        pltpu.make_async_copy(codes.at[z], cbuf.at[z], csem.at[z]).wait()
        base = sums[z, 0:1, :]
        turn = angular * base
        turn_sq = turn * turn
        turn_re = horner(COS_Q, turn_sq)
        turn_im = turn * horner(SIN_Q, turn_sq)

        def operators(n, carry):
            rows = n * 24
            k = rows + lax.broadcasted_iota(jnp.int32, (24, B), 0)
            kx = (k % B) * 4 + k // B
            kx = jnp.where(kx < N // 2, kx, kx - N).astype(F32) * (2.0 * math.pi / N)
            left_q = turn_sq - kx * kx
            for ry in range(3):
                ky = lax.broadcasted_iota(jnp.int32, (1, B), 1) * 4 + ry
                ky = jnp.where(ky < N // 2, ky, ky - N).astype(F32) * (2.0 * math.pi / N)
                q = left_q - ky * ky
                root = jnp.sqrt(jnp.abs(q))
                wave = jnp.maximum(q, 0.0)
                travels = q >= 0.0
                pre = jnp.where(travels, horner(COS_Q, wave), jnp.exp(-root))
                pim = jnp.where(travels, root * horner(SIN_Q, wave), 0.0)
                put = pl.ds(pl.multiple_of(rows, 8), 24)
                ph[0, ry, put, :] = pre * turn_re + pim * turn_im
                ph[1, ry, put, :] = pim * turn_re - pre * turn_im
            take = pl.ds(pl.multiple_of(n * 32, 32), 32)
            for q in range(4):
                index = cbuf[z, take, q * B:(q + 1) * B].astype(jnp.int32)
                sc[0, q, take, :] = lookup(cos_levels, index)
                sc[1, q, take, :] = lookup(sin_levels, index)
            return carry

        lax.fori_loop(0, 16, operators, 0)

        def wide(ref, kind, p, half, block):
            rows = slice(block * B, (block + 1) * B)
            return jnp.concatenate([ref[kind, p, half * 2, rows, :], ref[kind, p, half * 2 + 1, rows, :]], axis=1)

        def put_wide(ref, kind, p, half, block, value):
            rows = slice(block * B, (block + 1) * B)
            ref[kind, p, half * 2, rows, :] = value[:, :B]
            ref[kind, p, half * 2 + 1, rows, :] = value[:, B:]

        def forward_x(n, carry):
            kind, half = n // 2, n % 2
            re = [wide(u, kind, 0, half, q) for q in range(4)]
            im = [wide(u, kind, 1, half, q) for q in range(4)]
            sre, sim = split4(re, im)
            for r in range(4):
                got = jnp.dot(left_ref[r], jnp.concatenate([sre[r], sim[r]], axis=0),
                              preferred_element_type=F32).astype(BF16)
                put_wide(a, kind, 0, half, r, got[:B])
                put_wide(a, kind, 1, half, r, got[B:])
            return carry

        lax.fori_loop(0, 4, forward_x, 0)

        def along_y(n, carry):
            kind, rx = n // 4, n % 4
            sign = (1 - 2 * kind).astype(F32)
            prow = pl.ds(pl.multiple_of(jnp.where(rx == 3, 1, rx) * B, B), B)
            rows = pl.ds(pl.multiple_of(rx * B, B), B)
            re = [a[kind, 0, q, rows, :] for q in range(4)]
            im = [a[kind, 1, q, rows, :] for q in range(4)]
            sre, sim = split4(re, im)
            tre, tim = [], []
            for r in range(4):
                got = jnp.dot(jnp.concatenate([sre[r], sim[r]], axis=1), right_ref[r],
                              preferred_element_type=F32)
                gre, gim = got[:, :B], got[:, B:]
                py = 1 if r == 3 else r
                pre, pim = ph[0, py, prow, :], ph[1, py, prow, :] * sign
                turned = jnp.concatenate(
                    [(gre * pre - gim * pim).astype(BF16), (gre * pim + gim * pre).astype(BF16)], axis=1)
                back = jnp.dot(turned, left_ref[r], preferred_element_type=F32)
                tre.append(back[:, :B])
                tim.append(back[:, B:])
            cre, cim = join4(tre, tim)
            for q in range(4):
                a[kind, 0, q, rows, :] = cre[q].astype(BF16)
                a[kind, 1, q, rows, :] = cim[q].astype(BF16)
            return carry

        lax.fori_loop(0, 8, along_y, 0)

        @pl.when(z > first_plane)
        def _():
            pltpu.make_async_copy(u, out.at[0], osem.at[0]).wait()

        def inverse_x(n, carry):
            kind, half = n // 2, n % 2
            sign = (1 - 2 * kind).astype(F32)
            tre, tim = [], []
            for r in range(4):
                data = jnp.concatenate([wide(a, kind, 0, half, r), wide(a, kind, 1, half, r)], axis=0)
                got = jnp.dot(right_ref[r], data, preferred_element_type=F32)
                tre.append(got[:B])
                tim.append(got[B:])
            xre, xim = join4(tre, tim)
            for q in range(4):
                rows = slice(q * B, (q + 1) * B)
                for part in range(2):
                    cols = slice(part * B, (part + 1) * B)
                    cre = sc[0, half * 2 + part, rows, :]
                    cim = sc[1, half * 2 + part, rows, :] * sign
                    gre, gim = xre[q][:, cols], xim[q][:, cols]
                    u[kind, 0, half * 2 + part, rows, :] = (gre * cre - gim * cim).astype(BF16)
                    u[kind, 1, half * 2 + part, rows, :] = (gre * cim + gim * cre).astype(BF16)
            return carry

        lax.fori_loop(0, 4, inverse_x, 0)

        @pl.when(z == first_plane)
        def _():
            pltpu.make_async_copy(u, out.at[0], osem.at[0]).start()

        @pl.when(z == first_plane + 1)
        def _():
            pltpu.make_async_copy(u, out.at[1], osem.at[1]).start()

        return carry

    lax.fori_loop(0, steps, step, 0)

    def drain(z, carry):
        pltpu.make_async_copy(codes.at[z], cbuf.at[z], csem.at[z]).wait()
        return carry

    lax.fori_loop(steps, 4, drain, 0)
    pltpu.make_async_copy(u, out.at[1], osem.at[1]).wait()


def make_fields(src, rec, codes, sums, table, right, left):
    vmem = pl.BlockSpec(memory_space=pltpu.VMEM)
    hbm = pl.BlockSpec(memory_space=pl.ANY)
    return pl.pallas_call(
        fields_kernel,
        out_shape=jax.ShapeDtypeStruct((2, 2, 2, 4, N, B), BF16),
        in_specs=[hbm, hbm, hbm, vmem, pl.BlockSpec(memory_space=pltpu.SMEM), vmem, vmem],
        out_specs=hbm,
        scratch_shapes=[
            pltpu.VMEM((2, 2, 4, N, B), BF16),
            pltpu.VMEM((2, 2, 4, N, B), BF16),
            pltpu.VMEM((4, N, N), BF16),
            pltpu.VMEM((2, 3, 3 * B, B), F32),
            pltpu.VMEM((2, 4, N, B), F32),
            pltpu.SemaphoreType.DMA((2, 4)),
            pltpu.SemaphoreType.DMA((4,)),
            pltpu.SemaphoreType.DMA((2,)),
        ],
        compiler_params=pltpu.CompilerParams(vmem_limit_bytes=60 * 1024 * 1024),
        name="fields",
    )(src, rec, codes, sums, table, right, left)


def image_kernel(factor, fields, out, raw, pad, buf, r1, r2, r3, fa, fb,
                 lsem, esend, erecv, ssem, rsem, fsend, frecv):
    depth = lax.axis_index("depth")
    freq = lax.axis_index("freq")
    core = depth % 2
    other = depth + 1 - 2 * core
    x, z, yh = freq % 4, (freq // 4) % 4, freq // 16
    ring = (
        freq - x + (x + 1 - 2 * (x % 2)),
        freq - x + (3 - x),
        freq - 4 * z + 4 * (z + 1 - 2 * (z % 2)),
        freq - 4 * z + 4 * (3 - z),
    )
    far = freq - 16 * yh + 16 * (1 - yh)
    far_ring = [r - 16 * yh + 16 * (1 - yh) for r in ring]

    def bits(ix, iz):
        return [((ix + 1) // 2) % 2, ix // 2, ((iz + 1) // 2) % 2, iz // 2]

    mine = bits(x, z)

    barrier = pltpu.get_barrier_semaphore()
    peers = [(other, freq), (depth, far)]
    for i in range(4):
        peers += [(depth, ring[i]), (other, ring[i]), (depth, far_ring[i])]
    for who in peers:
        pl.semaphore_signal(barrier, inc=1, device_id=who, device_id_type=MESH)

    def window(i, side):
        return pl.ds(pl.multiple_of(side * 240, 16), 272)

    def keep(i):
        return pltpu.make_async_copy(
            fields.at[core, :, :, i, window(i, mine[i])], raw.at[i, 0], lsem.at[i])

    def hand(i, n):
        plane = (1 - core, core, 1 - core)[n]
        side = (mine[i], 1 - mine[i], 1 - mine[i])[n]
        who = ((other, freq), (depth, ring[i]), (other, ring[i]))[n]
        return pltpu.make_async_remote_copy(
            src_ref=fields.at[plane, :, :, i, window(i, side)], dst_ref=raw.at[i, n + 1],
            send_sem=esend.at[i, n], recv_sem=erecv.at[i, n],
            device_id=who, device_id_type=MESH)

    for i in range(4):
        keep(i).start()
    pl.semaphore_wait(barrier, len(peers))
    for n in (1, 2, 0):
        for i in range(4):
            hand(i, n).start()

    for i in range(4):
        for s in range(4):
            for k in range(2):
                for p in range(2):
                    pad[i, s, k, p, 0:8, :] = jnp.zeros((8, B), F32)
                    pad[i, s, k, p, 280:288, :] = jnp.zeros((8, B), F32)

    def widen(i, s):
        for k in range(2):
            for p in range(2):
                pad[i, s, k, p, 8:280, :] = raw[i, s, k, p].astype(F32)

    for i in range(4):
        keep(i).wait()
        widen(i, 0)
    for n in range(3):
        for i in range(4):
            hand(i, n).wait_recv()
            widen(i, n + 1)

    def weight(d, i):
        return (1, 8, 4, 2)[(d - i) % 4]

    flip_x = [[(mine[d] + bits(v, 0)[d]) % 2 for d in range(2)] for v in range(4)]
    slot_x = [[sum(flip_x[v][d] * weight(d, i) for d in range(2)) for i in range(4)] for v in range(4)]
    shift = [mine[i] * 16 for i in range(4)]

    def produce(g):
        def body(n, carry):
            theirs = bits(0, n)
            flip_z = [(mine[d] + theirs[d]) % 2 for d in (2, 3)]
            slot_z = [sum(flip_z[d - 2] * weight(d, i) for d in (2, 3)) for i in range(4)]
            for v in range(4):
                for i in range(4):
                    row = pl.multiple_of(n * 64 + v * 16 + shift[i], 16)
                    slot = slot_z[i] + slot_x[v][i]
                    for l in range(PER):
                        h = g * PER + l - LAG
                        total = None
                        for s in range(4):
                            for p in range(2):
                                left = pad[i, s, 0, p, pl.ds(row + (8 - h), 16), :]
                                right = pad[i, s, 1, p, pl.ds(row + (8 + h), 16), :]
                                term = left * right
                                total = term if total is None else total + term
                        buf[g, i, slot, l] = total.astype(BF16)
            return carry
        lax.fori_loop(0, 4, body, 0)

    recv = (None, r1, r2, r3)

    def copy(g, i, t):
        half = 16 >> t
        return pltpu.make_async_remote_copy(
            src_ref=buf.at[g, i, pl.ds(half, half)], dst_ref=recv[t].at[g, i],
            send_sem=ssem.at[g, i, t - 1], recv_sem=rsem.at[g, i, t - 1],
            device_id=(depth, ring[(i + t) % 4]), device_id_type=MESH)

    def last(g, i, slot, who, place):
        return pltpu.make_async_remote_copy(
            src_ref=buf.at[g, i, slot], dst_ref=(fa, fb)[place].at[g, i],
            send_sem=fsend.at[g, i, slot], recv_sem=frecv.at[g, i, place],
            device_id=who, device_id_type=MESH)

    at_home = [mine[i] == yh for i in range(4)]

    def sends_last(g, i, act):
        @pl.when(at_home[i])
        def _():
            act(last(g, i, 1, (depth, ring[i]), 0))

        @pl.when(jnp.logical_not(at_home[i]))
        def _():
            act(last(g, i, 0, (depth, far), 0))
            act(last(g, i, 1, (depth, far_ring[i]), 1))

    def arrive(g, i, t):
        copy(g, i, t).wait_recv()
        half = 16 >> t

        def body(n, carry):
            for k in (half - 1 - 2 * n, half - 2 - 2 * n):
                buf[g, i, k] = buf[g, i, k] + recv[t][g, i, k]
            return carry
        lax.fori_loop(0, half // 2, body, 0)
        if t < 3:
            copy(g, i, t + 1).start()
        else:
            sends_last(g, i, lambda c: c.start())

    def finish(g, i):
        last(g, i, 0, (depth, far), 0).wait_recv()
        put = (slice(g * PER, (g + 1) * PER), slice(None), slice(i * B, (i + 1) * B))

        @pl.when(at_home[i])
        def _():
            out[put] = (buf[g, i, 0].astype(F32) + fa[g, i].astype(F32)) * factor

        @pl.when(jnp.logical_not(at_home[i]))
        def _():
            last(g, i, 1, (depth, far_ring[i]), 1).wait_recv()
            out[put] = (fa[g, i].astype(F32) + fb[g, i].astype(F32)) * factor

    for g in range(GROUPS):
        produce(g)
        for i in range(4):
            copy(g, i, 1).start()
    for w in range(1, GROUPS + 4):
        for t in range(4, 0, -1):
            g = w - t
            if 0 <= g < GROUPS:
                for i in range(4):
                    if t == 4:
                        finish(g, i)
                    else:
                        arrive(g, i, t)
    for i in range(4):
        for n in range(3):
            hand(i, n).wait_send()
    for g in range(GROUPS):
        for i in range(4):
            for t in (1, 2, 3):
                copy(g, i, t).wait_send()
            sends_last(g, i, lambda c: c.wait_send())


def make_image(fields, factor):
    hbm = pl.BlockSpec(memory_space=pl.ANY)
    strip = (PER, 16, B)
    return pl.pallas_call(
        functools.partial(image_kernel, factor),
        out_shape=jax.ShapeDtypeStruct((LAGS, 16, N), F32),
        in_specs=[hbm],
        out_specs=pl.BlockSpec(memory_space=pltpu.VMEM),
        scratch_shapes=[
            pltpu.VMEM((4, 4, 2, 2, 272, B), BF16),
            pltpu.VMEM((4, 4, 2, 2, 288, B), F32),
            pltpu.VMEM((GROUPS, 4, 16) + strip, BF16),
            pltpu.VMEM((GROUPS, 4, 8) + strip, BF16),
            pltpu.VMEM((GROUPS, 4, 4) + strip, BF16),
            pltpu.VMEM((GROUPS, 4, 2) + strip, BF16),
            pltpu.VMEM((GROUPS, 4) + strip, BF16),
            pltpu.VMEM((GROUPS, 4) + strip, BF16),
            pltpu.SemaphoreType.DMA((4,)),
            pltpu.SemaphoreType.DMA((4, 3)),
            pltpu.SemaphoreType.DMA((4, 3)),
            pltpu.SemaphoreType.DMA((GROUPS, 4, 3)),
            pltpu.SemaphoreType.DMA((GROUPS, 4, 3)),
            pltpu.SemaphoreType.DMA((GROUPS, 4, 2)),
            pltpu.SemaphoreType.DMA((GROUPS, 4, 2)),
        ],
        compiler_params=pltpu.CompilerParams(
            collective_id=1, has_side_effects=True, vmem_limit_bytes=60 * 1024 * 1024),
        name="image",
    )(fields)


def shards(source_top, receiver_top, slowness_codes, slowness_table, anchors):
    right, left = butterfly_matrices()
    right = jnp.asarray(right, BF16)
    left = jnp.asarray(left, BF16)
    windows, means = make_windows(slowness_codes, slowness_table, anchors)
    codes, sums = exchange(windows, means)
    fields = make_fields(source_top, receiver_top, codes, sums, slowness_table, right, left)
    image = make_image(fields, 1.0 / math.sqrt(128.0))
    return image[None]


def solution(mesh):
    return jax.shard_map(
        shards,
        mesh=mesh,
        in_specs=(
            P(None, "freq", None, None, None),
            P(None, "freq", None, None, None),
            P("depth", None, None),
            P(),
            P(),
        ),
        out_specs=P("depth", None, "freq", None),
        check_vma=False,
    )
```

```python
import functools
import math

import jax
import jax.numpy as jnp
import numpy as np
from jax import lax
from jax.experimental import pallas as pl
from jax.experimental.pallas import tpu as pltpu
from jax.sharding import PartitionSpec as P

LAG = 7
LAGS = 2 * LAG + 1
N = 512
B = 128
GROUPS = 5
PER = LAGS // GROUPS
MESH = pl.DeviceIdType.MESH
F32 = jnp.float32
BF16 = jnp.bfloat16


def butterfly_matrices():
    j = np.arange(B)[:, None]
    k = np.arange(B)[None, :]
    mats = []
    for wave in (4 * k, 4 * k + 1, 4 * k + 2, -(4 * k + 1)):
        angle = 2.0 * np.pi * ((j * wave) % N) / N
        c = np.cos(angle) / math.sqrt(N)
        s = np.sin(angle) / math.sqrt(N)
        mats.append(np.block([[c, -s], [s, c]]))
    right = np.stack(mats)
    return right, np.swapaxes(right, 1, 2)


def even_poly(first, terms, top, samples=400):
    q = (np.cos(np.pi * (np.arange(samples) + 0.5) / samples) + 1.0) * 0.5 * top
    r = np.sqrt(q)
    want = np.cos(r) if first == 0 else np.sin(r) / r
    fit = np.polynomial.Chebyshev.fit(q, want, terms, domain=[0, top])
    return [float(v) for v in fit.convert(kind=np.polynomial.Polynomial).coef]


COS_Q = even_poly(0, 9, 14.0)
SIN_Q = even_poly(1, 9, 14.0)


def horner(coefs, q):
    value = coefs[-1] * q + coefs[-2]
    for c in coefs[-3::-1]:
        value = value * q + c
    return value


def split4(re, im):
    er, ei, dr, di = re[0] + re[2], im[0] + im[2], re[0] - re[2], im[0] - im[2]
    fr, fi, gr, gi = re[1] + re[3], im[1] + im[3], re[1] - re[3], im[1] - im[3]
    return (er + fr, dr + gi, er - fr, dr - gi), (ei + fi, di - gr, ei - fi, di + gr)


def join4(re, im):
    er, ei, dr, di = re[0] + re[2], im[0] + im[2], re[0] - re[2], im[0] - im[2]
    fr, fi, gr, gi = re[1] + re[3], im[1] + im[3], re[1] - re[3], im[1] - im[3]
    return (er + fr, dr - gi, er - fr, dr + gi), (ei + fi, di + gr, ei - fi, di - gr)


def level_row(table):
    lane = lax.broadcasted_iota(jnp.int32, (8, B), 1)
    levels = jnp.zeros((8, B), F32)
    for k in range(32):
        levels = jnp.where(lane == k, table[k], levels)
    return levels


TAKE = lax.GatherDimensionNumbers(
    offset_dims=(), collapsed_slice_dims=(1,), start_index_map=(1,),
    operand_batching_dims=(0,), start_indices_batching_dims=(0,))


def lookup(values, index):
    return lax.gather(
        jnp.tile(values, (index.shape[0] // 8, 1)), index[..., None], TAKE, (1, 1),
        mode=lax.GatherScatterMode.PROMISE_IN_BOUNDS)


def windows_kernel(codes, table, anchors, out, means, raw, sem):
    def fetch(s, h):
        ox = pl.multiple_of(anchors[s, 0], N)
        oy = pl.multiple_of(anchors[s, 1], N)
        return pltpu.make_async_copy(
            codes.at[0, pl.ds(ox + h * 256, 256), pl.ds(oy, N)], raw.at[s, h], sem.at[s, h])

    for s in range(2):
        for h in range(2):
            fetch(s, h).start()
    levels = level_row(table)
    for s in range(2):
        total = jnp.zeros((8, B), F32)
        for h in range(2):
            fetch(s, h).wait()

            def rows_of(n, total):
                take = pl.ds(pl.multiple_of(n * 32, 32), 32)
                for q in range(4):
                    index = raw[s, h, take, q * B:(q + 1) * B]
                    out[s, pl.ds(pl.multiple_of(h * 256 + n * 32, 32), 32), q * B:(q + 1) * B] = (
                        index.astype(F32).astype(BF16))
                    got = lookup(levels, index)
                    total = total + (got[0:8] + got[8:16]) + (got[16:24] + got[24:32])
                return total

            total = lax.fori_loop(0, 8, rows_of, total)
        means[s] = jnp.full((8, B), jnp.sum(total) * (1.0 / (N * N)), F32)


def make_windows(codes, table, anchors):
    vmem = pl.BlockSpec(memory_space=pltpu.VMEM)
    smem = pl.BlockSpec(memory_space=pltpu.SMEM)
    return pl.pallas_call(
        windows_kernel,
        out_shape=(
            jax.ShapeDtypeStruct((2, N, N), BF16),
            jax.ShapeDtypeStruct((2, 8, B), F32),
        ),
        in_specs=[pl.BlockSpec(memory_space=pl.ANY), smem, smem],
        out_specs=(vmem, vmem),
        scratch_shapes=[pltpu.VMEM((2, 2, 256, N), jnp.int32), pltpu.SemaphoreType.DMA((2, 2))],
        compiler_params=pltpu.CompilerParams(vmem_limit_bytes=60 * 1024 * 1024),
        name="windows",
    )(codes, table, anchors)


def exchange_kernel(win, means, out, outm, lsem, ssem, rsem, msend, mrecv):
    depth = lax.axis_index("depth")
    freq = lax.axis_index("freq")
    core = depth % 2
    section = depth // 2
    flipped = (freq + 16) % 32
    sibling = (depth + 1 - 2 * core, freq)
    half = N // 2
    up = lambda s: (2 * (1 - section) + s, freq)
    down = lambda s: (2 * (1 - section) + s, flipped)

    barrier = pltpu.get_barrier_semaphore()
    for who in (sibling, up(0), up(1), down(0), down(1)):
        pl.semaphore_signal(barrier, inc=1, device_id=who, device_id_type=MESH)
    pl.semaphore_wait(barrier, 5)

    def to_section(s, way):
        rows = pl.ds(way * half, half)
        who = (up(s), down(s))[way]
        return (
            pltpu.make_async_remote_copy(
                src_ref=win.at[s, rows], dst_ref=out.at[core, rows],
                send_sem=ssem.at[s, way], recv_sem=rsem.at[core, way],
                device_id=who, device_id_type=MESH),
        )

    def means_to_section(s):
        return pltpu.make_async_remote_copy(
            src_ref=means.at[s], dst_ref=outm.at[core],
            send_sem=msend.at[s], recv_sem=mrecv.at[core],
            device_id=up(s), device_id_type=MESH)

    @pl.when(section == 0)
    def _():
        for s in range(2):
            means_to_section(s).start()
            for way in range(2):
                for copy in to_section(s, way):
                    copy.start()

    swap = pltpu.make_async_remote_copy(
        src_ref=win.at[1 - core], dst_ref=out.at[depth],
        send_sem=ssem.at[2, 0], recv_sem=rsem.at[2, 0], device_id=sibling, device_id_type=MESH)
    swap.start()
    swap_means = pltpu.make_async_remote_copy(
        src_ref=means.at[1 - core], dst_ref=outm.at[depth],
        send_sem=msend.at[2], recv_sem=mrecv.at[2], device_id=sibling, device_id_type=MESH)
    swap_means.start()
    keep = pltpu.make_async_copy(win.at[core], out.at[depth], lsem)
    keep.start()
    outm[depth] = means[core]
    keep.wait()

    swap.wait()
    swap_means.wait()

    @pl.when(section == 0)
    def _():
        for s in range(2):
            means_to_section(s).wait_send()
            for way in range(2):
                for copy in to_section(s, way):
                    copy.wait_send()

    @pl.when(section == 1)
    def _():
        for plane in range(2):
            pltpu.make_async_copy(outm.at[plane], outm.at[plane], mrecv.at[plane]).wait()
            for way in range(2):
                rows = pl.ds(way * half, half)
                pltpu.make_async_copy(out.at[plane, rows], out.at[plane, rows], rsem.at[plane, way]).wait()


def exchange(win, means):
    vmem = pl.BlockSpec(memory_space=pltpu.VMEM)
    return pl.pallas_call(
        exchange_kernel,
        out_shape=(
            jax.ShapeDtypeStruct((4, N, N), BF16),
            jax.ShapeDtypeStruct((4, 8, B), F32),
        ),
        in_specs=[vmem, vmem],
        out_specs=(vmem, vmem),
        scratch_shapes=[
            pltpu.SemaphoreType.DMA,
            pltpu.SemaphoreType.DMA((3, 2)),
            pltpu.SemaphoreType.DMA((3, 2)),
            pltpu.SemaphoreType.DMA((3,)),
            pltpu.SemaphoreType.DMA((3,)),
        ],
        compiler_params=pltpu.CompilerParams(
            collective_id=2, has_side_effects=True, vmem_limit_bytes=60 * 1024 * 1024),
        name="exchange",
    )(win, means)


def fields_kernel(
    src, rec, codes, sums, table, right_ref, left_ref, out,
    u, a, cbuf, ph, sc, tsem, csem, osem,
):
    depth = lax.axis_index("depth")
    core = depth % 2
    first_plane = (depth // 2) * 2
    steps = first_plane + 2
    position = lax.axis_index("freq").astype(F32)
    angular = math.pi * (0.45 + 0.5 * (position + 0.5) / 32.0)

    tops = []
    for kind, top in enumerate((src, rec)):
        for q in range(4):
            tops.append(pltpu.make_async_copy(
                top.at[core, 0, :, :, pl.ds(q * B, B)], u.at[kind, :, q], tsem.at[kind, q]))
    for copy in tops:
        copy.start()
    for z in range(4):
        pltpu.make_async_copy(codes.at[z], cbuf.at[z], csem.at[z]).start()

    levels = level_row(table)
    angle = angular * levels
    squared = angle * angle
    cos_levels = horner(COS_Q, squared)
    sin_levels = angle * horner(SIN_Q, squared)

    for copy in tops:
        copy.wait()

    def step(z, carry):
        pltpu.make_async_copy(codes.at[z], cbuf.at[z], csem.at[z]).wait()
        base = sums[z, 0:1, :]
        turn = angular * base
        turn_sq = turn * turn
        turn_re = horner(COS_Q, turn_sq)
        turn_im = turn * horner(SIN_Q, turn_sq)

        def operators(n, carry):
            rows = n * 24
            k = rows + lax.broadcasted_iota(jnp.int32, (24, B), 0)
            kx = (k % B) * 4 + k // B
            kx = jnp.where(kx < N // 2, kx, kx - N).astype(F32) * (2.0 * math.pi / N)
            left_q = turn_sq - kx * kx
            for ry in range(3):
                ky = lax.broadcasted_iota(jnp.int32, (1, B), 1) * 4 + ry
                ky = jnp.where(ky < N // 2, ky, ky - N).astype(F32) * (2.0 * math.pi / N)
                q = left_q - ky * ky
                root = jnp.sqrt(jnp.abs(q))
                wave = jnp.maximum(q, 0.0)
                travels = q >= 0.0
                pre = jnp.where(travels, horner(COS_Q, wave), jnp.exp(-root))
                pim = jnp.where(travels, root * horner(SIN_Q, wave), 0.0)
                put = pl.ds(pl.multiple_of(rows, 8), 24)
                ph[0, ry, put, :] = pre * turn_re + pim * turn_im
                ph[1, ry, put, :] = pim * turn_re - pre * turn_im
            take = pl.ds(pl.multiple_of(n * 32, 32), 32)
            for q in range(4):
                index = cbuf[z, take, q * B:(q + 1) * B].astype(jnp.int32)
                sc[0, q, take, :] = lookup(cos_levels, index)
                sc[1, q, take, :] = lookup(sin_levels, index)
            return carry

        lax.fori_loop(0, 16, operators, 0)

        def wide(ref, kind, p, half, block):
            rows = slice(block * B, (block + 1) * B)
            return jnp.concatenate([ref[kind, p, half * 2, rows, :], ref[kind, p, half * 2 + 1, rows, :]], axis=1)

        def put_wide(ref, kind, p, half, block, value):
            rows = slice(block * B, (block + 1) * B)
            ref[kind, p, half * 2, rows, :] = value[:, :B]
            ref[kind, p, half * 2 + 1, rows, :] = value[:, B:]

        def forward_x(n, carry):
            kind, half = n // 2, n % 2
            re = [wide(u, kind, 0, half, q) for q in range(4)]
            im = [wide(u, kind, 1, half, q) for q in range(4)]
            sre, sim = split4(re, im)
            for r in range(4):
                got = jnp.dot(left_ref[r], jnp.concatenate([sre[r], sim[r]], axis=0),
                              preferred_element_type=F32).astype(BF16)
                put_wide(a, kind, 0, half, r, got[:B])
                put_wide(a, kind, 1, half, r, got[B:])
            return carry

        lax.fori_loop(0, 4, forward_x, 0)

        def along_y(n, carry):
            kind, rx = n // 4, n % 4
            sign = (1 - 2 * kind).astype(F32)
            prow = pl.ds(pl.multiple_of(jnp.where(rx == 3, 1, rx) * B, B), B)
            rows = pl.ds(pl.multiple_of(rx * B, B), B)
            re = [a[kind, 0, q, rows, :] for q in range(4)]
            im = [a[kind, 1, q, rows, :] for q in range(4)]
            sre, sim = split4(re, im)
            tre, tim = [], []
            for r in range(4):
                got = jnp.dot(jnp.concatenate([sre[r], sim[r]], axis=1), right_ref[r],
                              preferred_element_type=F32)
                gre, gim = got[:, :B], got[:, B:]
                py = 1 if r == 3 else r
                pre, pim = ph[0, py, prow, :], ph[1, py, prow, :] * sign
                turned = jnp.concatenate(
                    [(gre * pre - gim * pim).astype(BF16), (gre * pim + gim * pre).astype(BF16)], axis=1)
                back = jnp.dot(turned, left_ref[r], preferred_element_type=F32)
                tre.append(back[:, :B])
                tim.append(back[:, B:])
            cre, cim = join4(tre, tim)
            for q in range(4):
                a[kind, 0, q, rows, :] = cre[q].astype(BF16)
                a[kind, 1, q, rows, :] = cim[q].astype(BF16)
            return carry

        lax.fori_loop(0, 8, along_y, 0)

        @pl.when(z > first_plane)
        def _():
            pltpu.make_async_copy(u, out.at[0], osem.at[0]).wait()

        def inverse_x(n, carry):
            kind, half = n // 2, n % 2
            sign = (1 - 2 * kind).astype(F32)
            tre, tim = [], []
            for r in range(4):
                data = jnp.concatenate([wide(a, kind, 0, half, r), wide(a, kind, 1, half, r)], axis=0)
                got = jnp.dot(right_ref[r], data, preferred_element_type=F32)
                tre.append(got[:B])
                tim.append(got[B:])
            xre, xim = join4(tre, tim)
            for q in range(4):
                rows = slice(q * B, (q + 1) * B)
                for part in range(2):
                    cols = slice(part * B, (part + 1) * B)
                    cre = sc[0, half * 2 + part, rows, :]
                    cim = sc[1, half * 2 + part, rows, :] * sign
                    gre, gim = xre[q][:, cols], xim[q][:, cols]
                    u[kind, 0, half * 2 + part, rows, :] = (gre * cre - gim * cim).astype(BF16)
                    u[kind, 1, half * 2 + part, rows, :] = (gre * cim + gim * cre).astype(BF16)
            return carry

        lax.fori_loop(0, 4, inverse_x, 0)

        @pl.when(z == first_plane)
        def _():
            pltpu.make_async_copy(u, out.at[0], osem.at[0]).start()

        @pl.when(z == first_plane + 1)
        def _():
            pltpu.make_async_copy(u, out.at[1], osem.at[1]).start()

        return carry

    lax.fori_loop(0, steps, step, 0)

    def drain(z, carry):
        pltpu.make_async_copy(codes.at[z], cbuf.at[z], csem.at[z]).wait()
        return carry

    lax.fori_loop(steps, 4, drain, 0)
    pltpu.make_async_copy(u, out.at[1], osem.at[1]).wait()


def make_fields(src, rec, codes, sums, table, right, left):
    vmem = pl.BlockSpec(memory_space=pltpu.VMEM)
    hbm = pl.BlockSpec(memory_space=pl.ANY)
    return pl.pallas_call(
        fields_kernel,
        out_shape=jax.ShapeDtypeStruct((2, 2, 2, 4, N, B), BF16),
        in_specs=[hbm, hbm, hbm, vmem, pl.BlockSpec(memory_space=pltpu.SMEM), vmem, vmem],
        out_specs=hbm,
        scratch_shapes=[
            pltpu.VMEM((2, 2, 4, N, B), BF16),
            pltpu.VMEM((2, 2, 4, N, B), BF16),
            pltpu.VMEM((4, N, N), BF16),
            pltpu.VMEM((2, 3, 3 * B, B), F32),
            pltpu.VMEM((2, 4, N, B), F32),
            pltpu.SemaphoreType.DMA((2, 4)),
            pltpu.SemaphoreType.DMA((4,)),
            pltpu.SemaphoreType.DMA((2,)),
        ],
        compiler_params=pltpu.CompilerParams(vmem_limit_bytes=60 * 1024 * 1024),
        name="fields",
    )(src, rec, codes, sums, table, right, left)


def image_kernel(factor, fields, out, raw, pad, buf, r1, r2, r3, fa, fb,
                 lsem, esend, erecv, ssem, rsem, fsend, frecv):
    depth = lax.axis_index("depth")
    freq = lax.axis_index("freq")
    core = depth % 2
    other = depth + 1 - 2 * core
    x, z, yh = freq % 4, (freq // 4) % 4, freq // 16
    ring = (
        freq - x + (x + 1 - 2 * (x % 2)),
        freq - x + (3 - x),
        freq - 4 * z + 4 * (z + 1 - 2 * (z % 2)),
        freq - 4 * z + 4 * (3 - z),
    )
    far = freq - 16 * yh + 16 * (1 - yh)
    far_ring = [r - 16 * yh + 16 * (1 - yh) for r in ring]

    def bits(ix, iz):
        return [((ix + 1) // 2) % 2, ix // 2, ((iz + 1) // 2) % 2, iz // 2]

    mine = bits(x, z)
    side = mine

    barrier = pltpu.get_barrier_semaphore()
    peers = [(other, freq), (depth, far)]
    for i in range(4):
        peers += [(depth, ring[i]), (other, ring[i]), (depth, far_ring[i])]
    for who in peers:
        pl.semaphore_signal(barrier, inc=1, device_id=who, device_id_type=MESH)

    def window(i, half):
        return pl.ds(pl.multiple_of(half * 240, 16), 272)

    def keep(i):
        return pltpu.make_async_copy(
            fields.at[core, :, :, i, window(i, side[i])], raw.at[i, 0], lsem.at[i])

    def hand(i, n):
        plane = (1 - core, core, 1 - core)[n]
        half = (side[i], 1 - side[i], 1 - side[i])[n]
        who = ((other, freq), (depth, ring[i]), (other, ring[i]))[n]
        return pltpu.make_async_remote_copy(
            src_ref=fields.at[plane, :, :, i, window(i, half)], dst_ref=raw.at[i, n + 1],
            send_sem=esend.at[i, n], recv_sem=erecv.at[i, n],
            device_id=who, device_id_type=MESH)

    for i in range(4):
        keep(i).start()
    pl.semaphore_wait(barrier, len(peers))
    for n in (1, 2, 0):
        for i in range(4):
            hand(i, n).start()

    for i in range(4):
        for s in range(4):
            for k in range(2):
                for p in range(2):
                    pad[i, s, k, p, 0:8, :] = jnp.zeros((8, B), F32)
                    pad[i, s, k, p, 280:288, :] = jnp.zeros((8, B), F32)

    def widen(i, s):
        for k in range(2):
            for p in range(2):
                pad[i, s, k, p, 8:280, :] = raw[i, s, k, p].astype(F32)

    for i in range(4):
        keep(i).wait()
        widen(i, 0)
    for n in range(3):
        for i in range(4):
            hand(i, n).wait_recv()
            widen(i, n + 1)

    def weight(d, i):
        return (1, 8, 4, 2)[(d - i) % 4]

    flip_x = [[(mine[d] + bits(v, 0)[d]) % 2 for d in range(2)] for v in range(4)]
    slot_x = [[sum(flip_x[v][d] * weight(d, i) for d in range(2)) for i in range(4)] for v in range(4)]
    shift = [side[i] * 16 for i in range(4)]

    def produce(g):
        def body(n, carry):
            theirs = bits(0, n)
            flip_z = [(mine[d] + theirs[d]) % 2 for d in (2, 3)]
            slot_z = [sum(flip_z[d - 2] * weight(d, i) for d in (2, 3)) for i in range(4)]
            for v in range(4):
                for i in range(4):
                    row = pl.multiple_of(n * 64 + v * 16 + shift[i], 16)
                    slot = slot_z[i] + slot_x[v][i]
                    for l in range(PER):
                        h = g * PER + l - LAG
                        total = None
                        for s in range(4):
                            for p in range(2):
                                left = pad[i, s, 0, p, pl.ds(row + (8 - h), 16), :]
                                right = pad[i, s, 1, p, pl.ds(row + (8 + h), 16), :]
                                term = left * right
                                total = term if total is None else total + term
                        buf[g, i, slot, l] = total.astype(BF16)
            return carry
        lax.fori_loop(0, 4, body, 0)

    recv = (None, r1, r2, r3)

    def copy(g, i, t):
        half = 16 >> t
        return pltpu.make_async_remote_copy(
            src_ref=buf.at[g, i, pl.ds(half, half)], dst_ref=recv[t].at[g, i],
            send_sem=ssem.at[g, i, t - 1], recv_sem=rsem.at[g, i, t - 1],
            device_id=(depth, ring[(i + t) % 4]), device_id_type=MESH)

    def last(i, slot, who, place):
        return pltpu.make_async_remote_copy(
            src_ref=buf.at[:, i, slot], dst_ref=(fa, fb)[place].at[i],
            send_sem=fsend.at[i, slot], recv_sem=frecv.at[i, place],
            device_id=who, device_id_type=MESH)

    at_home = [side[i] == yh for i in range(4)]

    def sends_last(i, act):
        @pl.when(at_home[i])
        def _():
            act(last(i, 1, (depth, ring[i]), 0))

        @pl.when(jnp.logical_not(at_home[i]))
        def _():
            act(last(i, 0, (depth, far), 0))
            act(last(i, 1, (depth, far_ring[i]), 1))

    def arrive(g, i, t):
        copy(g, i, t).wait_recv()
        half = 16 >> t

        def body(n, carry):
            for k in (half - 1 - 2 * n, half - 2 - 2 * n):
                buf[g, i, k] = buf[g, i, k] + recv[t][g, i, k]
            return carry
        lax.fori_loop(0, half // 2, body, 0)
        if t < 3:
            copy(g, i, t + 1).start()

    def finish(i):
        last(i, 0, (depth, far), 0).wait_recv()
        cols = slice(i * B, (i + 1) * B)

        @pl.when(at_home[i])
        def _():
            for g in range(GROUPS):
                out[g * PER:(g + 1) * PER, :, cols] = (buf[g, i, 0].astype(F32) + fa[i, g].astype(F32)) * factor

        @pl.when(jnp.logical_not(at_home[i]))
        def _():
            last(i, 1, (depth, far_ring[i]), 1).wait_recv()
            for g in range(GROUPS):
                out[g * PER:(g + 1) * PER, :, cols] = (fa[i, g].astype(F32) + fb[i, g].astype(F32)) * factor

    for g in range(GROUPS):
        produce(g)
        for i in range(4):
            copy(g, i, 1).start()
        if g >= 2:
            for i in range(4):
                arrive(g - 2, i, 1)
    for g in range(GROUPS - 2, GROUPS):
        for i in range(4):
            arrive(g, i, 1)
    for t in (2, 3):
        for g in range(GROUPS):
            for i in range(4):
                arrive(g, i, t)
                if t == 3 and g == GROUPS - 1:
                    sends_last(i, lambda c: c.start())
    for i in range(4):
        finish(i)
    for i in range(4):
        for n in range(3):
            hand(i, n).wait_send()
    for g in range(GROUPS):
        for i in range(4):
            for t in (1, 2, 3):
                copy(g, i, t).wait_send()
    for i in range(4):
        sends_last(i, lambda c: c.wait_send())


def make_image(fields, factor):
    hbm = pl.BlockSpec(memory_space=pl.ANY)
    strip = (PER, 16, B)
    return pl.pallas_call(
        functools.partial(image_kernel, factor),
        out_shape=jax.ShapeDtypeStruct((LAGS, 16, N), F32),
        in_specs=[hbm],
        out_specs=pl.BlockSpec(memory_space=pltpu.VMEM),
        scratch_shapes=[
            pltpu.VMEM((4, 4, 2, 2, 272, B), BF16),
            pltpu.VMEM((4, 4, 2, 2, 288, B), F32),
            pltpu.VMEM((GROUPS, 4, 16) + strip, BF16),
            pltpu.VMEM((GROUPS, 4, 8) + strip, BF16),
            pltpu.VMEM((GROUPS, 4, 4) + strip, BF16),
            pltpu.VMEM((GROUPS, 4, 2) + strip, BF16),
            pltpu.VMEM((4, GROUPS) + strip, BF16),
            pltpu.VMEM((4, GROUPS) + strip, BF16),
            pltpu.SemaphoreType.DMA((4,)),
            pltpu.SemaphoreType.DMA((4, 3)),
            pltpu.SemaphoreType.DMA((4, 3)),
            pltpu.SemaphoreType.DMA((GROUPS, 4, 3)),
            pltpu.SemaphoreType.DMA((GROUPS, 4, 3)),
            pltpu.SemaphoreType.DMA((4, 2)),
            pltpu.SemaphoreType.DMA((4, 2)),
        ],
        compiler_params=pltpu.CompilerParams(
            collective_id=1, has_side_effects=True, vmem_limit_bytes=60 * 1024 * 1024),
        name="image",
    )(fields)


def shards(source_top, receiver_top, slowness_codes, slowness_table, anchors):
    right, left = butterfly_matrices()
    right = jnp.asarray(right, BF16)
    left = jnp.asarray(left, BF16)
    windows, means = make_windows(slowness_codes, slowness_table, anchors)
    codes, sums = exchange(windows, means)
    fields = make_fields(source_top, receiver_top, codes, sums, slowness_table, right, left)
    image = make_image(fields, 1.0 / math.sqrt(128.0))
    return image[None]


def solution(mesh):
    return jax.shard_map(
        shards,
        mesh=mesh,
        in_specs=(
            P(None, "freq", None, None, None),
            P(None, "freq", None, None, None),
            P("depth", None, None),
            P(),
            P(),
        ),
        out_specs=P("depth", None, "freq", None),
        check_vma=False,
    )
```

```python
import functools
import math

import jax
import jax.numpy as jnp
import numpy as np
from jax import lax
from jax.experimental import pallas as pl
from jax.experimental.pallas import tpu as pltpu
from jax.sharding import PartitionSpec as P

LAG = 7
LAGS = 2 * LAG + 1
N = 512
B = 128
GROUPS = 5
PER = LAGS // GROUPS
MESH = pl.DeviceIdType.MESH
F32 = jnp.float32
BF16 = jnp.bfloat16


def butterfly_matrices():
    j = np.arange(B)[:, None]
    k = np.arange(B)[None, :]
    mats = []
    for wave in (4 * k, 4 * k + 1, 4 * k + 2, -(4 * k + 1)):
        angle = 2.0 * np.pi * ((j * wave) % N) / N
        c = np.cos(angle) / math.sqrt(N)
        s = np.sin(angle) / math.sqrt(N)
        mats.append(np.block([[c, -s], [s, c]]))
    right = np.stack(mats)
    return right, np.swapaxes(right, 1, 2)


def even_poly(first, terms, top, samples=400):
    q = (np.cos(np.pi * (np.arange(samples) + 0.5) / samples) + 1.0) * 0.5 * top
    r = np.sqrt(q)
    want = np.cos(r) if first == 0 else np.sin(r) / r
    fit = np.polynomial.Chebyshev.fit(q, want, terms, domain=[0, top])
    return [float(v) for v in fit.convert(kind=np.polynomial.Polynomial).coef]


COS_Q = even_poly(0, 6, 14.0)
SIN_Q = even_poly(1, 6, 14.0)


def horner(coefs, q):
    value = coefs[-1] * q + coefs[-2]
    for c in coefs[-3::-1]:
        value = value * q + c
    return value


def split4(re, im):
    er, ei, dr, di = re[0] + re[2], im[0] + im[2], re[0] - re[2], im[0] - im[2]
    fr, fi, gr, gi = re[1] + re[3], im[1] + im[3], re[1] - re[3], im[1] - im[3]
    return (er + fr, dr + gi, er - fr, dr - gi), (ei + fi, di - gr, ei - fi, di + gr)


def join4(re, im):
    er, ei, dr, di = re[0] + re[2], im[0] + im[2], re[0] - re[2], im[0] - im[2]
    fr, fi, gr, gi = re[1] + re[3], im[1] + im[3], re[1] - re[3], im[1] - im[3]
    return (er + fr, dr - gi, er - fr, dr + gi), (ei + fi, di + gr, ei - fi, di - gr)


def level_row(table):
    lane = lax.broadcasted_iota(jnp.int32, (8, B), 1)
    levels = jnp.zeros((8, B), F32)
    for k in range(32):
        levels = jnp.where(lane == k, table[k], levels)
    return levels


TAKE = lax.GatherDimensionNumbers(
    offset_dims=(), collapsed_slice_dims=(1,), start_index_map=(1,),
    operand_batching_dims=(0,), start_indices_batching_dims=(0,))


def lookup(values, index):
    return lax.gather(
        jnp.tile(values, (index.shape[0] // 8, 1)), index[..., None], TAKE, (1, 1),
        mode=lax.GatherScatterMode.PROMISE_IN_BOUNDS)


def windows_kernel(codes, table, anchors, out, means, raw, sem):
    def fetch(s, h):
        ox = pl.multiple_of(anchors[s, 0], N)
        oy = pl.multiple_of(anchors[s, 1], N)
        return pltpu.make_async_copy(
            codes.at[0, pl.ds(ox + h * 256, 256), pl.ds(oy, N)], raw.at[s, h], sem.at[s, h])

    for s in range(2):
        for h in range(2):
            fetch(s, h).start()
    levels = level_row(table)
    for s in range(2):
        total = jnp.zeros((8, B), F32)
        for h in range(2):
            fetch(s, h).wait()

            def rows_of(n, total):
                take = pl.ds(pl.multiple_of(n * 32, 32), 32)
                for q in range(4):
                    index = raw[s, h, take, q * B:(q + 1) * B]
                    out[s, pl.ds(pl.multiple_of(h * 256 + n * 32, 32), 32), q * B:(q + 1) * B] = (
                        index.astype(F32).astype(BF16))
                    got = lookup(levels, index)
                    total = total + (got[0:8] + got[8:16]) + (got[16:24] + got[24:32])
                return total

            total = lax.fori_loop(0, 8, rows_of, total)
        means[s] = jnp.full((8, B), jnp.sum(total) * (1.0 / (N * N)), F32)


def make_windows(codes, table, anchors):
    vmem = pl.BlockSpec(memory_space=pltpu.VMEM)
    smem = pl.BlockSpec(memory_space=pltpu.SMEM)
    return pl.pallas_call(
        windows_kernel,
        out_shape=(
            jax.ShapeDtypeStruct((2, N, N), BF16),
            jax.ShapeDtypeStruct((2, 8, B), F32),
        ),
        in_specs=[pl.BlockSpec(memory_space=pl.ANY), smem, smem],
        out_specs=(vmem, vmem),
        scratch_shapes=[pltpu.VMEM((2, 2, 256, N), jnp.int32), pltpu.SemaphoreType.DMA((2, 2))],
        compiler_params=pltpu.CompilerParams(vmem_limit_bytes=60 * 1024 * 1024),
        name="windows",
    )(codes, table, anchors)


def migrate_kernel(
    factor, src, rec, win, means, table, right_ref, left_ref, out,
    u, a, cbuf, mbuf, ph, sc, raw, pad, buf, r1, r2, r3, fa, fb,
    tsem, csend, crecv, msend, mrecv, esend, erecv, ssem, rsem, fsend, frecv,
):
    depth = lax.axis_index("depth")
    freq = lax.axis_index("freq")
    core = depth % 2
    section = depth // 2
    other = depth + 1 - 2 * core
    x, z, yh = freq % 4, (freq // 4) % 4, freq // 16
    first_plane = section * 2
    steps = first_plane + 2
    ring = (
        freq - x + (x + 1 - 2 * (x % 2)),
        freq - x + (3 - x),
        freq - 4 * z + 4 * (z + 1 - 2 * (z % 2)),
        freq - 4 * z + 4 * (3 - z),
    )
    far = freq - 16 * yh + 16 * (1 - yh)
    far_ring = [r - 16 * yh + 16 * (1 - yh) for r in ring]
    sibling = (other, freq)
    beside = [[(2 * (1 - section) + s, freq) for s in range(2)], [(2 * (1 - section) + s, far) for s in range(2)]]

    def bits(ix, iz):
        return [((ix + 1) // 2) % 2, ix // 2, ((iz + 1) // 2) % 2, iz // 2]

    mine = bits(x, z)
    side = mine

    tops = []
    for kind, top in enumerate((src, rec)):
        for q in range(4):
            tops.append(pltpu.make_async_copy(
                top.at[core, 0, :, :, pl.ds(q * B, B)], u.at[2, kind, :, q], tsem.at[kind, q]))
    for copy_in in tops:
        copy_in.start()

    def half_rows(way):
        return pl.ds(way * (N // 2), N // 2)

    for way in range(2):
        pltpu.make_async_copy(
            win.at[core, half_rows(way)], cbuf.at[depth, half_rows(way)], crecv.at[depth, way]).start()
    mbuf[depth] = means[core]

    barrier = pltpu.get_barrier_semaphore()
    peers = [sibling, (depth, far)] + beside[0] + beside[1]
    for i in range(4):
        peers += [(depth, ring[i]), (other, ring[i]), (depth, far_ring[i])]
    for who in peers:
        pl.semaphore_signal(barrier, inc=1, device_id=who, device_id_type=MESH)

    position = freq.astype(F32)
    angular = math.pi * (0.45 + 0.5 * (position + 0.5) / 32.0)
    levels = level_row(table)
    angle = angular * levels
    squared = angle * angle
    cos_levels = horner(COS_Q, squared)
    sin_levels = angle * horner(SIN_Q, squared)
    pl.semaphore_wait(barrier, len(peers))

    def codes_to(n, way, who):
        shot = (0, 1, 1 - core)[n]
        return pltpu.make_async_remote_copy(
            src_ref=win.at[shot, half_rows(way)], dst_ref=cbuf.at[depth, half_rows(way)],
            send_sem=csend.at[n, way], recv_sem=crecv.at[depth, way],
            device_id=who, device_id_type=MESH)

    def mean_to(n, who):
        shot = (0, 1, 1 - core)[n]
        return pltpu.make_async_remote_copy(
            src_ref=means.at[shot], dst_ref=mbuf.at[depth],
            send_sem=msend.at[n], recv_sem=mrecv.at[depth],
            device_id=who, device_id_type=MESH)

    def section_codes(act):
        for s in range(2):
            for way in range(2):
                act(codes_to(s, way, beside[way][s]))

    mean_to(2, sibling).start()

    @pl.when(section == 0)
    def _():
        for s in range(2):
            mean_to(s, beside[0][s]).start()

    for way in range(2):
        codes_to(2, way, sibling).start()

    @pl.when(jnp.logical_and(section == 0, core == 0))
    def _():
        section_codes(lambda c: c.start())

    def window(i, half):
        return pl.ds(pl.multiple_of(half * 240, 16), 272)

    def hand(i, n):
        plane = (1 - core, core, 1 - core)[n]
        half = (side[i], 1 - side[i], 1 - side[i])[n]
        who = (sibling, (depth, ring[i]), (other, ring[i]))[n]
        return pltpu.make_async_remote_copy(
            src_ref=u.at[plane, :, :, i, window(i, half)], dst_ref=raw.at[i, n],
            send_sem=esend.at[i, n], recv_sem=erecv.at[i, n],
            device_id=who, device_id_type=MESH)

    def hand_plane(q):
        @pl.when(core == q)
        def _():
            for i in range(4):
                hand(i, 1).start()

        @pl.when(core != q)
        def _():
            for n in (2, 0):
                for i in range(4):
                    hand(i, n).start()

    for copy_in in tops:
        copy_in.wait()

    def step(plane, carry):
        z = plane
        new = jnp.where(z < first_plane, 2, z - first_plane)
        old = jnp.where(z <= first_plane, 2, z - 1 - first_plane)

        def wide(ref, kind, p, half, block):
            rows = slice(block * B, (block + 1) * B)
            return jnp.concatenate([ref[kind, p, half * 2, rows, :], ref[kind, p, half * 2 + 1, rows, :]], axis=1)

        def put_wide(ref, kind, p, half, block, value):
            rows = slice(block * B, (block + 1) * B)
            ref[kind, p, half * 2, rows, :] = value[:, :B]
            ref[kind, p, half * 2 + 1, rows, :] = value[:, B:]

        def wide_u(kind, p, half, block):
            rows = slice(block * B, (block + 1) * B)
            return jnp.concatenate([u[old, kind, p, half * 2, rows, :], u[old, kind, p, half * 2 + 1, rows, :]], axis=1)

        def forward_x(n, carry):
            kind, half = n % 2, n // 2
            re = [wide_u(kind, 0, half, q) for q in range(4)]
            im = [wide_u(kind, 1, half, q) for q in range(4)]
            sre, sim = split4(re, im)
            for r in range(4):
                got = jnp.dot(left_ref[r], jnp.concatenate([sre[r], sim[r]], axis=0),
                              preferred_element_type=F32).astype(BF16)
                put_wide(a, kind, 0, half, r, got[:B])
                put_wide(a, kind, 1, half, r, got[B:])
            return carry

        lax.fori_loop(0, 4, forward_x, 0, unroll=2)

        @pl.when(z == first_plane + 1)
        def _():
            hand_plane(0)

        for way in range(2):
            pltpu.make_async_copy(
                win.at[0, half_rows(way)], cbuf.at[z, half_rows(way)], crecv.at[z, way]).wait()

        @pl.when(z != depth)
        def _():
            pltpu.make_async_copy(means.at[0], mbuf.at[z], mrecv.at[z]).wait()

        base = mbuf[z, 0:1, :]
        turn = angular * base
        turn_sq = turn * turn
        turn_re = horner(COS_Q, turn_sq)
        turn_im = turn * horner(SIN_Q, turn_sq)

        def operators(n, carry):
            rows = n * 24
            k = rows + lax.broadcasted_iota(jnp.int32, (24, B), 0)
            kx = (k % B) * 4 + k // B
            kx = jnp.where(kx < N // 2, kx, kx - N).astype(F32) * (2.0 * math.pi / N)
            left_q = turn_sq - kx * kx
            for ry in range(3):
                ky = lax.broadcasted_iota(jnp.int32, (1, B), 1) * 4 + ry
                ky = jnp.where(ky < N // 2, ky, ky - N).astype(F32) * (2.0 * math.pi / N)
                q = left_q - ky * ky
                root = jnp.sqrt(jnp.abs(q))
                wave = jnp.maximum(q, 0.0)
                travels = q >= 0.0
                pre = jnp.where(travels, horner(COS_Q, wave), jnp.exp(-root))
                pim = jnp.where(travels, root * horner(SIN_Q, wave), 0.0)
                put = pl.ds(pl.multiple_of(rows, 8), 24)
                ph[0, ry, put, :] = pre * turn_re + pim * turn_im
                ph[1, ry, put, :] = pim * turn_re - pre * turn_im
            take = pl.ds(pl.multiple_of(n * 32, 32), 32)
            for q in range(4):
                index = cbuf[z, take, q * B:(q + 1) * B].astype(jnp.int32)
                sc[0, q, take, :] = lookup(cos_levels, index)
                sc[1, q, take, :] = lookup(sin_levels, index)
            return carry

        lax.fori_loop(0, 16, operators, 0, unroll=2)

        def along_y(rx, carry):
            prow = pl.ds(pl.multiple_of(jnp.where(rx == 3, 1, rx) * B, B), B)
            rows = pl.ds(pl.multiple_of(rx * B, B), B)
            sums_of = [split4([a[k, 0, q, rows, :] for q in range(4)], [a[k, 1, q, rows, :] for q in range(4)])
                       for k in range(2)]
            tre, tim = ([], []), ([], [])
            for r in range(4):
                data = jnp.concatenate(
                    [jnp.concatenate([sums_of[k][0][r], sums_of[k][1][r]], axis=1) for k in range(2)], axis=0)
                got = jnp.dot(data, right_ref[r], preferred_element_type=F32)
                py = 1 if r == 3 else r
                pre, pim = ph[0, py, prow, :], ph[1, py, prow, :]
                turned = []
                for k in range(2):
                    gre, gim = got[k * B:(k + 1) * B, :B], got[k * B:(k + 1) * B, B:]
                    rr, ii, ri, ir = gre * pre, gim * pim, gre * pim, gim * pre
                    nre, nim = (rr - ii, ri + ir) if k == 0 else (rr + ii, ir - ri)
                    turned.append(jnp.concatenate([nre.astype(BF16), nim.astype(BF16)], axis=1))
                back = jnp.dot(jnp.concatenate(turned, axis=0), left_ref[r], preferred_element_type=F32)
                for k in range(2):
                    tre[k].append(back[k * B:(k + 1) * B, :B])
                    tim[k].append(back[k * B:(k + 1) * B, B:])
            for k in range(2):
                cre, cim = join4(tre[k], tim[k])
                for q in range(4):
                    a[k, 0, q, rows, :] = cre[q].astype(BF16)
                    a[k, 1, q, rows, :] = cim[q].astype(BF16)
            return carry

        lax.fori_loop(0, 4, along_y, 0)

        @pl.when(jnp.logical_and(z == 0, jnp.logical_and(section == 0, core == 1)))
        def _():
            section_codes(lambda c: c.start())

        def inverse_x(n, carry):
            kind, half = n % 2, n // 2
            sign = (1 - 2 * kind).astype(F32)
            tre, tim = [], []
            for r in range(4):
                data = jnp.concatenate([wide(a, kind, 0, half, r), wide(a, kind, 1, half, r)], axis=0)
                got = jnp.dot(right_ref[r], data, preferred_element_type=F32)
                tre.append(got[:B])
                tim.append(got[B:])
            xre, xim = join4(tre, tim)
            for q in range(4):
                rows = slice(q * B, (q + 1) * B)
                for part in range(2):
                    cols = slice(part * B, (part + 1) * B)
                    cre = sc[0, half * 2 + part, rows, :]
                    cim = sc[1, half * 2 + part, rows, :] * sign
                    gre, gim = xre[q][:, cols], xim[q][:, cols]
                    u[new, kind, 0, half * 2 + part, rows, :] = (gre * cre - gim * cim).astype(BF16)
                    u[new, kind, 1, half * 2 + part, rows, :] = (gre * cim + gim * cre).astype(BF16)
            return carry

        lax.fori_loop(0, 4, inverse_x, 0, unroll=2)

        return carry

    lax.fori_loop(0, steps, step, 0)

    for i in range(4):
        for s in range(4):
            for k in range(2):
                for p in range(2):
                    pad[i, s, k, p, 0:8, :] = jnp.zeros((8, B), F32)
                    pad[i, s, k, p, 280:288, :] = jnp.zeros((8, B), F32)
    hand_plane(1)

    for i in range(4):
        for k in range(2):
            for p in range(2):
                pad[i, 0, k, p, 8:280, :] = u[core, k, p, i, window(i, side[i]), :].astype(F32)
    for n in range(3):
        for i in range(4):
            hand(i, n).wait_recv()
            for k in range(2):
                for p in range(2):
                    pad[i, n + 1, k, p, 8:280, :] = raw[i, n, k, p].astype(F32)

    def weight(d, i):
        return (1, 8, 4, 2)[(d - i) % 4]

    flip_x = [[(mine[d] + bits(v, 0)[d]) % 2 for d in range(2)] for v in range(4)]
    slot_x = [[sum(flip_x[v][d] * weight(d, i) for d in range(2)) for i in range(4)] for v in range(4)]
    shift = [side[i] * 16 for i in range(4)]

    def produce(g):
        def body(n, carry):
            theirs = bits(0, n)
            flip_z = [(mine[d] + theirs[d]) % 2 for d in (2, 3)]
            slot_z = [sum(flip_z[d - 2] * weight(d, i) for d in (2, 3)) for i in range(4)]
            for v in range(4):
                for i in range(4):
                    row = pl.multiple_of(n * 64 + v * 16 + shift[i], 16)
                    slot = slot_z[i] + slot_x[v][i]
                    for l in range(PER):
                        h = g * PER + l - LAG
                        total = None
                        for s in range(4):
                            for p in range(2):
                                left = pad[i, s, 0, p, pl.ds(row + (8 - h), 16), :]
                                right = pad[i, s, 1, p, pl.ds(row + (8 + h), 16), :]
                                term = left * right
                                total = term if total is None else total + term
                        buf[g, i, slot, l] = total.astype(BF16)
            return carry
        lax.fori_loop(0, 4, body, 0)

    recv = (None, r1, r2, r3)

    def copy(g, i, t):
        half = 16 >> t
        return pltpu.make_async_remote_copy(
            src_ref=buf.at[g, i, pl.ds(half, half)], dst_ref=recv[t].at[g, i],
            send_sem=ssem.at[g, i, t - 1], recv_sem=rsem.at[g, i, t - 1],
            device_id=(depth, ring[(i + t) % 4]), device_id_type=MESH)

    def last(i, slot, who, place):
        return pltpu.make_async_remote_copy(
            src_ref=buf.at[:, i, slot], dst_ref=(fa, fb)[place].at[i],
            send_sem=fsend.at[i, slot], recv_sem=frecv.at[i, place],
            device_id=who, device_id_type=MESH)

    at_home = [side[i] == yh for i in range(4)]

    def sends_last(i, act):
        @pl.when(at_home[i])
        def _():
            act(last(i, 1, (depth, ring[i]), 0))

        @pl.when(jnp.logical_not(at_home[i]))
        def _():
            act(last(i, 0, (depth, far), 0))
            act(last(i, 1, (depth, far_ring[i]), 1))

    def arrive(g, i, t):
        copy(g, i, t).wait_recv()
        half = 16 >> t

        def body(n, carry):
            for k in (half - 1 - 2 * n, half - 2 - 2 * n):
                buf[g, i, k] = buf[g, i, k] + recv[t][g, i, k]
            return carry
        lax.fori_loop(0, half // 2, body, 0)
        if t < 3:
            copy(g, i, t + 1).start()

    def finish(i):
        last(i, 0, (depth, far), 0).wait_recv()
        cols = slice(i * B, (i + 1) * B)

        @pl.when(at_home[i])
        def _():
            for g in range(GROUPS):
                out[g * PER:(g + 1) * PER, :, cols] = (buf[g, i, 0].astype(F32) + fa[i, g].astype(F32)) * factor

        @pl.when(jnp.logical_not(at_home[i]))
        def _():
            last(i, 1, (depth, far_ring[i]), 1).wait_recv()
            for g in range(GROUPS):
                out[g * PER:(g + 1) * PER, :, cols] = (fa[i, g].astype(F32) + fb[i, g].astype(F32)) * factor

    for g in range(GROUPS):
        produce(g)
        for i in range(4):
            copy(g, i, 1).start()
        if g >= 2:
            for i in range(4):
                arrive(g - 2, i, 1)
    for g in range(GROUPS - 2, GROUPS):
        for i in range(4):
            arrive(g, i, 1)
    for t in (2, 3):
        for g in range(GROUPS):
            for i in range(4):
                arrive(g, i, t)
                if t == 3 and g == GROUPS - 1:
                    sends_last(i, lambda c: c.start())
    for i in range(4):
        finish(i)
    for i in range(4):
        for n in range(3):
            hand(i, n).wait_send()
    for g in range(GROUPS):
        for i in range(4):
            for t in (1, 2, 3):
                copy(g, i, t).wait_send()
    for i in range(4):
        sends_last(i, lambda c: c.wait_send())
    for way in range(2):
        codes_to(2, way, sibling).wait_send()
    mean_to(2, sibling).wait_send()

    @pl.when(section == 0)
    def _():
        section_codes(lambda c: c.wait_send())
        for s in range(2):
            mean_to(s, beside[0][s]).wait_send()


def migrate(src, rec, win, means, table, right, left, factor):
    vmem = pl.BlockSpec(memory_space=pltpu.VMEM)
    hbm = pl.BlockSpec(memory_space=pl.ANY)
    dma = pltpu.SemaphoreType.DMA
    strip = (PER, 16, B)
    return pl.pallas_call(
        functools.partial(migrate_kernel, factor),
        out_shape=jax.ShapeDtypeStruct((LAGS, 16, N), F32),
        in_specs=[hbm, hbm, hbm, vmem, pl.BlockSpec(memory_space=pltpu.SMEM), vmem, vmem],
        out_specs=vmem,
        scratch_shapes=[
            pltpu.VMEM((3, 2, 2, 4, N, B), BF16),
            pltpu.VMEM((2, 2, 4, N, B), BF16),
            pltpu.VMEM((4, N, N), BF16),
            pltpu.VMEM((4, 8, B), F32),
            pltpu.VMEM((2, 3, 3 * B, B), F32),
            pltpu.VMEM((2, 4, N, B), F32),
            pltpu.VMEM((4, 3, 2, 2, 272, B), BF16),
            pltpu.VMEM((4, 4, 2, 2, 288, B), F32),
            pltpu.VMEM((GROUPS, 4, 16) + strip, BF16),
            pltpu.VMEM((GROUPS, 4, 8) + strip, BF16),
            pltpu.VMEM((GROUPS, 4, 4) + strip, BF16),
            pltpu.VMEM((GROUPS, 4, 2) + strip, BF16),
            pltpu.VMEM((4, GROUPS) + strip, BF16),
            pltpu.VMEM((4, GROUPS) + strip, BF16),
            dma((2, 4)), dma((3, 2)), dma((4, 2)), dma((3,)), dma((4,)),
            dma((4, 3)), dma((4, 3)),
            dma((GROUPS, 4, 3)), dma((GROUPS, 4, 3)), dma((4, 2)), dma((4, 2)),
        ],
        compiler_params=pltpu.CompilerParams(
            collective_id=1, has_side_effects=True, vmem_limit_bytes=62 * 1024 * 1024),
        name="migrate",
    )(src, rec, win, means, table, right, left)


def shards(source_top, receiver_top, slowness_codes, slowness_table, anchors):
    right, left = butterfly_matrices()
    right = jnp.asarray(right, BF16)
    left = jnp.asarray(left, BF16)
    windows, means = make_windows(slowness_codes, slowness_table, anchors)
    image = migrate(
        source_top, receiver_top, windows, means, slowness_table, right, left, 1.0 / math.sqrt(128.0))
    return image[None]


def solution(mesh):
    return jax.shard_map(
        shards,
        mesh=mesh,
        in_specs=(
            P(None, "freq", None, None, None),
            P(None, "freq", None, None, None),
            P("depth", None, None),
            P(),
            P(),
        ),
        out_specs=P("depth", None, "freq", None),
        check_vma=False,
    )
```

```python
import functools
import math

import jax
import jax.numpy as jnp
import numpy as np
from jax import lax
from jax.experimental import pallas as pl
from jax.experimental.pallas import tpu as pltpu
from jax.sharding import PartitionSpec as P

LAG = 7
LAGS = 2 * LAG + 1
N = 512
B = 128
GROUPS = 5
PER = LAGS // GROUPS
MESH = pl.DeviceIdType.MESH
F32 = jnp.float32
BF16 = jnp.bfloat16


def butterfly_matrices():
    j = np.arange(B)[:, None]
    k = np.arange(B)[None, :]
    mats = []
    for wave in (4 * k, 4 * k + 1, 4 * k + 2, -(4 * k + 1)):
        angle = 2.0 * np.pi * ((j * wave) % N) / N
        c = np.cos(angle) / math.sqrt(N)
        s = np.sin(angle) / math.sqrt(N)
        mats.append(np.block([[c, -s], [s, c]]))
    right = np.stack(mats)
    return right, np.swapaxes(right, 1, 2)


def even_poly(first, terms, top, samples=400):
    q = (np.cos(np.pi * (np.arange(samples) + 0.5) / samples) + 1.0) * 0.5 * top
    r = np.sqrt(q)
    want = np.cos(r) if first == 0 else np.sin(r) / r
    fit = np.polynomial.Chebyshev.fit(q, want, terms, domain=[0, top])
    return [float(v) for v in fit.convert(kind=np.polynomial.Polynomial).coef]


COS_Q = even_poly(0, 6, 14.0)
SIN_Q = even_poly(1, 5, 14.0)


def horner(coefs, q):
    value = coefs[-1] * q + coefs[-2]
    for c in coefs[-3::-1]:
        value = value * q + c
    return value


def split4(re, im):
    er, ei, dr, di = re[0] + re[2], im[0] + im[2], re[0] - re[2], im[0] - im[2]
    fr, fi, gr, gi = re[1] + re[3], im[1] + im[3], re[1] - re[3], im[1] - im[3]
    return (er + fr, dr + gi, er - fr, dr - gi), (ei + fi, di - gr, ei - fi, di + gr)


def join4(re, im):
    er, ei, dr, di = re[0] + re[2], im[0] + im[2], re[0] - re[2], im[0] - im[2]
    fr, fi, gr, gi = re[1] + re[3], im[1] + im[3], re[1] - re[3], im[1] - im[3]
    return (er + fr, dr - gi, er - fr, dr + gi), (ei + fi, di + gr, ei - fi, di - gr)


def level_row(table):
    lane = lax.broadcasted_iota(jnp.int32, (8, B), 1)
    levels = jnp.zeros((8, B), F32)
    for k in range(32):
        levels = jnp.where(lane == k, table[k], levels)
    return levels


TAKE = lax.GatherDimensionNumbers(
    offset_dims=(), collapsed_slice_dims=(1,), start_index_map=(1,),
    operand_batching_dims=(0,), start_indices_batching_dims=(0,))


def lookup(values, index):
    return lax.gather(
        jnp.tile(values, (index.shape[0] // 8, 1)), index[..., None], TAKE, (1, 1),
        mode=lax.GatherScatterMode.PROMISE_IN_BOUNDS)


def windows_kernel(codes, table, anchors, out, means, raw, sem):
    def fetch(s, h):
        ox = pl.multiple_of(anchors[s, 0], N)
        oy = pl.multiple_of(anchors[s, 1], N)
        return pltpu.make_async_copy(
            codes.at[0, pl.ds(ox + h * 256, 256), pl.ds(oy, N)], raw.at[s, h], sem.at[s, h])

    for s in range(2):
        for h in range(2):
            fetch(s, h).start()
    levels = level_row(table)
    for s in range(2):
        total = jnp.zeros((8, B), F32)
        for h in range(2):
            fetch(s, h).wait()

            def rows_of(n, total):
                take = pl.ds(pl.multiple_of(n * 32, 32), 32)
                for q in range(4):
                    index = raw[s, h, take, q * B:(q + 1) * B]
                    out[s, pl.ds(pl.multiple_of(h * 256 + n * 32, 32), 32), q * B:(q + 1) * B] = (
                        index.astype(F32).astype(BF16))
                    got = lookup(levels, index)
                    total = total + (got[0:8] + got[8:16]) + (got[16:24] + got[24:32])
                return total

            total = lax.fori_loop(0, 8, rows_of, total)
        means[s] = jnp.full((8, B), jnp.sum(total) * (1.0 / (N * N)), F32)


def make_windows(codes, table, anchors):
    vmem = pl.BlockSpec(memory_space=pltpu.VMEM)
    smem = pl.BlockSpec(memory_space=pltpu.SMEM)
    return pl.pallas_call(
        windows_kernel,
        out_shape=(
            jax.ShapeDtypeStruct((2, N, N), BF16),
            jax.ShapeDtypeStruct((2, 8, B), F32),
        ),
        in_specs=[pl.BlockSpec(memory_space=pl.ANY), smem, smem],
        out_specs=(vmem, vmem),
        scratch_shapes=[pltpu.VMEM((2, 2, 256, N), jnp.int32), pltpu.SemaphoreType.DMA((2, 2))],
        compiler_params=pltpu.CompilerParams(vmem_limit_bytes=60 * 1024 * 1024),
        name="windows",
    )(codes, table, anchors)


def migrate_kernel(
    factor, src, rec, win, means, table, right_ref, left_ref, out,
    u, a, cbuf, mbuf, ph, sc, raw, pad, buf, r1, r2, r3, fa, fb,
    tsem, csend, crecv, msend, mrecv, esend, erecv, ssem, rsem, fsend, frecv,
):
    depth = lax.axis_index("depth")
    freq = lax.axis_index("freq")
    core = depth % 2
    section = depth // 2
    other = depth + 1 - 2 * core
    x, z, yh = freq % 4, (freq // 4) % 4, freq // 16
    first_plane = section * 2
    steps = first_plane + 2
    ring = (
        freq - x + (x + 1 - 2 * (x % 2)),
        freq - x + (3 - x),
        freq - 4 * z + 4 * (z + 1 - 2 * (z % 2)),
        freq - 4 * z + 4 * (3 - z),
    )
    far = freq - 16 * yh + 16 * (1 - yh)
    far_ring = [r - 16 * yh + 16 * (1 - yh) for r in ring]
    sibling = (other, freq)
    beside = [[(2 * (1 - section) + s, freq) for s in range(2)], [(2 * (1 - section) + s, far) for s in range(2)]]

    def bits(ix, iz):
        return [((ix + 1) // 2) % 2, ix // 2, ((iz + 1) // 2) % 2, iz // 2]

    mine = bits(x, z)
    side = mine

    tops = []
    for kind, top in enumerate((src, rec)):
        for q in range(4):
            tops.append(pltpu.make_async_copy(
                top.at[core, 0, :, :, pl.ds(q * B, B)], u.at[2, kind, :, q], tsem.at[kind, q]))
    for copy_in in tops:
        copy_in.start()

    def half_rows(way):
        return pl.ds(way * (N // 2), N // 2)

    for way in range(2):
        pltpu.make_async_copy(
            win.at[core, half_rows(way)], cbuf.at[depth, half_rows(way)], crecv.at[depth, way]).start()
    mbuf[depth] = means[core]

    barrier = pltpu.get_barrier_semaphore()
    peers = [sibling, (depth, far)] + beside[0] + beside[1]
    for i in range(4):
        peers += [(depth, ring[i]), (other, ring[i]), (depth, far_ring[i])]
    for who in peers:
        pl.semaphore_signal(barrier, inc=1, device_id=who, device_id_type=MESH)

    position = freq.astype(F32)
    angular = math.pi * (0.45 + 0.5 * (position + 0.5) / 32.0)
    levels = level_row(table)
    pl.semaphore_wait(barrier, len(peers))

    def codes_to(n, way, who):
        shot = (0, 1, 1 - core)[n]
        return pltpu.make_async_remote_copy(
            src_ref=win.at[shot, half_rows(way)], dst_ref=cbuf.at[depth, half_rows(way)],
            send_sem=csend.at[n, way], recv_sem=crecv.at[depth, way],
            device_id=who, device_id_type=MESH)

    def mean_to(n, who):
        shot = (0, 1, 1 - core)[n]
        return pltpu.make_async_remote_copy(
            src_ref=means.at[shot], dst_ref=mbuf.at[depth],
            send_sem=msend.at[n], recv_sem=mrecv.at[depth],
            device_id=who, device_id_type=MESH)

    def section_codes(act):
        for s in range(2):
            for way in range(2):
                act(codes_to(s, way, beside[way][s]))

    mean_to(2, sibling).start()

    @pl.when(section == 0)
    def _():
        for s in range(2):
            mean_to(s, beside[0][s]).start()

    for way in range(2):
        codes_to(2, way, sibling).start()

    @pl.when(jnp.logical_and(section == 0, core == 0))
    def _():
        section_codes(lambda c: c.start())

    def window(i, half):
        return pl.ds(pl.multiple_of(half * 240, 16), 272)

    def hand(i, n):
        plane = (1 - core, core, 1 - core)[n]
        half = (side[i], 1 - side[i], 1 - side[i])[n]
        who = (sibling, (depth, ring[i]), (other, ring[i]))[n]
        return pltpu.make_async_remote_copy(
            src_ref=u.at[plane, :, :, i, window(i, half)], dst_ref=raw.at[i, n],
            send_sem=esend.at[i, n], recv_sem=erecv.at[i, n],
            device_id=who, device_id_type=MESH)

    def hand_plane(q):
        @pl.when(core == q)
        def _():
            for i in range(4):
                hand(i, 1).start()

        @pl.when(core != q)
        def _():
            for n in (2, 0):
                for i in range(4):
                    hand(i, n).start()

    for copy_in in tops:
        copy_in.wait()

    def step(plane, carry):
        z = plane
        new = jnp.where(z < first_plane, 2, z - first_plane)
        old = jnp.where(z <= first_plane, 2, z - 1 - first_plane)

        def wide(ref, kind, p, half, block):
            rows = slice(block * B, (block + 1) * B)
            return jnp.concatenate([ref[kind, p, half * 2, rows, :], ref[kind, p, half * 2 + 1, rows, :]], axis=1)

        def put_wide(ref, kind, p, half, block, value):
            rows = slice(block * B, (block + 1) * B)
            ref[kind, p, half * 2, rows, :] = value[:, :B]
            ref[kind, p, half * 2 + 1, rows, :] = value[:, B:]

        def wide_u(kind, p, half, block):
            rows = slice(block * B, (block + 1) * B)
            return jnp.concatenate([u[old, kind, p, half * 2, rows, :], u[old, kind, p, half * 2 + 1, rows, :]], axis=1)

        def forward_x(n, carry):
            kind, half = n % 2, n // 2
            re = [wide_u(kind, 0, half, q) for q in range(4)]
            im = [wide_u(kind, 1, half, q) for q in range(4)]
            sre, sim = split4(re, im)
            for r in range(4):
                got = jnp.dot(left_ref[r], jnp.concatenate([sre[r], sim[r]], axis=0),
                              preferred_element_type=F32).astype(BF16)
                put_wide(a, kind, 0, half, r, got[:B])
                put_wide(a, kind, 1, half, r, got[B:])
            return carry

        lax.fori_loop(0, 4, forward_x, 0, unroll=4)

        @pl.when(z == first_plane + 1)
        def _():
            hand_plane(0)

        for way in range(2):
            pltpu.make_async_copy(
                win.at[0, half_rows(way)], cbuf.at[z, half_rows(way)], crecv.at[z, way]).wait()

        @pl.when(z != depth)
        def _():
            pltpu.make_async_copy(means.at[0], mbuf.at[z], mrecv.at[z]).wait()

        base = mbuf[z, 0:1, :]
        turn = angular * base
        turn_sq = turn * turn
        angle = angular * (levels - base)
        squared = angle * angle
        cos_levels = horner(COS_Q, squared)
        sin_levels = angle * horner(SIN_Q, squared)

        def operators(n, carry):
            rows = n * 48
            k = rows + lax.broadcasted_iota(jnp.int32, (48, B), 0)
            kx = (k % B) * 4 + k // B
            kx = jnp.where(kx < N // 2, kx, kx - N).astype(F32) * (2.0 * math.pi / N)
            left_q = turn_sq - kx * kx
            for ry in range(3):
                ky = lax.broadcasted_iota(jnp.int32, (1, B), 1) * 4 + ry
                ky = jnp.where(ky < N // 2, ky, ky - N).astype(F32) * (2.0 * math.pi / N)
                q = left_q - ky * ky
                size = jnp.maximum(jnp.abs(q), 1e-30)
                root = size * lax.rsqrt(size)
                travels = q >= 0.0
                put = pl.ds(pl.multiple_of(rows, 16), 48)
                ph[0, ry, put, :] = jnp.where(travels, horner(COS_Q, q), jnp.exp(-root)).astype(BF16)
                ph[1, ry, put, :] = jnp.where(travels, root * horner(SIN_Q, q), 0.0).astype(BF16)
            take = pl.ds(pl.multiple_of(n * 64, 64), 64)
            for q in range(4):
                index = cbuf[z, take, q * B:(q + 1) * B].astype(jnp.int32)
                sc[0, q, take, :] = lookup(cos_levels, index).astype(BF16)
                sc[1, q, take, :] = lookup(sin_levels, index).astype(BF16)
            return carry

        lax.fori_loop(0, 8, operators, 0)

        def along_y(rx, carry):
            prow = pl.ds(pl.multiple_of(jnp.where(rx == 3, 1, rx) * B, B), B)
            rows = pl.ds(pl.multiple_of(rx * B, B), B)
            sums_of = [split4([a[k, 0, q, rows, :] for q in range(4)], [a[k, 1, q, rows, :] for q in range(4)])
                       for k in range(2)]
            tre, tim = ([], []), ([], [])
            for r in range(4):
                data = jnp.concatenate(
                    [jnp.concatenate([sums_of[k][0][r], sums_of[k][1][r]], axis=1) for k in range(2)], axis=0)
                got = jnp.dot(data, right_ref[r], preferred_element_type=F32).astype(BF16)
                py = 1 if r == 3 else r
                pre, pim = ph[0, py, prow, :], ph[1, py, prow, :]
                turned = []
                for k in range(2):
                    gre, gim = got[k * B:(k + 1) * B, :B], got[k * B:(k + 1) * B, B:]
                    rr, ii, ri, ir = gre * pre, gim * pim, gre * pim, gim * pre
                    nre, nim = (rr - ii, ri + ir) if k == 0 else (rr + ii, ir - ri)
                    turned.append(jnp.concatenate([nre, nim], axis=1))
                back = jnp.dot(jnp.concatenate(turned, axis=0), left_ref[r], preferred_element_type=F32).astype(BF16)
                for k in range(2):
                    tre[k].append(back[k * B:(k + 1) * B, :B])
                    tim[k].append(back[k * B:(k + 1) * B, B:])
            for k in range(2):
                cre, cim = join4(tre[k], tim[k])
                for q in range(4):
                    a[k, 0, q, rows, :] = cre[q]
                    a[k, 1, q, rows, :] = cim[q]
            return carry

        lax.fori_loop(0, 4, along_y, 0, unroll=4)

        @pl.when(jnp.logical_and(z == 0, jnp.logical_and(section == 0, core == 1)))
        def _():
            section_codes(lambda c: c.start())

        def inverse_x(n, carry):
            kind, half = n % 2, n // 2
            sign = (1 - 2 * kind).astype(F32).astype(BF16)
            tre, tim = [], []
            for r in range(4):
                data = jnp.concatenate([wide(a, kind, 0, half, r), wide(a, kind, 1, half, r)], axis=0)
                got = jnp.dot(right_ref[r], data, preferred_element_type=F32).astype(BF16)
                tre.append(got[:B])
                tim.append(got[B:])
            xre, xim = join4(tre, tim)
            for q in range(4):
                rows = slice(q * B, (q + 1) * B)
                for part in range(2):
                    cols = slice(part * B, (part + 1) * B)
                    cre = sc[0, half * 2 + part, rows, :]
                    cim = sc[1, half * 2 + part, rows, :] * sign
                    gre, gim = xre[q][:, cols], xim[q][:, cols]
                    u[new, kind, 0, half * 2 + part, rows, :] = gre * cre - gim * cim
                    u[new, kind, 1, half * 2 + part, rows, :] = gre * cim + gim * cre
            return carry

        lax.fori_loop(0, 4, inverse_x, 0, unroll=4)

        return carry

    lax.fori_loop(0, steps, step, 0)

    for i in range(4):
        for s in range(4):
            for k in range(2):
                for p in range(2):
                    pad[i, s, k, p, 0:8, :] = jnp.zeros((8, B), F32)
                    pad[i, s, k, p, 280:288, :] = jnp.zeros((8, B), F32)
    hand_plane(1)

    for i in range(4):
        for k in range(2):
            for p in range(2):
                pad[i, 0, k, p, 8:280, :] = u[core, k, p, i, window(i, side[i]), :].astype(F32)
    for n in range(3):
        for i in range(4):
            hand(i, n).wait_recv()
            for k in range(2):
                for p in range(2):
                    pad[i, n + 1, k, p, 8:280, :] = raw[i, n, k, p].astype(F32)

    def weight(d, i):
        return (1, 8, 4, 2)[(d - i) % 4]

    flip_x = [[(mine[d] + bits(v, 0)[d]) % 2 for d in range(2)] for v in range(4)]
    slot_x = [[sum(flip_x[v][d] * weight(d, i) for d in range(2)) for i in range(4)] for v in range(4)]
    shift = [side[i] * 16 for i in range(4)]

    def produce(g):
        def body(n, carry):
            theirs = bits(0, n)
            flip_z = [(mine[d] + theirs[d]) % 2 for d in (2, 3)]
            slot_z = [sum(flip_z[d - 2] * weight(d, i) for d in (2, 3)) for i in range(4)]
            for v in range(4):
                for i in range(4):
                    row = pl.multiple_of(n * 64 + v * 16 + shift[i], 16)
                    slot = slot_z[i] + slot_x[v][i]
                    for l in range(PER):
                        h = g * PER + l - LAG
                        total = None
                        for s in range(4):
                            for p in range(2):
                                left = pad[i, s, 0, p, pl.ds(row + (8 - h), 16), :]
                                right = pad[i, s, 1, p, pl.ds(row + (8 + h), 16), :]
                                term = left * right
                                total = term if total is None else total + term
                        buf[g, i, slot, l] = total.astype(BF16)
            return carry
        lax.fori_loop(0, 4, body, 0)

    recv = (None, r1, r2, r3)

    def copy(g, i, t):
        half = 16 >> t
        return pltpu.make_async_remote_copy(
            src_ref=buf.at[g, i, pl.ds(half, half)], dst_ref=recv[t].at[g, i],
            send_sem=ssem.at[g, i, t - 1], recv_sem=rsem.at[g, i, t - 1],
            device_id=(depth, ring[(i + t) % 4]), device_id_type=MESH)

    def last(g, i, slot, who, place):
        return pltpu.make_async_remote_copy(
            src_ref=buf.at[g, i, slot], dst_ref=(fa, fb)[place].at[g, i],
            send_sem=fsend.at[g, i, slot], recv_sem=frecv.at[g, i, place],
            device_id=who, device_id_type=MESH)

    at_home = [side[i] == yh for i in range(4)]

    def sends_last(g, i, act):
        @pl.when(at_home[i])
        def _():
            act(last(g, i, 1, (depth, ring[i]), 0))

        @pl.when(jnp.logical_not(at_home[i]))
        def _():
            act(last(g, i, 0, (depth, far), 0))
            act(last(g, i, 1, (depth, far_ring[i]), 1))

    def arrive(g, i, t):
        copy(g, i, t).wait_recv()
        half = 16 >> t

        def body(n, carry):
            for k in (half - 1 - 2 * n, half - 2 - 2 * n):
                buf[g, i, k] = buf[g, i, k] + recv[t][g, i, k]
            return carry
        lax.fori_loop(0, half // 2, body, 0)
        if t < 3:
            copy(g, i, t + 1).start()
        else:
            sends_last(g, i, lambda c: c.start())

    def finish(g, i):
        last(g, i, 0, (depth, far), 0).wait_recv()
        put = (slice(g * PER, (g + 1) * PER), slice(None), slice(i * B, (i + 1) * B))

        @pl.when(at_home[i])
        def _():
            out[put] = (buf[g, i, 0].astype(F32) + fa[g, i].astype(F32)) * factor

        @pl.when(jnp.logical_not(at_home[i]))
        def _():
            last(g, i, 1, (depth, far_ring[i]), 1).wait_recv()
            out[put] = (fa[g, i].astype(F32) + fb[g, i].astype(F32)) * factor

    for g in range(GROUPS):
        produce(g)
        for i in range(4):
            copy(g, i, 1).start()
        for t in (3, 2, 1):
            if g - 1 - t >= 0:
                for i in range(4):
                    arrive(g - 1 - t, i, t)
    left = [(g, t) for t in (1, 2, 3) for g in range(GROUPS) if g + t > GROUPS - 2]
    for g, t in sorted(left, key=lambda gt: (gt[0] + gt[1], gt[1])):
        for i in range(4):
            arrive(g, i, t)
    for g in range(GROUPS):
        for i in range(4):
            finish(g, i)
    for i in range(4):
        for n in range(3):
            hand(i, n).wait_send()
    for g in range(GROUPS):
        for i in range(4):
            for t in (1, 2, 3):
                copy(g, i, t).wait_send()
            sends_last(g, i, lambda c: c.wait_send())
    for way in range(2):
        codes_to(2, way, sibling).wait_send()
    mean_to(2, sibling).wait_send()

    @pl.when(section == 0)
    def _():
        section_codes(lambda c: c.wait_send())
        for s in range(2):
            mean_to(s, beside[0][s]).wait_send()


def migrate(src, rec, win, means, table, right, left, factor):
    vmem = pl.BlockSpec(memory_space=pltpu.VMEM)
    hbm = pl.BlockSpec(memory_space=pl.ANY)
    dma = pltpu.SemaphoreType.DMA
    strip = (PER, 16, B)
    return pl.pallas_call(
        functools.partial(migrate_kernel, factor),
        out_shape=jax.ShapeDtypeStruct((LAGS, 16, N), F32),
        in_specs=[hbm, hbm, hbm, vmem, pl.BlockSpec(memory_space=pltpu.SMEM), vmem, vmem],
        out_specs=vmem,
        scratch_shapes=[
            pltpu.VMEM((3, 2, 2, 4, N, B), BF16),
            pltpu.VMEM((2, 2, 4, N, B), BF16),
            pltpu.VMEM((4, N, N), BF16),
            pltpu.VMEM((4, 8, B), F32),
            pltpu.VMEM((2, 3, 3 * B, B), BF16),
            pltpu.VMEM((2, 4, N, B), BF16),
            pltpu.VMEM((4, 3, 2, 2, 272, B), BF16),
            pltpu.VMEM((4, 4, 2, 2, 288, B), F32),
            pltpu.VMEM((GROUPS, 4, 16) + strip, BF16),
            pltpu.VMEM((GROUPS, 4, 8) + strip, BF16),
            pltpu.VMEM((GROUPS, 4, 4) + strip, BF16),
            pltpu.VMEM((GROUPS, 4, 2) + strip, BF16),
            pltpu.VMEM((GROUPS, 4) + strip, BF16),
            pltpu.VMEM((GROUPS, 4) + strip, BF16),
            dma((2, 4)), dma((3, 2)), dma((4, 2)), dma((3,)), dma((4,)),
            dma((4, 3)), dma((4, 3)),
            dma((GROUPS, 4, 3)), dma((GROUPS, 4, 3)), dma((GROUPS, 4, 2)), dma((GROUPS, 4, 2)),
        ],
        compiler_params=pltpu.CompilerParams(
            collective_id=1, has_side_effects=True, vmem_limit_bytes=62 * 1024 * 1024),
        name="migrate",
    )(src, rec, win, means, table, right, left)


def shards(source_top, receiver_top, slowness_codes, slowness_table, anchors):
    right, left = butterfly_matrices()
    right = jnp.asarray(right, BF16)
    left = jnp.asarray(left, BF16)
    windows, means = make_windows(slowness_codes, slowness_table, anchors)
    image = migrate(
        source_top, receiver_top, windows, means, slowness_table, right, left, 1.0 / math.sqrt(128.0))
    return image[None]


def solution(mesh):
    return jax.shard_map(
        shards,
        mesh=mesh,
        in_specs=(
            P(None, "freq", None, None, None),
            P(None, "freq", None, None, None),
            P("depth", None, None),
            P(),
            P(),
        ),
        out_specs=P("depth", None, "freq", None),
        check_vma=False,
    )
```

```python
import functools
import math

import jax
import jax.numpy as jnp
import numpy as np
from jax import lax
from jax.experimental import pallas as pl
from jax.experimental.pallas import tpu as pltpu
from jax.sharding import PartitionSpec as P

LAG = 7
LAGS = 2 * LAG + 1
N = 512
B = 128
GROUPS = 5
PER = LAGS // GROUPS
MESH = pl.DeviceIdType.MESH
F32 = jnp.float32
BF16 = jnp.bfloat16


def butterfly_matrices():
    j = np.arange(B)[:, None]
    k = np.arange(B)[None, :]
    mats = []
    for wave in (4 * k, 4 * k + 1, 4 * k + 2, -(4 * k + 1)):
        angle = 2.0 * np.pi * ((j * wave) % N) / N
        c = np.cos(angle) / math.sqrt(N)
        s = np.sin(angle) / math.sqrt(N)
        mats.append(np.block([[c, -s], [s, c]]))
    right = np.stack(mats)
    return right, np.swapaxes(right, 1, 2)


def even_poly(first, terms, top, samples=400):
    q = (np.cos(np.pi * (np.arange(samples) + 0.5) / samples) + 1.0) * 0.5 * top
    r = np.sqrt(q)
    want = np.cos(r) if first == 0 else np.sin(r) / r
    fit = np.polynomial.Chebyshev.fit(q, want, terms, domain=[0, top])
    return [float(v) for v in fit.convert(kind=np.polynomial.Polynomial).coef]


COS_Q = even_poly(0, 6, 14.0)
SIN_Q = even_poly(1, 5, 14.0)


def horner(coefs, q):
    value = coefs[-1] * q + coefs[-2]
    for c in coefs[-3::-1]:
        value = value * q + c
    return value


def split4(re, im):
    er, ei, dr, di = re[0] + re[2], im[0] + im[2], re[0] - re[2], im[0] - im[2]
    fr, fi, gr, gi = re[1] + re[3], im[1] + im[3], re[1] - re[3], im[1] - im[3]
    return (er + fr, dr + gi, er - fr, dr - gi), (ei + fi, di - gr, ei - fi, di + gr)


def join4(re, im):
    er, ei, dr, di = re[0] + re[2], im[0] + im[2], re[0] - re[2], im[0] - im[2]
    fr, fi, gr, gi = re[1] + re[3], im[1] + im[3], re[1] - re[3], im[1] - im[3]
    return (er + fr, dr - gi, er - fr, dr + gi), (ei + fi, di + gr, ei - fi, di - gr)


def level_row(table):
    lane = lax.broadcasted_iota(jnp.int32, (8, B), 1)
    levels = jnp.zeros((8, B), F32)
    for k in range(32):
        levels = jnp.where(lane == k, table[k], levels)
    return levels


TAKE = lax.GatherDimensionNumbers(
    offset_dims=(), collapsed_slice_dims=(1,), start_index_map=(1,),
    operand_batching_dims=(0,), start_indices_batching_dims=(0,))


def lookup(values, index):
    return lax.gather(
        jnp.tile(values, (index.shape[0] // 8, 1)), index[..., None], TAKE, (1, 1),
        mode=lax.GatherScatterMode.PROMISE_IN_BOUNDS)


def migrate_kernel(
    factor, src, rec, model, table, anchors, right_ref, left_ref, out,
    rawc, win, means, wsem, u, a, cbuf, mbuf, ph, sc, raw, pad, buf, r1, r2, r3, fa, fb,
    tsem, csend, crecv, msend, mrecv, esend, erecv, ssem, rsem, fsend, frecv,
):
    depth = lax.axis_index("depth")
    freq = lax.axis_index("freq")
    core = depth % 2
    section = depth // 2
    other = depth + 1 - 2 * core
    x, z, yh = freq % 4, (freq // 4) % 4, freq // 16
    first_plane = section * 2
    steps = first_plane + 2
    ring = (
        freq - x + (x + 1 - 2 * (x % 2)),
        freq - x + (3 - x),
        freq - 4 * z + 4 * (z + 1 - 2 * (z % 2)),
        freq - 4 * z + 4 * (3 - z),
    )
    far = freq - 16 * yh + 16 * (1 - yh)
    far_ring = [r - 16 * yh + 16 * (1 - yh) for r in ring]
    sibling = (other, freq)
    beside = [[(2 * (1 - section) + s, freq) for s in range(2)], [(2 * (1 - section) + s, far) for s in range(2)]]

    def bits(ix, iz):
        return [((ix + 1) // 2) % 2, ix // 2, ((iz + 1) // 2) % 2, iz // 2]

    mine = bits(x, z)
    side = mine

    loads = []
    for qx in range(2):
        for qy in range(2):
            loads.append(pltpu.make_async_copy(
                model.at[0, pl.ds(qx * N, N), pl.ds(qy * N, N)], rawc.at[qx, qy], wsem.at[qx, qy]))
    for copy_in in loads:
        copy_in.start()
    tops = []
    for kind, top in enumerate((src, rec)):
        for q in range(4):
            tops.append(pltpu.make_async_copy(
                top.at[core, 0, :, :, pl.ds(q * B, B)], u.at[2, kind, :, q], tsem.at[kind, q]))
    for copy_in in tops:
        copy_in.start()

    def half_rows(way):
        return pl.ds(way * (N // 2), N // 2)

    barrier = pltpu.get_barrier_semaphore()
    peers = [sibling, (depth, far)] + beside[0] + beside[1]
    for i in range(4):
        peers += [(depth, ring[i]), (other, ring[i]), (depth, far_ring[i])]
    for who in peers:
        pl.semaphore_signal(barrier, inc=1, device_id=who, device_id_type=MESH)

    position = freq.astype(F32)
    angular = math.pi * (0.45 + 0.5 * (position + 0.5) / 32.0)
    levels = level_row(table)

    for copy_in in loads:
        copy_in.wait()
    for s in range(2):
        qx = anchors[s, 0] // N
        qy = anchors[s, 1] // N

        def rows_of(n, total):
            take = pl.ds(pl.multiple_of(n * 32, 32), 32)
            for q in range(4):
                index = rawc[qx, qy, take, q * B:(q + 1) * B]
                win[s, take, q * B:(q + 1) * B] = index.astype(F32).astype(BF16)
                got = lookup(levels, index)
                total = total + (got[0:8] + got[8:16]) + (got[16:24] + got[24:32])
            return total

        total = lax.fori_loop(0, N // 32, rows_of, jnp.zeros((8, B), F32))
        means[s] = jnp.full((8, B), jnp.sum(total) * (1.0 / (N * N)), F32)

    pl.semaphore_wait(barrier, len(peers))

    def codes_to(n, way, who):
        shot = (0, 1, 1 - core)[n]
        return pltpu.make_async_remote_copy(
            src_ref=win.at[shot, half_rows(way)], dst_ref=cbuf.at[depth, half_rows(way)],
            send_sem=csend.at[n, way], recv_sem=crecv.at[depth, way],
            device_id=who, device_id_type=MESH)

    def mean_to(n, who):
        shot = (0, 1, 1 - core)[n]
        return pltpu.make_async_remote_copy(
            src_ref=means.at[shot], dst_ref=mbuf.at[depth],
            send_sem=msend.at[n], recv_sem=mrecv.at[depth],
            device_id=who, device_id_type=MESH)

    def section_codes(act):
        for s in range(2):
            for way in range(2):
                act(codes_to(s, way, beside[way][s]))

    for way in range(2):
        pltpu.make_async_copy(
            win.at[core, half_rows(way)], cbuf.at[depth, half_rows(way)], crecv.at[depth, way]).start()
    mbuf[depth] = means[core]

    mean_to(2, sibling).start()

    @pl.when(section == 0)
    def _():
        for s in range(2):
            mean_to(s, beside[0][s]).start()

    for way in range(2):
        codes_to(2, way, sibling).start()

    @pl.when(jnp.logical_and(section == 0, core == 0))
    def _():
        section_codes(lambda c: c.start())

    def window(i, half):
        return pl.ds(pl.multiple_of(half * 240, 16), 272)

    def hand(i, n):
        plane = (1 - core, core, 1 - core)[n]
        half = (side[i], 1 - side[i], 1 - side[i])[n]
        who = (sibling, (depth, ring[i]), (other, ring[i]))[n]
        return pltpu.make_async_remote_copy(
            src_ref=u.at[plane, :, :, i, window(i, half)], dst_ref=raw.at[i, n],
            send_sem=esend.at[i, n], recv_sem=erecv.at[i, n],
            device_id=who, device_id_type=MESH)

    def hand_plane(q):
        @pl.when(core == q)
        def _():
            for i in range(4):
                hand(i, 1).start()

        @pl.when(core != q)
        def _():
            for n in (2, 0):
                for i in range(4):
                    hand(i, n).start()

    for copy_in in tops:
        copy_in.wait()

    def step(plane, carry):
        z = plane
        new = jnp.where(z < first_plane, 2, z - first_plane)
        old = jnp.where(z <= first_plane, 2, z - 1 - first_plane)

        @pl.when(z != depth)
        def _():
            pltpu.make_async_copy(means.at[0], mbuf.at[z], mrecv.at[z]).wait()

        base = mbuf[z, 0:1, :]
        turn = angular * base
        turn_sq = turn * turn
        angle = angular * (levels - base)
        squared = angle * angle
        cos_levels = horner(COS_Q, squared)
        sin_levels = angle * horner(SIN_Q, squared)

        def operators(n):
            rows = n * 96
            k = rows + lax.broadcasted_iota(jnp.int32, (96, B), 0)
            kx = (k % B) * 4 + k // B
            kx = jnp.where(kx < N // 2, kx, kx - N).astype(F32) * (2.0 * math.pi / N)
            left_q = turn_sq - kx * kx
            for ry in range(3):
                ky = lax.broadcasted_iota(jnp.int32, (1, B), 1) * 4 + ry
                ky = jnp.where(ky < N // 2, ky, ky - N).astype(F32) * (2.0 * math.pi / N)
                q = left_q - ky * ky
                size = jnp.maximum(jnp.abs(q), 1e-30)
                root = size * lax.rsqrt(size)
                travels = q >= 0.0
                put = slice(rows, rows + 96)
                ph[0, ry, put, :] = jnp.where(travels, horner(COS_Q, q), jnp.exp(-root)).astype(BF16)
                ph[1, ry, put, :] = jnp.where(travels, root * horner(SIN_Q, q), 0.0).astype(BF16)

        def wide(ref, kind, p, half, block):
            rows = slice(block * B, (block + 1) * B)
            return jnp.concatenate([ref[kind, p, half * 2, rows, :], ref[kind, p, half * 2 + 1, rows, :]], axis=1)

        def put_wide(ref, kind, p, half, block, value):
            rows = slice(block * B, (block + 1) * B)
            ref[kind, p, half * 2, rows, :] = value[:, :B]
            ref[kind, p, half * 2 + 1, rows, :] = value[:, B:]

        def wide_u(kind, p, half, block):
            rows = slice(block * B, (block + 1) * B)
            return jnp.concatenate([u[old, kind, p, half * 2, rows, :], u[old, kind, p, half * 2 + 1, rows, :]], axis=1)

        def forward_x(n, carry):
            kind, half = n % 2, n // 2
            re = [wide_u(kind, 0, half, q) for q in range(4)]
            im = [wide_u(kind, 1, half, q) for q in range(4)]
            sre, sim = split4(re, im)
            for r in range(4):
                got = jnp.dot(left_ref[r], jnp.concatenate([sre[r], sim[r]], axis=0),
                              preferred_element_type=F32).astype(BF16)
                put_wide(a, kind, 0, half, r, got[:B])
                put_wide(a, kind, 1, half, r, got[B:])
            return carry

        for n in range(4):
            forward_x(n, 0)
            operators(n)

        @pl.when(z == first_plane + 1)
        def _():
            hand_plane(0)

        def along_y(rx, carry):
            prow = pl.ds(pl.multiple_of(jnp.where(rx == 3, 1, rx) * B, B), B)
            rows = pl.ds(pl.multiple_of(rx * B, B), B)
            sums_of = [split4([a[k, 0, q, rows, :] for q in range(4)], [a[k, 1, q, rows, :] for q in range(4)])
                       for k in range(2)]
            tre, tim = ([], []), ([], [])
            for r in range(4):
                data = jnp.concatenate(
                    [jnp.concatenate([sums_of[k][0][r], sums_of[k][1][r]], axis=1) for k in range(2)], axis=0)
                got = jnp.dot(data, right_ref[r], preferred_element_type=F32).astype(BF16)
                py = 1 if r == 3 else r
                pre, pim = ph[0, py, prow, :], ph[1, py, prow, :]
                turned = []
                for k in range(2):
                    gre, gim = got[k * B:(k + 1) * B, :B], got[k * B:(k + 1) * B, B:]
                    rr, ii, ri, ir = gre * pre, gim * pim, gre * pim, gim * pre
                    nre, nim = (rr - ii, ri + ir) if k == 0 else (rr + ii, ir - ri)
                    turned.append(jnp.concatenate([nre, nim], axis=1))
                back = jnp.dot(jnp.concatenate(turned, axis=0), left_ref[r], preferred_element_type=F32).astype(BF16)
                for k in range(2):
                    tre[k].append(back[k * B:(k + 1) * B, :B])
                    tim[k].append(back[k * B:(k + 1) * B, B:])
            for k in range(2):
                cre, cim = join4(tre[k], tim[k])
                for q in range(4):
                    a[k, 0, q, rows, :] = cre[q]
                    a[k, 1, q, rows, :] = cim[q]
            return carry

        lax.fori_loop(0, 4, along_y, 0, unroll=4)

        for way in range(2):
            pltpu.make_async_copy(
                win.at[0, half_rows(way)], cbuf.at[z, half_rows(way)], crecv.at[z, way]).wait()

        @pl.when(jnp.logical_and(z == 0, jnp.logical_and(section == 0, core == 1)))
        def _():
            section_codes(lambda c: c.start())

        for half in range(2):
            for q in range(4):
                rows = slice(q * B, (q + 1) * B)
                for part in range(2):
                    block = half * 2 + part
                    index = cbuf[z, rows, block * B:(block + 1) * B].astype(jnp.int32)
                    sc[0, block, rows, :] = lookup(cos_levels, index).astype(BF16)
                    sc[1, block, rows, :] = lookup(sin_levels, index).astype(BF16)
            for kind in range(2):
                tre, tim = [], []
                for r in range(4):
                    data = jnp.concatenate([wide(a, kind, 0, half, r), wide(a, kind, 1, half, r)], axis=0)
                    got = jnp.dot(right_ref[r], data, preferred_element_type=F32).astype(BF16)
                    tre.append(got[:B])
                    tim.append(got[B:])
                xre, xim = join4(tre, tim)
                for q in range(4):
                    rows = slice(q * B, (q + 1) * B)
                    for part in range(2):
                        block = half * 2 + part
                        cols = slice(part * B, (part + 1) * B)
                        cre, cim = sc[0, block, rows, :], sc[1, block, rows, :]
                        gre, gim = xre[q][:, cols], xim[q][:, cols]
                        rr, ii, ri, ir = gre * cre, gim * cim, gre * cim, gim * cre
                        nre, nim = (rr - ii, ri + ir) if kind == 0 else (rr + ii, ir - ri)
                        u[new, kind, 0, block, rows, :] = nre
                        u[new, kind, 1, block, rows, :] = nim
        return carry

    lax.fori_loop(0, steps, step, 0)

    for i in range(4):
        for s in range(4):
            for k in range(2):
                for p in range(2):
                    pad[i, s, k, p, 0:8, :] = jnp.zeros((8, B), F32)
                    pad[i, s, k, p, 280:288, :] = jnp.zeros((8, B), F32)
    hand_plane(1)

    for i in range(4):
        for k in range(2):
            for p in range(2):
                pad[i, 0, k, p, 8:280, :] = u[core, k, p, i, window(i, side[i]), :].astype(F32)
    for n in range(3):
        for i in range(4):
            hand(i, n).wait_recv()
            for k in range(2):
                for p in range(2):
                    pad[i, n + 1, k, p, 8:280, :] = raw[i, n, k, p].astype(F32)

    def weight(d, i):
        return (1, 8, 4, 2)[(d - i) % 4]

    flip_x = [[(mine[d] + bits(v, 0)[d]) % 2 for d in range(2)] for v in range(4)]
    slot_x = [[sum(flip_x[v][d] * weight(d, i) for d in range(2)) for i in range(4)] for v in range(4)]
    shift = [side[i] * 16 for i in range(4)]

    def produce(g):
        def body(n, carry):
            theirs = bits(0, n)
            flip_z = [(mine[d] + theirs[d]) % 2 for d in (2, 3)]
            slot_z = [sum(flip_z[d - 2] * weight(d, i) for d in (2, 3)) for i in range(4)]
            for v in range(4):
                for i in range(4):
                    row = pl.multiple_of(n * 64 + v * 16 + shift[i], 16)
                    slot = slot_z[i] + slot_x[v][i]
                    for l in range(PER):
                        h = g * PER + l - LAG
                        total = None
                        for s in range(4):
                            for p in range(2):
                                left = pad[i, s, 0, p, pl.ds(row + (8 - h), 16), :]
                                right = pad[i, s, 1, p, pl.ds(row + (8 + h), 16), :]
                                term = left * right
                                total = term if total is None else total + term
                        buf[g, i, slot, l] = total.astype(BF16)
            return carry
        lax.fori_loop(0, 4, body, 0)

    recv = (None, r1, r2, r3)

    def copy(g, i, t):
        half = 16 >> t
        return pltpu.make_async_remote_copy(
            src_ref=buf.at[g, i, pl.ds(half, half)], dst_ref=recv[t].at[g, i],
            send_sem=ssem.at[g, i, t - 1], recv_sem=rsem.at[g, i, t - 1],
            device_id=(depth, ring[(i + t) % 4]), device_id_type=MESH)

    def last(g, i, slot, who, place):
        return pltpu.make_async_remote_copy(
            src_ref=buf.at[g, i, slot], dst_ref=(fa, fb)[place].at[g, i],
            send_sem=fsend.at[g, i, slot], recv_sem=frecv.at[g, i, place],
            device_id=who, device_id_type=MESH)

    at_home = [side[i] == yh for i in range(4)]

    def sends_last(g, i, act):
        @pl.when(at_home[i])
        def _():
            act(last(g, i, 1, (depth, ring[i]), 0))

        @pl.when(jnp.logical_not(at_home[i]))
        def _():
            act(last(g, i, 0, (depth, far), 0))
            act(last(g, i, 1, (depth, far_ring[i]), 1))

    def arrive(g, i, t):
        copy(g, i, t).wait_recv()
        half = 16 >> t

        def body(n, carry):
            for k in (half - 1 - 2 * n, half - 2 - 2 * n):
                buf[g, i, k] = buf[g, i, k] + recv[t][g, i, k]
            return carry
        lax.fori_loop(0, half // 2, body, 0)
        if t < 3:
            copy(g, i, t + 1).start()
        else:
            sends_last(g, i, lambda c: c.start())

    def finish(g, i):
        last(g, i, 0, (depth, far), 0).wait_recv()
        put = (slice(g * PER, (g + 1) * PER), slice(None), slice(i * B, (i + 1) * B))

        @pl.when(at_home[i])
        def _():
            out[put] = (buf[g, i, 0].astype(F32) + fa[g, i].astype(F32)) * factor

        @pl.when(jnp.logical_not(at_home[i]))
        def _():
            last(g, i, 1, (depth, far_ring[i]), 1).wait_recv()
            out[put] = (fa[g, i].astype(F32) + fb[g, i].astype(F32)) * factor

    for g in range(GROUPS):
        produce(g)
        for i in range(4):
            copy(g, i, 1).start()
        for t in (3, 2, 1):
            if g - 1 - t >= 0:
                for i in range(4):
                    arrive(g - 1 - t, i, t)
    left = [(g, t) for t in (1, 2, 3) for g in range(GROUPS) if g + t > GROUPS - 2]
    for g, t in sorted(left, key=lambda gt: (gt[0] + gt[1], gt[1])):
        for i in range(4):
            arrive(g, i, t)
    for g in range(GROUPS):
        for i in range(4):
            finish(g, i)
    for i in range(4):
        for n in range(3):
            hand(i, n).wait_send()
    for g in range(GROUPS):
        for i in range(4):
            for t in (1, 2, 3):
                copy(g, i, t).wait_send()
            sends_last(g, i, lambda c: c.wait_send())
    for way in range(2):
        codes_to(2, way, sibling).wait_send()
    mean_to(2, sibling).wait_send()

    @pl.when(section == 0)
    def _():
        section_codes(lambda c: c.wait_send())
        for s in range(2):
            mean_to(s, beside[0][s]).wait_send()


def migrate(src, rec, model, table, anchors, right, left, factor):
    vmem = pl.BlockSpec(memory_space=pltpu.VMEM)
    hbm = pl.BlockSpec(memory_space=pl.ANY)
    smem = pl.BlockSpec(memory_space=pltpu.SMEM)
    dma = pltpu.SemaphoreType.DMA
    strip = (PER, 16, B)
    return pl.pallas_call(
        functools.partial(migrate_kernel, factor),
        out_shape=jax.ShapeDtypeStruct((LAGS, 16, N), F32),
        in_specs=[hbm, hbm, hbm, smem, smem, vmem, vmem],
        out_specs=vmem,
        scratch_shapes=[
            pltpu.VMEM((2, 2, N, N), jnp.int32),
            pltpu.VMEM((2, N, N), BF16),
            pltpu.VMEM((2, 8, B), F32),
            dma((2, 2)),
            pltpu.VMEM((3, 2, 2, 4, N, B), BF16),
            pltpu.VMEM((2, 2, 4, N, B), BF16),
            pltpu.VMEM((4, N, N), BF16),
            pltpu.VMEM((4, 8, B), F32),
            pltpu.VMEM((2, 3, 3 * B, B), BF16),
            pltpu.VMEM((2, 4, N, B), BF16),
            pltpu.VMEM((4, 3, 2, 2, 272, B), BF16),
            pltpu.VMEM((4, 4, 2, 2, 288, B), F32),
            pltpu.VMEM((GROUPS, 4, 16) + strip, BF16),
            pltpu.VMEM((GROUPS, 4, 8) + strip, BF16),
            pltpu.VMEM((GROUPS, 4, 4) + strip, BF16),
            pltpu.VMEM((GROUPS, 4, 2) + strip, BF16),
            pltpu.VMEM((GROUPS, 4) + strip, BF16),
            pltpu.VMEM((GROUPS, 4) + strip, BF16),
            dma((2, 4)), dma((3, 2)), dma((4, 2)), dma((3,)), dma((4,)),
            dma((4, 3)), dma((4, 3)),
            dma((GROUPS, 4, 3)), dma((GROUPS, 4, 3)), dma((GROUPS, 4, 2)), dma((GROUPS, 4, 2)),
        ],
        compiler_params=pltpu.CompilerParams(
            collective_id=1, has_side_effects=True, vmem_limit_bytes=62 * 1024 * 1024),
        name="migrate",
    )(src, rec, model, table, anchors, right, left)


def shards(source_top, receiver_top, slowness_codes, slowness_table, anchors):
    right, left = butterfly_matrices()
    right = jnp.asarray(right, BF16)
    left = jnp.asarray(left, BF16)
    image = migrate(
        source_top, receiver_top, slowness_codes, slowness_table, anchors, right, left, 1.0 / math.sqrt(128.0))
    return image[None]


def solution(mesh):
    return jax.shard_map(
        shards,
        mesh=mesh,
        in_specs=(
            P(None, "freq", None, None, None),
            P(None, "freq", None, None, None),
            P("depth", None, None),
            P(),
            P(),
        ),
        out_specs=P("depth", None, "freq", None),
        check_vma=False,
    )
```

```python
import functools
import math

import jax
import jax.numpy as jnp
import numpy as np
from jax import lax
from jax.experimental import pallas as pl
from jax.experimental.pallas import tpu as pltpu
from jax.sharding import PartitionSpec as P

LAG = 7
LAGS = 2 * LAG + 1
N = 512
B = 128
GROUPS = 5
PER = LAGS // GROUPS
MESH = pl.DeviceIdType.MESH
F32 = jnp.float32
BF16 = jnp.bfloat16


def butterfly_matrices():
    j = np.arange(B)[:, None]
    k = np.arange(B)[None, :]
    mats = []
    for wave in (4 * k, 4 * k + 1, 4 * k + 2, -(4 * k + 1)):
        angle = 2.0 * np.pi * ((j * wave) % N) / N
        c = np.cos(angle) / math.sqrt(N)
        s = np.sin(angle) / math.sqrt(N)
        mats.append(np.block([[c, -s], [s, c]]))
    right = np.stack(mats)
    return right, np.swapaxes(right, 1, 2)


def even_poly(first, terms, top, samples=400):
    q = (np.cos(np.pi * (np.arange(samples) + 0.5) / samples) + 1.0) * 0.5 * top
    r = np.sqrt(q)
    want = np.cos(r) if first == 0 else np.sin(r) / r
    fit = np.polynomial.Chebyshev.fit(q, want, terms, domain=[0, top])
    return [float(v) for v in fit.convert(kind=np.polynomial.Polynomial).coef]


COS_Q = even_poly(0, 6, 14.0)
SIN_Q = even_poly(1, 5, 14.0)


def horner(coefs, q):
    value = coefs[-1] * q + coefs[-2]
    for c in coefs[-3::-1]:
        value = value * q + c
    return value


def split4(re, im):
    er, ei, dr, di = re[0] + re[2], im[0] + im[2], re[0] - re[2], im[0] - im[2]
    fr, fi, gr, gi = re[1] + re[3], im[1] + im[3], re[1] - re[3], im[1] - im[3]
    return (er + fr, dr + gi, er - fr, dr - gi), (ei + fi, di - gr, ei - fi, di + gr)


def join4(re, im):
    er, ei, dr, di = re[0] + re[2], im[0] + im[2], re[0] - re[2], im[0] - im[2]
    fr, fi, gr, gi = re[1] + re[3], im[1] + im[3], re[1] - re[3], im[1] - im[3]
    return (er + fr, dr - gi, er - fr, dr + gi), (ei + fi, di + gr, ei - fi, di - gr)


def level_row(table):
    lane = lax.broadcasted_iota(jnp.int32, (8, B), 1)
    levels = jnp.zeros((8, B), F32)
    for k in range(32):
        levels = jnp.where(lane == k, table[k], levels)
    return levels


TAKE = lax.GatherDimensionNumbers(
    offset_dims=(), collapsed_slice_dims=(1,), start_index_map=(1,),
    operand_batching_dims=(0,), start_indices_batching_dims=(0,))


def lookup(values, index):
    return lax.gather(
        jnp.tile(values, (index.shape[0] // 8, 1)), index[..., None], TAKE, (1, 1),
        mode=lax.GatherScatterMode.PROMISE_IN_BOUNDS)


def migrate_kernel(
    factor, src, rec, model, table, anchors, right_ref, left_ref, out,
    rawc, win, means, wsem, u, a, cbuf, mbuf, ph, sc, raw, pad, buf, r1, r2, r3, fa, fb,
    tsem, csend, crecv, msend, mrecv, esend, erecv, ssem, rsem, fsend, frecv,
):
    depth = lax.axis_index("depth")
    freq = lax.axis_index("freq")
    core = depth % 2
    section = depth // 2
    other = depth + 1 - 2 * core
    x, z, yh = freq % 4, (freq // 4) % 4, freq // 16
    first_plane = section * 2
    steps = first_plane + 2
    ring = (
        freq - x + (x + 1 - 2 * (x % 2)),
        freq - x + (3 - x),
        freq - 4 * z + 4 * (z + 1 - 2 * (z % 2)),
        freq - 4 * z + 4 * (3 - z),
    )
    far = freq - 16 * yh + 16 * (1 - yh)
    far_ring = [r - 16 * yh + 16 * (1 - yh) for r in ring]
    sibling = (other, freq)
    beside = [[(2 * (1 - section) + s, freq) for s in range(2)], [(2 * (1 - section) + s, far) for s in range(2)]]

    def bits(ix, iz):
        return [((ix + 1) // 2) % 2, ix // 2, ((iz + 1) // 2) % 2, iz // 2]

    mine = bits(x, z)
    at_home = [mine[i] == yh for i in range(4)]
    first = x + core * (z - x)
    second = z + core * (x - z)
    near = [ring[d] + core * (ring[(d + 2) % 4] - ring[d]) for d in range(4)]
    far_near = [r - 16 * yh + 16 * (1 - yh) for r in near]
    own = bits(first, second)
    first_stride = 16 + 48 * core
    second_stride = 64 - 48 * core

    loads = []
    for qx in range(2):
        for qy in range(2):
            loads.append(pltpu.make_async_copy(
                model.at[0, pl.ds(qx * N, N), pl.ds(qy * N, N)], rawc.at[qx, qy], wsem.at[qx, qy]))
    for copy_in in loads:
        copy_in.start()
    tops = []
    for kind, top in enumerate((src, rec)):
        for q in range(4):
            tops.append(pltpu.make_async_copy(
                top.at[core, 0, :, :, pl.ds(q * B, B)], u.at[2, kind, :, q], tsem.at[kind, q]))
    for copy_in in tops:
        copy_in.start()

    def half_rows(way):
        return pl.ds(way * (N // 2), N // 2)

    barrier = pltpu.get_barrier_semaphore()
    peers = [sibling, (depth, far), (other, far)] + beside[0] + beside[1]
    for i in range(4):
        peers += [(depth, ring[i]), (other, ring[i]), (depth, far_ring[i]), (other, far_ring[i])]
    for who in peers:
        pl.semaphore_signal(barrier, inc=1, device_id=who, device_id_type=MESH)

    position = freq.astype(F32)
    angular = math.pi * (0.45 + 0.5 * (position + 0.5) / 32.0)
    levels = level_row(table)

    for copy_in in loads:
        copy_in.wait()
    for s in range(2):
        qx = anchors[s, 0] // N
        qy = anchors[s, 1] // N

        def rows_of(n, total):
            take = pl.ds(pl.multiple_of(n * 32, 32), 32)
            for q in range(4):
                index = rawc[qx, qy, take, q * B:(q + 1) * B]
                win[s, take, q * B:(q + 1) * B] = index.astype(F32).astype(BF16)
                got = lookup(levels, index)
                total = total + (got[0:8] + got[8:16]) + (got[16:24] + got[24:32])
            return total

        total = lax.fori_loop(0, N // 32, rows_of, jnp.zeros((8, B), F32))
        means[s] = jnp.full((8, B), jnp.sum(total) * (1.0 / (N * N)), F32)

    pl.semaphore_wait(barrier, len(peers))

    def codes_to(n, way, who):
        shot = (0, 1, 1 - core)[n]
        return pltpu.make_async_remote_copy(
            src_ref=win.at[shot, half_rows(way)], dst_ref=cbuf.at[depth, half_rows(way)],
            send_sem=csend.at[n, way], recv_sem=crecv.at[depth, way],
            device_id=who, device_id_type=MESH)

    def mean_to(n, who):
        shot = (0, 1, 1 - core)[n]
        return pltpu.make_async_remote_copy(
            src_ref=means.at[shot], dst_ref=mbuf.at[depth],
            send_sem=msend.at[n], recv_sem=mrecv.at[depth],
            device_id=who, device_id_type=MESH)

    def section_codes(act):
        for s in range(2):
            for way in range(2):
                act(codes_to(s, way, beside[way][s]))

    for way in range(2):
        pltpu.make_async_copy(
            win.at[core, half_rows(way)], cbuf.at[depth, half_rows(way)], crecv.at[depth, way]).start()
    mbuf[depth] = means[core]

    mean_to(2, sibling).start()

    @pl.when(section == 0)
    def _():
        for s in range(2):
            mean_to(s, beside[0][s]).start()

    for way in range(2):
        codes_to(2, way, sibling).start()

    @pl.when(jnp.logical_and(section == 0, core == 0))
    def _():
        section_codes(lambda c: c.start())

    def window(i, half):
        return pl.ds(pl.multiple_of(half * 240, 16), 272)

    def hand(q, j, n):
        part = (2 * (1 - core) + j, 2 * core + j, 2 * (1 - core) + j)[n]
        half = (own[2 + j], 1 - own[j], 1 - own[2 + j])[n]
        who = (sibling, (depth, near[j]), (other, near[2 + j]))[n]
        return pltpu.make_async_remote_copy(
            src_ref=u.at[q, :, :, part, window(part, half)], dst_ref=raw.at[q, j, n],
            send_sem=esend.at[q, j, n], recv_sem=erecv.at[q, j, n],
            device_id=who, device_id_type=MESH)

    def hand_plane(q):
        for n in (2, 1, 0):
            for j in range(2):
                hand(q, j, n).start()

    for copy_in in tops:
        copy_in.wait()

    def step(plane, carry):
        z = plane
        new = jnp.where(z < first_plane, 2, z - first_plane)
        old = jnp.where(z <= first_plane, 2, z - 1 - first_plane)

        @pl.when(z != depth)
        def _():
            pltpu.make_async_copy(means.at[0], mbuf.at[z], mrecv.at[z]).wait()

        base = mbuf[z, 0:1, :]
        turn = angular * base
        turn_sq = turn * turn
        angle = angular * (levels - base)
        squared = angle * angle
        cos_levels = horner(COS_Q, squared)
        sin_levels = angle * horner(SIN_Q, squared)

        def operators(n):
            rows = n * 96
            k = rows + lax.broadcasted_iota(jnp.int32, (96, B), 0)
            kx = (k % B) * 4 + k // B
            kx = jnp.where(kx < N // 2, kx, kx - N).astype(F32) * (2.0 * math.pi / N)
            left_q = turn_sq - kx * kx
            for ry in range(3):
                ky = lax.broadcasted_iota(jnp.int32, (1, B), 1) * 4 + ry
                ky = jnp.where(ky < N // 2, ky, ky - N).astype(F32) * (2.0 * math.pi / N)
                q = left_q - ky * ky
                size = jnp.maximum(jnp.abs(q), 1e-30)
                root = size * lax.rsqrt(size)
                travels = q >= 0.0
                put = slice(rows, rows + 96)
                ph[0, ry, put, :] = jnp.where(travels, horner(COS_Q, q), jnp.exp(-root)).astype(BF16)
                ph[1, ry, put, :] = jnp.where(travels, root * horner(SIN_Q, q), 0.0).astype(BF16)

        def wide(ref, kind, p, half, block):
            rows = slice(block * B, (block + 1) * B)
            return jnp.concatenate([ref[kind, p, half * 2, rows, :], ref[kind, p, half * 2 + 1, rows, :]], axis=1)

        def put_wide(ref, kind, p, half, block, value):
            rows = slice(block * B, (block + 1) * B)
            ref[kind, p, half * 2, rows, :] = value[:, :B]
            ref[kind, p, half * 2 + 1, rows, :] = value[:, B:]

        def wide_u(kind, p, half, block):
            rows = slice(block * B, (block + 1) * B)
            return jnp.concatenate([u[old, kind, p, half * 2, rows, :], u[old, kind, p, half * 2 + 1, rows, :]], axis=1)

        def forward_x(n, carry):
            kind, half = n % 2, n // 2
            re = [wide_u(kind, 0, half, q) for q in range(4)]
            im = [wide_u(kind, 1, half, q) for q in range(4)]
            sre, sim = split4(re, im)
            for r in range(4):
                got = jnp.dot(left_ref[r], jnp.concatenate([sre[r], sim[r]], axis=0),
                              preferred_element_type=F32).astype(BF16)
                put_wide(a, kind, 0, half, r, got[:B])
                put_wide(a, kind, 1, half, r, got[B:])
            return carry

        for n in range(4):
            forward_x(n, 0)
            operators(n)

        @pl.when(z == first_plane + 1)
        def _():
            hand_plane(0)

        def along_y(rx, carry):
            prow = pl.ds(pl.multiple_of(jnp.where(rx == 3, 1, rx) * B, B), B)
            rows = pl.ds(pl.multiple_of(rx * B, B), B)
            sums_of = [split4([a[k, 0, q, rows, :] for q in range(4)], [a[k, 1, q, rows, :] for q in range(4)])
                       for k in range(2)]
            tre, tim = ([], []), ([], [])
            for r in range(4):
                data = jnp.concatenate(
                    [jnp.concatenate([sums_of[k][0][r], sums_of[k][1][r]], axis=1) for k in range(2)], axis=0)
                got = jnp.dot(data, right_ref[r], preferred_element_type=F32).astype(BF16)
                py = 1 if r == 3 else r
                pre, pim = ph[0, py, prow, :], ph[1, py, prow, :]
                turned = []
                for k in range(2):
                    gre, gim = got[k * B:(k + 1) * B, :B], got[k * B:(k + 1) * B, B:]
                    rr, ii, ri, ir = gre * pre, gim * pim, gre * pim, gim * pre
                    nre, nim = (rr - ii, ri + ir) if k == 0 else (rr + ii, ir - ri)
                    turned.append(jnp.concatenate([nre, nim], axis=1))
                back = jnp.dot(jnp.concatenate(turned, axis=0), left_ref[r], preferred_element_type=F32).astype(BF16)
                for k in range(2):
                    tre[k].append(back[k * B:(k + 1) * B, :B])
                    tim[k].append(back[k * B:(k + 1) * B, B:])
            for k in range(2):
                cre, cim = join4(tre[k], tim[k])
                for q in range(4):
                    a[k, 0, q, rows, :] = cre[q]
                    a[k, 1, q, rows, :] = cim[q]
            return carry

        lax.fori_loop(0, 4, along_y, 0, unroll=4)

        for way in range(2):
            pltpu.make_async_copy(
                win.at[0, half_rows(way)], cbuf.at[z, half_rows(way)], crecv.at[z, way]).wait()

        @pl.when(jnp.logical_and(z == 0, jnp.logical_and(section == 0, core == 1)))
        def _():
            section_codes(lambda c: c.start())

        for half in range(2):
            for q in range(4):
                rows = slice(q * B, (q + 1) * B)
                for part in range(2):
                    block = half * 2 + part
                    index = cbuf[z, rows, block * B:(block + 1) * B].astype(jnp.int32)
                    sc[0, block, rows, :] = lookup(cos_levels, index).astype(BF16)
                    sc[1, block, rows, :] = lookup(sin_levels, index).astype(BF16)
            for kind in range(2):
                tre, tim = [], []
                for r in range(4):
                    data = jnp.concatenate([wide(a, kind, 0, half, r), wide(a, kind, 1, half, r)], axis=0)
                    got = jnp.dot(right_ref[r], data, preferred_element_type=F32).astype(BF16)
                    tre.append(got[:B])
                    tim.append(got[B:])
                xre, xim = join4(tre, tim)
                for q in range(4):
                    rows = slice(q * B, (q + 1) * B)
                    for part in range(2):
                        block = half * 2 + part
                        cols = slice(part * B, (part + 1) * B)
                        cre, cim = sc[0, block, rows, :], sc[1, block, rows, :]
                        gre, gim = xre[q][:, cols], xim[q][:, cols]
                        rr, ii, ri, ir = gre * cre, gim * cim, gre * cim, gim * cre
                        nre, nim = (rr - ii, ri + ir) if kind == 0 else (rr + ii, ir - ri)
                        u[new, kind, 0, block, rows, :] = nre
                        u[new, kind, 1, block, rows, :] = nim
        return carry

    lax.fori_loop(0, steps, step, 0)

    for q in range(2):
        for j in range(2):
            for s in range(4):
                for k in range(2):
                    for p in range(2):
                        pad[q, j, s, k, p, 0:8, :] = jnp.zeros((8, B), F32)
                        pad[q, j, s, k, p, 280:288, :] = jnp.zeros((8, B), F32)
    hand_plane(1)

    def gather_plane(q):
        for j in range(2):
            for k in range(2):
                for p in range(2):
                    pad[q, j, 0, k, p, 8:280, :] = u[q, k, p, 2 * core + j, window(j, own[j]), :].astype(F32)
        for n in range(3):
            for j in range(2):
                hand(q, j, n).wait_recv()
                for k in range(2):
                    for p in range(2):
                        pad[q, j, n + 1, k, p, 8:280, :] = raw[q, j, n, k, p].astype(F32)

    def weight(d, j):
        return (1, 8, 4, 2)[(d - j) % 4]

    flip_1 = [[(own[d] + bits(v, 0)[d]) % 2 for d in range(2)] for v in range(4)]
    slot_1 = [[sum(flip_1[v][d] * weight(d, j) for d in range(2)) for j in range(2)] for v in range(4)]

    def produce(q, g):
        def body(n, carry):
            theirs = bits(0, n)
            flip_2 = [(own[d] + theirs[d]) % 2 for d in (2, 3)]
            slot_2 = [sum(flip_2[d - 2] * weight(d, j) for d in (2, 3)) for j in range(2)]
            for v in range(4):
                for j in range(2):
                    row = pl.multiple_of(n * second_stride + v * first_stride + own[j] * 16, 16)
                    slot = slot_2[j] + slot_1[v][j]
                    for l in range(PER):
                        h = g * PER + l - LAG
                        total = None
                        for s in range(4):
                            for p in range(2):
                                left = pad[q, j, s, 0, p, pl.ds(row + (8 - h), 16), :]
                                right = pad[q, j, s, 1, p, pl.ds(row + (8 + h), 16), :]
                                term = left * right
                                total = term if total is None else total + term
                        buf[q, g, j, slot, l] = total.astype(BF16)
            return carry
        lax.fori_loop(0, 4, body, 0)

    recv = (None, r1, r2, r3)

    def copy(q, g, j, t):
        half = 16 >> t
        return pltpu.make_async_remote_copy(
            src_ref=buf.at[q, g, j, pl.ds(half, half)], dst_ref=recv[t].at[q, g, j],
            send_sem=ssem.at[q, g, j, t - 1], recv_sem=rsem.at[q, g, j, t - 1],
            device_id=(depth, near[(j + t) % 4]), device_id_type=MESH)

    def last(q, g, j, slot, who, place):
        part = 2 * core + j
        return pltpu.make_async_remote_copy(
            src_ref=buf.at[q, g, j, slot], dst_ref=(fa, fb)[place].at[g, part],
            send_sem=fsend.at[q, g, j, slot], recv_sem=frecv.at[g, part, place],
            device_id=who, device_id_type=MESH)

    def sends_last(q, g, j, act):
        owner = first_plane + q

        @pl.when(own[j] == yh)
        def _():
            act(last(q, g, j, 1, (owner, near[j]), 0))

        @pl.when(jnp.logical_and(own[j] == yh, core != q))
        def _():
            act(last(q, g, j, 0, sibling, 1))

        @pl.when(own[j] != yh)
        def _():
            act(last(q, g, j, 0, (owner, far), 0))
            act(last(q, g, j, 1, (owner, far_near[j]), 1))

    def arrive(q, g, j, t):
        copy(q, g, j, t).wait_recv()
        half = 16 >> t

        def body(n, carry):
            for k in (half - 1 - 2 * n, half - 2 - 2 * n):
                buf[q, g, j, k] = buf[q, g, j, k] + recv[t][q, g, j, k]
            return carry
        lax.fori_loop(0, half // 2, body, 0)
        if t < 3:
            copy(q, g, j, t + 1).start()
        else:
            sends_last(q, g, j, lambda c: c.start())

    def came(g, i, place):
        pltpu.make_async_remote_copy(
            src_ref=buf.at[0, g, 0, 0], dst_ref=(fa, fb)[place].at[g, i],
            send_sem=fsend.at[0, g, 0, 0], recv_sem=frecv.at[g, i, place],
            device_id=sibling, device_id_type=MESH).wait_recv()

    def finish(g, i):
        came(g, i, 0)
        put = (slice(g * PER, (g + 1) * PER), slice(None), slice(i * B, (i + 1) * B))
        kept = jnp.logical_and(at_home[i], core == i // 2)

        @pl.when(kept)
        def _():
            out[put] = (buf[core, g, i % 2, 0].astype(F32) + fa[g, i].astype(F32)) * factor

        @pl.when(jnp.logical_not(kept))
        def _():
            came(g, i, 1)
            out[put] = (fa[g, i].astype(F32) + fb[g, i].astype(F32)) * factor

    events = [(q, g) for q in range(2) for g in range(GROUPS)]
    for e, (q, g) in enumerate(events):
        if g == 0:
            gather_plane(q)
        produce(q, g)
        for j in range(2):
            copy(q, g, j, 1).start()
        for t in (3, 2, 1):
            if e - 1 - t >= 0:
                for j in range(2):
                    arrive(*events[e - 1 - t], j, t)
    still = [(e, t) for t in (1, 2, 3) for e in range(len(events)) if e + t > len(events) - 2]
    for e, t in sorted(still, key=lambda et: (et[0] + et[1], et[1])):
        for j in range(2):
            arrive(*events[e], j, t)
    for g in range(GROUPS):
        for i in range(4):
            finish(g, i)
    for q in range(2):
        for j in range(2):
            for n in range(3):
                hand(q, j, n).wait_send()
            for g in range(GROUPS):
                for t in (1, 2, 3):
                    copy(q, g, j, t).wait_send()
                sends_last(q, g, j, lambda c: c.wait_send())
    for way in range(2):
        codes_to(2, way, sibling).wait_send()
    mean_to(2, sibling).wait_send()

    @pl.when(section == 0)
    def _():
        section_codes(lambda c: c.wait_send())
        for s in range(2):
            mean_to(s, beside[0][s]).wait_send()


def migrate(src, rec, model, table, anchors, right, left, factor):
    vmem = pl.BlockSpec(memory_space=pltpu.VMEM)
    hbm = pl.BlockSpec(memory_space=pl.ANY)
    smem = pl.BlockSpec(memory_space=pltpu.SMEM)
    dma = pltpu.SemaphoreType.DMA
    strip = (PER, 16, B)
    return pl.pallas_call(
        functools.partial(migrate_kernel, factor),
        out_shape=jax.ShapeDtypeStruct((LAGS, 16, N), F32),
        in_specs=[hbm, hbm, hbm, smem, smem, vmem, vmem],
        out_specs=vmem,
        scratch_shapes=[
            pltpu.VMEM((2, 2, N, N), jnp.int32),
            pltpu.VMEM((2, N, N), BF16),
            pltpu.VMEM((2, 8, B), F32),
            dma((2, 2)),
            pltpu.VMEM((3, 2, 2, 4, N, B), BF16),
            pltpu.VMEM((2, 2, 4, N, B), BF16),
            pltpu.VMEM((4, N, N), BF16),
            pltpu.VMEM((4, 8, B), F32),
            pltpu.VMEM((2, 3, 3 * B, B), BF16),
            pltpu.VMEM((2, 4, N, B), BF16),
            pltpu.VMEM((2, 2, 3, 2, 2, 272, B), BF16),
            pltpu.VMEM((2, 2, 4, 2, 2, 288, B), F32),
            pltpu.VMEM((2, GROUPS, 2, 16) + strip, BF16),
            pltpu.VMEM((2, GROUPS, 2, 8) + strip, BF16),
            pltpu.VMEM((2, GROUPS, 2, 4) + strip, BF16),
            pltpu.VMEM((2, GROUPS, 2, 2) + strip, BF16),
            pltpu.VMEM((GROUPS, 4) + strip, BF16),
            pltpu.VMEM((GROUPS, 4) + strip, BF16),
            dma((2, 4)), dma((3, 2)), dma((4, 2)), dma((3,)), dma((4,)),
            dma((2, 2, 3)), dma((2, 2, 3)),
            dma((2, GROUPS, 2, 3)), dma((2, GROUPS, 2, 3)), dma((2, GROUPS, 2, 2)), dma((GROUPS, 4, 2)),
        ],
        compiler_params=pltpu.CompilerParams(
            collective_id=1, has_side_effects=True, vmem_limit_bytes=62 * 1024 * 1024),
        name="migrate",
    )(src, rec, model, table, anchors, right, left)


def shards(source_top, receiver_top, slowness_codes, slowness_table, anchors):
    right, left = butterfly_matrices()
    right = jnp.asarray(right, BF16)
    left = jnp.asarray(left, BF16)
    image = migrate(
        source_top, receiver_top, slowness_codes, slowness_table, anchors, right, left, 1.0 / math.sqrt(128.0))
    return image[None]


def solution(mesh):
    return jax.shard_map(
        shards,
        mesh=mesh,
        in_specs=(
            P(None, "freq", None, None, None),
            P(None, "freq", None, None, None),
            P("depth", None, None),
            P(),
            P(),
        ),
        out_specs=P("depth", None, "freq", None),
        check_vma=False,
    )
```

```python
import functools
import math

import jax
import jax.numpy as jnp
import numpy as np
from jax import lax
from jax.experimental import pallas as pl
from jax.experimental.pallas import tpu as pltpu
from jax.sharding import PartitionSpec as P

LAG = 7
LAGS = 2 * LAG + 1
N = 512
B = 128
GROUPS = 3
PER = LAGS // GROUPS
MESH = pl.DeviceIdType.MESH
F32 = jnp.float32
BF16 = jnp.bfloat16


def butterfly_matrices():
    j = np.arange(B)[:, None]
    k = np.arange(B)[None, :]
    mats = []
    for wave in (4 * k, 4 * k + 1, 4 * k + 2, -(4 * k + 1)):
        angle = 2.0 * np.pi * ((j * wave) % N) / N
        c = np.cos(angle) / math.sqrt(N)
        s = np.sin(angle) / math.sqrt(N)
        mats.append(np.block([[c, -s], [s, c]]))
    right = np.stack(mats)
    return right, np.swapaxes(right, 1, 2)


def even_poly(first, terms, top, samples=400):
    q = (np.cos(np.pi * (np.arange(samples) + 0.5) / samples) + 1.0) * 0.5 * top
    r = np.sqrt(q)
    want = np.cos(r) if first == 0 else np.sin(r) / r
    fit = np.polynomial.Chebyshev.fit(q, want, terms, domain=[0, top])
    return [float(v) for v in fit.convert(kind=np.polynomial.Polynomial).coef]


COS_Q = even_poly(0, 6, 14.0)
SIN_Q = even_poly(1, 5, 14.0)


def horner(coefs, q):
    value = coefs[-1] * q + coefs[-2]
    for c in coefs[-3::-1]:
        value = value * q + c
    return value


def split4(re, im):
    er, ei, dr, di = re[0] + re[2], im[0] + im[2], re[0] - re[2], im[0] - im[2]
    fr, fi, gr, gi = re[1] + re[3], im[1] + im[3], re[1] - re[3], im[1] - im[3]
    return (er + fr, dr + gi, er - fr, dr - gi), (ei + fi, di - gr, ei - fi, di + gr)


def join4(re, im):
    er, ei, dr, di = re[0] + re[2], im[0] + im[2], re[0] - re[2], im[0] - im[2]
    fr, fi, gr, gi = re[1] + re[3], im[1] + im[3], re[1] - re[3], im[1] - im[3]
    return (er + fr, dr - gi, er - fr, dr + gi), (ei + fi, di + gr, ei - fi, di - gr)


def level_row(table):
    lane = lax.broadcasted_iota(jnp.int32, (8, B), 1)
    levels = jnp.zeros((8, B), F32)
    for k in range(32):
        levels = jnp.where(lane == k, table[k], levels)
    return levels


TAKE = lax.GatherDimensionNumbers(
    offset_dims=(), collapsed_slice_dims=(1,), start_index_map=(1,),
    operand_batching_dims=(0,), start_indices_batching_dims=(0,))


def lookup(values, index):
    return lax.gather(
        jnp.tile(values, (index.shape[0] // 8, 1)), index[..., None], TAKE, (1, 1),
        mode=lax.GatherScatterMode.PROMISE_IN_BOUNDS)


def migrate_kernel(
    factor, src, rec, model, table, anchors, right_ref, left_ref, out,
    rawc, win, means, wsem, u, a, cbuf, mbuf, ph, sc, raw, pad, buf, r1, r2, r3, fa, fb,
    tsem, csend, crecv, msend, mrecv, esend, erecv, ssem, rsem, fsend, frecv,
):
    depth = lax.axis_index("depth")
    freq = lax.axis_index("freq")
    core = depth % 2
    section = depth // 2
    other = depth + 1 - 2 * core
    x, z, yh = freq % 4, (freq // 4) % 4, freq // 16
    first_plane = section * 2
    steps = first_plane + 2
    ring = (
        freq - x + (x + 1 - 2 * (x % 2)),
        freq - x + (3 - x),
        freq - 4 * z + 4 * (z + 1 - 2 * (z % 2)),
        freq - 4 * z + 4 * (3 - z),
    )
    far = freq - 16 * yh + 16 * (1 - yh)
    far_ring = [r - 16 * yh + 16 * (1 - yh) for r in ring]
    sibling = (other, freq)
    beside = [[(2 * (1 - section) + s, freq) for s in range(2)], [(2 * (1 - section) + s, far) for s in range(2)]]

    def bits(ix, iz):
        return [((ix + 1) // 2) % 2, ix // 2, ((iz + 1) // 2) % 2, iz // 2]

    mine = bits(x, z)
    at_home = [mine[i] == yh for i in range(4)]
    first = x + core * (z - x)
    second = z + core * (x - z)
    near = [ring[d] + core * (ring[(d + 2) % 4] - ring[d]) for d in range(4)]
    far_near = [r - 16 * yh + 16 * (1 - yh) for r in near]
    own = bits(first, second)
    first_stride = 16 + 48 * core
    second_stride = 64 - 48 * core

    loads = []
    for qx in range(2):
        for qy in range(2):
            loads.append(pltpu.make_async_copy(
                model.at[0, pl.ds(qx * N, N), pl.ds(qy * N, N)], rawc.at[qx, qy], wsem.at[qx, qy]))
    for copy_in in loads:
        copy_in.start()
    tops = []
    for kind, top in enumerate((src, rec)):
        for q in range(4):
            tops.append(pltpu.make_async_copy(
                top.at[core, 0, :, :, pl.ds(q * B, B)], u.at[2, kind, :, q], tsem.at[kind, q]))
    for copy_in in tops:
        copy_in.start()

    def half_rows(way):
        return pl.ds(way * (N // 2), N // 2)

    barrier = pltpu.get_barrier_semaphore()
    peers = [sibling, (depth, far), (other, far)] + beside[0] + beside[1]
    for i in range(4):
        peers += [(depth, ring[i]), (other, ring[i]), (depth, far_ring[i]), (other, far_ring[i])]
    for who in peers:
        pl.semaphore_signal(barrier, inc=1, device_id=who, device_id_type=MESH)

    position = freq.astype(F32)
    angular = math.pi * (0.45 + 0.5 * (position + 0.5) / 32.0)
    levels = level_row(table)

    for copy_in in loads:
        copy_in.wait()
    for s in range(2):
        qx = anchors[s, 0] // N
        qy = anchors[s, 1] // N

        def rows_of(n, total):
            take = pl.ds(pl.multiple_of(n * 32, 32), 32)
            for q in range(4):
                index = rawc[qx, qy, take, q * B:(q + 1) * B]
                win[s, take, q * B:(q + 1) * B] = index.astype(F32).astype(BF16)
                got = lookup(levels, index)
                total = total + (got[0:8] + got[8:16]) + (got[16:24] + got[24:32])
            return total

        total = lax.fori_loop(0, N // 32, rows_of, jnp.zeros((8, B), F32))
        means[s] = jnp.full((8, B), jnp.sum(total) * (1.0 / (N * N)), F32)

    pl.semaphore_wait(barrier, len(peers))

    def codes_to(n, way, who):
        shot = (0, 1, 1 - core)[n]
        return pltpu.make_async_remote_copy(
            src_ref=win.at[shot, half_rows(way)], dst_ref=cbuf.at[depth, half_rows(way)],
            send_sem=csend.at[n, way], recv_sem=crecv.at[depth, way],
            device_id=who, device_id_type=MESH)

    def mean_to(n, who):
        shot = (0, 1, 1 - core)[n]
        return pltpu.make_async_remote_copy(
            src_ref=means.at[shot], dst_ref=mbuf.at[depth],
            send_sem=msend.at[n], recv_sem=mrecv.at[depth],
            device_id=who, device_id_type=MESH)

    def section_codes(act):
        for s in range(2):
            for way in range(2):
                act(codes_to(s, way, beside[way][s]))

    for way in range(2):
        pltpu.make_async_copy(
            win.at[core, half_rows(way)], cbuf.at[depth, half_rows(way)], crecv.at[depth, way]).start()
    mbuf[depth] = means[core]

    mean_to(2, sibling).start()

    @pl.when(section == 0)
    def _():
        for s in range(2):
            mean_to(s, beside[0][s]).start()

    for way in range(2):
        codes_to(2, way, sibling).start()

    @pl.when(jnp.logical_and(section == 0, core == 0))
    def _():
        section_codes(lambda c: c.start())

    def window(i, half):
        return pl.ds(pl.multiple_of(half * 240, 16), 272)

    def hand(q, j, n):
        part = (2 * (1 - core) + j, 2 * core + j, 2 * (1 - core) + j)[n]
        half = (own[2 + j], 1 - own[j], 1 - own[2 + j])[n]
        who = (sibling, (depth, near[j]), (other, near[2 + j]))[n]
        return pltpu.make_async_remote_copy(
            src_ref=u.at[q, :, :, part, window(part, half)], dst_ref=raw.at[q, j, n],
            send_sem=esend.at[q, j, n], recv_sem=erecv.at[q, j, n],
            device_id=who, device_id_type=MESH)

    def hand_plane(q):
        for n in (2, 1, 0):
            for j in range(2):
                hand(q, j, n).start()

    for copy_in in tops:
        copy_in.wait()

    def step(plane, carry):
        z = plane
        new = jnp.where(z < first_plane, 2, z - first_plane)
        old = jnp.where(z <= first_plane, 2, z - 1 - first_plane)

        @pl.when(z != depth)
        def _():
            pltpu.make_async_copy(means.at[0], mbuf.at[z], mrecv.at[z]).wait()

        base = mbuf[z, 0:1, :]
        turn = angular * base
        turn_sq = turn * turn
        angle = angular * (levels - base)
        squared = angle * angle
        cos_levels = horner(COS_Q, squared)
        sin_levels = angle * horner(SIN_Q, squared)

        def operators(n):
            rows = n * 96
            k = rows + lax.broadcasted_iota(jnp.int32, (96, B), 0)
            kx = (k % B) * 4 + k // B
            kx = jnp.where(kx < N // 2, kx, kx - N).astype(F32) * (2.0 * math.pi / N)
            left_q = turn_sq - kx * kx
            for ry in range(3):
                ky = lax.broadcasted_iota(jnp.int32, (1, B), 1) * 4 + ry
                ky = jnp.where(ky < N // 2, ky, ky - N).astype(F32) * (2.0 * math.pi / N)
                q = left_q - ky * ky
                size = jnp.maximum(jnp.abs(q), 1e-30)
                root = size * lax.rsqrt(size)
                travels = q >= 0.0
                put = slice(rows, rows + 96)
                ph[0, ry, put, :] = jnp.where(travels, horner(COS_Q, q), jnp.exp(-root)).astype(BF16)
                ph[1, ry, put, :] = jnp.where(travels, root * horner(SIN_Q, q), 0.0).astype(BF16)

        def wide(ref, kind, p, half, block):
            rows = slice(block * B, (block + 1) * B)
            return jnp.concatenate([ref[kind, p, half * 2, rows, :], ref[kind, p, half * 2 + 1, rows, :]], axis=1)

        def put_wide(ref, kind, p, half, block, value):
            rows = slice(block * B, (block + 1) * B)
            ref[kind, p, half * 2, rows, :] = value[:, :B]
            ref[kind, p, half * 2 + 1, rows, :] = value[:, B:]

        def wide_u(kind, p, half, block):
            rows = slice(block * B, (block + 1) * B)
            return jnp.concatenate([u[old, kind, p, half * 2, rows, :], u[old, kind, p, half * 2 + 1, rows, :]], axis=1)

        def forward_x(n, carry):
            kind, half = n % 2, n // 2
            re = [wide_u(kind, 0, half, q) for q in range(4)]
            im = [wide_u(kind, 1, half, q) for q in range(4)]
            sre, sim = split4(re, im)
            for r in range(4):
                got = jnp.dot(left_ref[r], jnp.concatenate([sre[r], sim[r]], axis=0),
                              preferred_element_type=F32).astype(BF16)
                put_wide(a, kind, 0, half, r, got[:B])
                put_wide(a, kind, 1, half, r, got[B:])
            return carry

        for n in range(4):
            forward_x(n, 0)
            operators(n)

        @pl.when(z == first_plane + 1)
        def _():
            hand_plane(0)

        def along_y(rx, carry):
            prow = pl.ds(pl.multiple_of(jnp.where(rx == 3, 1, rx) * B, B), B)
            rows = pl.ds(pl.multiple_of(rx * B, B), B)
            sums_of = [split4([a[k, 0, q, rows, :] for q in range(4)], [a[k, 1, q, rows, :] for q in range(4)])
                       for k in range(2)]
            tre, tim = ([], []), ([], [])
            for r in range(4):
                data = jnp.concatenate(
                    [jnp.concatenate([sums_of[k][0][r], sums_of[k][1][r]], axis=1) for k in range(2)], axis=0)
                got = jnp.dot(data, right_ref[r], preferred_element_type=F32).astype(BF16)
                py = 1 if r == 3 else r
                pre, pim = ph[0, py, prow, :], ph[1, py, prow, :]
                turned = []
                for k in range(2):
                    gre, gim = got[k * B:(k + 1) * B, :B], got[k * B:(k + 1) * B, B:]
                    rr, ii, ri, ir = gre * pre, gim * pim, gre * pim, gim * pre
                    nre, nim = (rr - ii, ri + ir) if k == 0 else (rr + ii, ir - ri)
                    turned.append(jnp.concatenate([nre, nim], axis=1))
                back = jnp.dot(jnp.concatenate(turned, axis=0), left_ref[r], preferred_element_type=F32).astype(BF16)
                for k in range(2):
                    tre[k].append(back[k * B:(k + 1) * B, :B])
                    tim[k].append(back[k * B:(k + 1) * B, B:])
            for k in range(2):
                cre, cim = join4(tre[k], tim[k])
                for q in range(4):
                    a[k, 0, q, rows, :] = cre[q]
                    a[k, 1, q, rows, :] = cim[q]
            return carry

        lax.fori_loop(0, 4, along_y, 0, unroll=4)

        for way in range(2):
            pltpu.make_async_copy(
                win.at[0, half_rows(way)], cbuf.at[z, half_rows(way)], crecv.at[z, way]).wait()

        @pl.when(jnp.logical_and(z == 0, jnp.logical_and(section == 0, core == 1)))
        def _():
            section_codes(lambda c: c.start())

        for half in range(2):
            for q in range(4):
                rows = slice(q * B, (q + 1) * B)
                for part in range(2):
                    block = half * 2 + part
                    index = cbuf[z, rows, block * B:(block + 1) * B].astype(jnp.int32)
                    sc[0, block, rows, :] = lookup(cos_levels, index).astype(BF16)
                    sc[1, block, rows, :] = lookup(sin_levels, index).astype(BF16)
            for kind in range(2):
                tre, tim = [], []
                for r in range(4):
                    data = jnp.concatenate([wide(a, kind, 0, half, r), wide(a, kind, 1, half, r)], axis=0)
                    got = jnp.dot(right_ref[r], data, preferred_element_type=F32).astype(BF16)
                    tre.append(got[:B])
                    tim.append(got[B:])
                xre, xim = join4(tre, tim)
                for q in range(4):
                    rows = slice(q * B, (q + 1) * B)
                    for part in range(2):
                        block = half * 2 + part
                        cols = slice(part * B, (part + 1) * B)
                        cre, cim = sc[0, block, rows, :], sc[1, block, rows, :]
                        gre, gim = xre[q][:, cols], xim[q][:, cols]
                        rr, ii, ri, ir = gre * cre, gim * cim, gre * cim, gim * cre
                        nre, nim = (rr - ii, ri + ir) if kind == 0 else (rr + ii, ir - ri)
                        u[new, kind, 0, block, rows, :] = nre
                        u[new, kind, 1, block, rows, :] = nim
        return carry

    lax.fori_loop(0, steps, step, 0)

    for q in range(2):
        for j in range(2):
            for s in range(4):
                for k in range(2):
                    for p in range(2):
                        pad[q, j, s, k, p, 0:8, :] = jnp.zeros((8, B), F32)
                        pad[q, j, s, k, p, 280:288, :] = jnp.zeros((8, B), F32)
    hand_plane(1)

    def gather_plane(q):
        for j in range(2):
            for k in range(2):
                for p in range(2):
                    pad[q, j, 0, k, p, 8:280, :] = u[q, k, p, 2 * core + j, window(j, own[j]), :].astype(F32)
        for n in range(3):
            for j in range(2):
                hand(q, j, n).wait_recv()
                for k in range(2):
                    for p in range(2):
                        pad[q, j, n + 1, k, p, 8:280, :] = raw[q, j, n, k, p].astype(F32)

    def weight(d, j):
        return (1, 8, 4, 2)[(d - j) % 4]

    flip_1 = [[(own[d] + bits(v, 0)[d]) % 2 for d in range(2)] for v in range(4)]
    slot_1 = [[sum(flip_1[v][d] * weight(d, j) for d in range(2)) for j in range(2)] for v in range(4)]

    def produce(q, g):
        def body(n, carry):
            theirs = bits(0, n)
            flip_2 = [(own[d] + theirs[d]) % 2 for d in (2, 3)]
            slot_2 = [sum(flip_2[d - 2] * weight(d, j) for d in (2, 3)) for j in range(2)]
            for v in range(4):
                for j in range(2):
                    row = pl.multiple_of(n * second_stride + v * first_stride + own[j] * 16, 16)
                    slot = slot_2[j] + slot_1[v][j]
                    for l in range(PER):
                        h = g * PER + l - LAG
                        total = None
                        for s in range(4):
                            for p in range(2):
                                left = pad[q, j, s, 0, p, pl.ds(row + (8 - h), 16), :]
                                right = pad[q, j, s, 1, p, pl.ds(row + (8 + h), 16), :]
                                term = left * right
                                total = term if total is None else total + term
                        buf[q, g, j, slot, l] = total.astype(BF16)
            return carry
        lax.fori_loop(0, 4, body, 0)

    recv = (None, r1, r2, r3)

    def copy(q, g, j, t):
        half = 16 >> t
        return pltpu.make_async_remote_copy(
            src_ref=buf.at[q, g, j, pl.ds(half, half)], dst_ref=recv[t].at[q, g, j],
            send_sem=ssem.at[q, g, j, t - 1], recv_sem=rsem.at[q, g, j, t - 1],
            device_id=(depth, near[(j + t) % 4]), device_id_type=MESH)

    def last(q, g, j, slot, who, place):
        part = 2 * core + j
        return pltpu.make_async_remote_copy(
            src_ref=buf.at[q, g, j, slot], dst_ref=(fa, fb)[place].at[g, part],
            send_sem=fsend.at[q, g, j, slot], recv_sem=frecv.at[g, part, place],
            device_id=who, device_id_type=MESH)

    def sends_last(q, g, j, act):
        owner = first_plane + q

        @pl.when(own[j] == yh)
        def _():
            act(last(q, g, j, 1, (owner, near[j]), 0))

        @pl.when(jnp.logical_and(own[j] == yh, core != q))
        def _():
            act(last(q, g, j, 0, sibling, 1))

        @pl.when(own[j] != yh)
        def _():
            act(last(q, g, j, 0, (owner, far), 0))
            act(last(q, g, j, 1, (owner, far_near[j]), 1))

    def arrive(q, g, j, t):
        copy(q, g, j, t).wait_recv()
        half = 16 >> t

        def body(n, carry):
            for k in (half - 1 - 2 * n, half - 2 - 2 * n):
                buf[q, g, j, k] = buf[q, g, j, k] + recv[t][q, g, j, k]
            return carry
        lax.fori_loop(0, half // 2, body, 0)
        if t < 3:
            copy(q, g, j, t + 1).start()
        else:
            sends_last(q, g, j, lambda c: c.start())

    def came(g, i, place):
        pltpu.make_async_remote_copy(
            src_ref=buf.at[0, g, 0, 0], dst_ref=(fa, fb)[place].at[g, i],
            send_sem=fsend.at[0, g, 0, 0], recv_sem=frecv.at[g, i, place],
            device_id=sibling, device_id_type=MESH).wait_recv()

    def finish(g, i):
        came(g, i, 0)
        put = (slice(g * PER, (g + 1) * PER), slice(None), slice(i * B, (i + 1) * B))
        kept = jnp.logical_and(at_home[i], core == i // 2)

        @pl.when(kept)
        def _():
            out[put] = (buf[core, g, i % 2, 0].astype(F32) + fa[g, i].astype(F32)) * factor

        @pl.when(jnp.logical_not(kept))
        def _():
            came(g, i, 1)
            out[put] = (fa[g, i].astype(F32) + fb[g, i].astype(F32)) * factor

    events = [(q, g) for q in range(2) for g in range(GROUPS)]
    for e, (q, g) in enumerate(events):
        if g == 0:
            gather_plane(q)
        produce(q, g)
        for j in range(2):
            copy(q, g, j, 1).start()
    for t in (1, 2, 3):
        for event in events:
            for j in range(2):
                arrive(*event, j, t)
    for g in range(GROUPS):
        for i in range(4):
            finish(g, i)
    for q in range(2):
        for j in range(2):
            for n in range(3):
                hand(q, j, n).wait_send()
            for g in range(GROUPS):
                for t in (1, 2, 3):
                    copy(q, g, j, t).wait_send()
                sends_last(q, g, j, lambda c: c.wait_send())
    for way in range(2):
        codes_to(2, way, sibling).wait_send()
    mean_to(2, sibling).wait_send()

    @pl.when(section == 0)
    def _():
        section_codes(lambda c: c.wait_send())
        for s in range(2):
            mean_to(s, beside[0][s]).wait_send()


def migrate(src, rec, model, table, anchors, right, left, factor):
    vmem = pl.BlockSpec(memory_space=pltpu.VMEM)
    hbm = pl.BlockSpec(memory_space=pl.ANY)
    smem = pl.BlockSpec(memory_space=pltpu.SMEM)
    dma = pltpu.SemaphoreType.DMA
    strip = (PER, 16, B)
    return pl.pallas_call(
        functools.partial(migrate_kernel, factor),
        out_shape=jax.ShapeDtypeStruct((LAGS, 16, N), F32),
        in_specs=[hbm, hbm, hbm, smem, smem, vmem, vmem],
        out_specs=vmem,
        scratch_shapes=[
            pltpu.VMEM((2, 2, N, N), jnp.int32),
            pltpu.VMEM((2, N, N), BF16),
            pltpu.VMEM((2, 8, B), F32),
            dma((2, 2)),
            pltpu.VMEM((3, 2, 2, 4, N, B), BF16),
            pltpu.VMEM((2, 2, 4, N, B), BF16),
            pltpu.VMEM((4, N, N), BF16),
            pltpu.VMEM((4, 8, B), F32),
            pltpu.VMEM((2, 3, 3 * B, B), BF16),
            pltpu.VMEM((2, 4, N, B), BF16),
            pltpu.VMEM((2, 2, 3, 2, 2, 272, B), BF16),
            pltpu.VMEM((2, 2, 4, 2, 2, 288, B), F32),
            pltpu.VMEM((2, GROUPS, 2, 16) + strip, BF16),
            pltpu.VMEM((2, GROUPS, 2, 8) + strip, BF16),
            pltpu.VMEM((2, GROUPS, 2, 4) + strip, BF16),
            pltpu.VMEM((2, GROUPS, 2, 2) + strip, BF16),
            pltpu.VMEM((GROUPS, 4) + strip, BF16),
            pltpu.VMEM((GROUPS, 4) + strip, BF16),
            dma((2, 4)), dma((3, 2)), dma((4, 2)), dma((3,)), dma((4,)),
            dma((2, 2, 3)), dma((2, 2, 3)),
            dma((2, GROUPS, 2, 3)), dma((2, GROUPS, 2, 3)), dma((2, GROUPS, 2, 2)), dma((GROUPS, 4, 2)),
        ],
        compiler_params=pltpu.CompilerParams(
            collective_id=1, has_side_effects=True, vmem_limit_bytes=62 * 1024 * 1024),
        name="migrate",
    )(src, rec, model, table, anchors, right, left)


def shards(source_top, receiver_top, slowness_codes, slowness_table, anchors):
    right, left = butterfly_matrices()
    right = jnp.asarray(right, BF16)
    left = jnp.asarray(left, BF16)
    image = migrate(
        source_top, receiver_top, slowness_codes, slowness_table, anchors, right, left, 1.0 / math.sqrt(128.0))
    return image[None]


def solution(mesh):
    return jax.shard_map(
        shards,
        mesh=mesh,
        in_specs=(
            P(None, "freq", None, None, None),
            P(None, "freq", None, None, None),
            P("depth", None, None),
            P(),
            P(),
        ),
        out_specs=P("depth", None, "freq", None),
        check_vma=False,
    )
```

```python
import functools
import math

import jax
import jax.numpy as jnp
import numpy as np
from jax import lax
from jax.experimental import pallas as pl
from jax.experimental.pallas import tpu as pltpu
from jax.sharding import PartitionSpec as P

LAG = 7
LAGS = 2 * LAG + 1
N = 512
B = 128
GROUPS = 3
PER = LAGS // GROUPS
MESH = pl.DeviceIdType.MESH
F32 = jnp.float32
BF16 = jnp.bfloat16


def butterfly_matrices():
    j = np.arange(B)[:, None]
    k = np.arange(B)[None, :]
    mats = []
    for wave in (4 * k, 4 * k + 1, 4 * k + 2, -(4 * k + 1)):
        angle = 2.0 * np.pi * ((j * wave) % N) / N
        c = np.cos(angle) / math.sqrt(N)
        s = np.sin(angle) / math.sqrt(N)
        mats.append(np.block([[c, -s], [s, c]]))
    right = np.stack(mats)
    return right, np.swapaxes(right, 1, 2)


def even_poly(first, terms, top, samples=400):
    q = (np.cos(np.pi * (np.arange(samples) + 0.5) / samples) + 1.0) * 0.5 * top
    r = np.sqrt(q)
    want = np.cos(r) if first == 0 else np.sin(r) / r
    fit = np.polynomial.Chebyshev.fit(q, want, terms, domain=[0, top])
    return [float(v) for v in fit.convert(kind=np.polynomial.Polynomial).coef]


COS_Q = even_poly(0, 6, 14.0)
SIN_Q = even_poly(1, 5, 14.0)


def horner(coefs, q):
    value = coefs[-1] * q + coefs[-2]
    for c in coefs[-3::-1]:
        value = value * q + c
    return value


def split4(re, im):
    er, ei, dr, di = re[0] + re[2], im[0] + im[2], re[0] - re[2], im[0] - im[2]
    fr, fi, gr, gi = re[1] + re[3], im[1] + im[3], re[1] - re[3], im[1] - im[3]
    return (er + fr, dr + gi, er - fr, dr - gi), (ei + fi, di - gr, ei - fi, di + gr)


def join4(re, im):
    er, ei, dr, di = re[0] + re[2], im[0] + im[2], re[0] - re[2], im[0] - im[2]
    fr, fi, gr, gi = re[1] + re[3], im[1] + im[3], re[1] - re[3], im[1] - im[3]
    return (er + fr, dr - gi, er - fr, dr + gi), (ei + fi, di + gr, ei - fi, di - gr)


def level_row(table):
    lane = lax.broadcasted_iota(jnp.int32, (8, B), 1)
    levels = jnp.zeros((8, B), F32)
    for k in range(32):
        levels = jnp.where(lane == k, table[k], levels)
    return levels


TAKE = lax.GatherDimensionNumbers(
    offset_dims=(), collapsed_slice_dims=(1,), start_index_map=(1,),
    operand_batching_dims=(0,), start_indices_batching_dims=(0,))


def lookup(values, index):
    return lax.gather(
        jnp.tile(values, (index.shape[0] // 8, 1)), index[..., None], TAKE, (1, 1),
        mode=lax.GatherScatterMode.PROMISE_IN_BOUNDS)


def migrate_kernel(
    factor, src, rec, model, table, anchors, right_in, left_in, out,
    right_ref, left_ref, msem, rawc, win, means, wsem, u, a, cbuf, mbuf, ph, sc, raw, pad, buf, r1, r2, r3, fa, fb,
    tsem, csend, crecv, msend, mrecv, esend, erecv, ssem, rsem, fsend, frecv,
):
    depth = lax.axis_index("depth")
    freq = lax.axis_index("freq")
    core = depth % 2
    section = depth // 2
    other = depth + 1 - 2 * core
    x, z, yh = freq % 4, (freq // 4) % 4, freq // 16
    first_plane = section * 2
    steps = first_plane + 2
    ring = (
        freq - x + (x + 1 - 2 * (x % 2)),
        freq - x + (3 - x),
        freq - 4 * z + 4 * (z + 1 - 2 * (z % 2)),
        freq - 4 * z + 4 * (3 - z),
    )
    far = freq - 16 * yh + 16 * (1 - yh)
    far_ring = [r - 16 * yh + 16 * (1 - yh) for r in ring]
    sibling = (other, freq)
    beside = [[(2 * (1 - section) + s, freq) for s in range(2)], [(2 * (1 - section) + s, far) for s in range(2)]]

    def bits(ix, iz):
        return [((ix + 1) // 2) % 2, ix // 2, ((iz + 1) // 2) % 2, iz // 2]

    mine = bits(x, z)
    at_home = [mine[i] == yh for i in range(4)]
    first = x + core * (z - x)
    second = z + core * (x - z)
    near = [ring[d] + core * (ring[(d + 2) % 4] - ring[d]) for d in range(4)]
    far_near = [r - 16 * yh + 16 * (1 - yh) for r in near]
    own = bits(first, second)
    first_stride = 16 + 48 * core
    second_stride = 64 - 48 * core

    loads = []
    for qx in range(2):
        for qy in range(2):
            loads.append(pltpu.make_async_copy(
                model.at[0, pl.ds(qx * N, N), pl.ds(qy * N, N)], rawc.at[qx, qy], wsem.at[qx, qy]))
    for copy_in in loads:
        copy_in.start()
    tops = []
    for kind, top in enumerate((src, rec)):
        for q in range(4):
            tops.append(pltpu.make_async_copy(
                top.at[core, 0, :, :, pl.ds(q * B, B)], u.at[2, kind, :, q], tsem.at[kind, q]))
    tops.append(pltpu.make_async_copy(left_in, left_ref, msem.at[0]))
    tops.append(pltpu.make_async_copy(right_in, right_ref, msem.at[1]))
    for copy_in in tops:
        copy_in.start()

    def half_rows(way):
        return pl.ds(way * (N // 2), N // 2)

    barrier = pltpu.get_barrier_semaphore()
    peers = [sibling, (depth, far), (other, far)] + beside[0] + beside[1]
    for i in range(4):
        peers += [(depth, ring[i]), (other, ring[i]), (depth, far_ring[i]), (other, far_ring[i])]
    for who in peers:
        pl.semaphore_signal(barrier, inc=1, device_id=who, device_id_type=MESH)

    position = freq.astype(F32)
    angular = math.pi * (0.45 + 0.5 * (position + 0.5) / 32.0)
    levels = level_row(table)

    for copy_in in loads:
        copy_in.wait()
    for s in range(2):
        qx = anchors[s, 0] // N
        qy = anchors[s, 1] // N

        def rows_of(n, total):
            take = pl.ds(pl.multiple_of(n * 32, 32), 32)
            for q in range(4):
                index = rawc[qx, qy, take, q * B:(q + 1) * B]
                win[s, take, q * B:(q + 1) * B] = index.astype(F32).astype(BF16)
                got = lookup(levels, index)
                total = total + (got[0:8] + got[8:16]) + (got[16:24] + got[24:32])
            return total

        total = lax.fori_loop(0, N // 32, rows_of, jnp.zeros((8, B), F32))
        means[s] = jnp.full((8, B), jnp.sum(total) * (1.0 / (N * N)), F32)

    pl.semaphore_wait(barrier, len(peers))

    def codes_to(n, way, who):
        shot = (0, 1, 1 - core)[n]
        return pltpu.make_async_remote_copy(
            src_ref=win.at[shot, half_rows(way)], dst_ref=cbuf.at[depth, half_rows(way)],
            send_sem=csend.at[n, way], recv_sem=crecv.at[depth, way],
            device_id=who, device_id_type=MESH)

    def mean_to(n, who):
        shot = (0, 1, 1 - core)[n]
        return pltpu.make_async_remote_copy(
            src_ref=means.at[shot], dst_ref=mbuf.at[depth],
            send_sem=msend.at[n], recv_sem=mrecv.at[depth],
            device_id=who, device_id_type=MESH)

    def section_codes(act):
        for s in range(2):
            for way in range(2):
                act(codes_to(s, way, beside[way][s]))

    for way in range(2):
        pltpu.make_async_copy(
            win.at[core, half_rows(way)], cbuf.at[depth, half_rows(way)], crecv.at[depth, way]).start()
    mbuf[depth] = means[core]

    mean_to(2, sibling).start()

    @pl.when(section == 0)
    def _():
        for s in range(2):
            mean_to(s, beside[0][s]).start()

    for way in range(2):
        codes_to(2, way, sibling).start()

    @pl.when(jnp.logical_and(section == 0, core == 0))
    def _():
        section_codes(lambda c: c.start())

    def window(i, half):
        return pl.ds(pl.multiple_of(half * 240, 16), 272)

    def hand(q, j, n):
        part = (2 * (1 - core) + j, 2 * core + j, 2 * (1 - core) + j)[n]
        half = (own[2 + j], 1 - own[j], 1 - own[2 + j])[n]
        who = (sibling, (depth, near[j]), (other, near[2 + j]))[n]
        return pltpu.make_async_remote_copy(
            src_ref=u.at[q, :, :, part, window(part, half)], dst_ref=raw.at[q, j, n],
            send_sem=esend.at[q, j, n], recv_sem=erecv.at[q, j, n],
            device_id=who, device_id_type=MESH)

    def hand_plane(q):
        for n in (2, 1, 0):
            for j in range(2):
                hand(q, j, n).start()

    for copy_in in tops:
        copy_in.wait()

    def step(plane, carry):
        z = plane
        new = jnp.where(z < first_plane, 2, z - first_plane)
        old = jnp.where(z <= first_plane, 2, z - 1 - first_plane)

        @pl.when(z != depth)
        def _():
            pltpu.make_async_copy(means.at[0], mbuf.at[z], mrecv.at[z]).wait()

        base = mbuf[z, 0:1, :]
        turn = angular * base
        turn_sq = turn * turn
        angle = angular * (levels - base)
        squared = angle * angle
        cos_levels = horner(COS_Q, squared)
        sin_levels = angle * horner(SIN_Q, squared)

        def operators(n):
            rows = n * 96
            k = rows + lax.broadcasted_iota(jnp.int32, (96, B), 0)
            kx = (k % B) * 4 + k // B
            kx = jnp.where(kx < N // 2, kx, kx - N).astype(F32) * (2.0 * math.pi / N)
            left_q = turn_sq - kx * kx
            for ry in range(3):
                ky = lax.broadcasted_iota(jnp.int32, (1, B), 1) * 4 + ry
                ky = jnp.where(ky < N // 2, ky, ky - N).astype(F32) * (2.0 * math.pi / N)
                q = left_q - ky * ky
                size = jnp.maximum(jnp.abs(q), 1e-30)
                root = size * lax.rsqrt(size)
                travels = q >= 0.0
                put = slice(rows, rows + 96)
                ph[0, ry, put, :] = jnp.where(travels, horner(COS_Q, q), jnp.exp(-root)).astype(BF16)
                ph[1, ry, put, :] = jnp.where(travels, root * horner(SIN_Q, q), 0.0).astype(BF16)

        def wide(ref, kind, p, half, block):
            rows = slice(block * B, (block + 1) * B)
            return jnp.concatenate([ref[kind, p, half * 2, rows, :], ref[kind, p, half * 2 + 1, rows, :]], axis=1)

        def put_wide(ref, kind, p, half, block, value):
            rows = slice(block * B, (block + 1) * B)
            ref[kind, p, half * 2, rows, :] = value[:, :B]
            ref[kind, p, half * 2 + 1, rows, :] = value[:, B:]

        def wide_u(kind, p, half, block):
            rows = slice(block * B, (block + 1) * B)
            return jnp.concatenate([u[old, kind, p, half * 2, rows, :], u[old, kind, p, half * 2 + 1, rows, :]], axis=1)

        def forward_x(n, carry):
            kind, half = n % 2, n // 2
            re = [wide_u(kind, 0, half, q) for q in range(4)]
            im = [wide_u(kind, 1, half, q) for q in range(4)]
            sre, sim = split4(re, im)
            for r in range(4):
                got = jnp.dot(left_ref[r], jnp.concatenate([sre[r], sim[r]], axis=0),
                              preferred_element_type=F32).astype(BF16)
                put_wide(a, kind, 0, half, r, got[:B])
                put_wide(a, kind, 1, half, r, got[B:])
            return carry

        @pl.when(z == first_plane + 1)
        def _():
            hand_plane(0)

        for n in range(4):
            forward_x(n, 0)
            operators(n)

        def along_y(rx, carry):
            prow = pl.ds(pl.multiple_of(jnp.where(rx == 3, 1, rx) * B, B), B)
            rows = pl.ds(pl.multiple_of(rx * B, B), B)
            sums_of = [split4([a[k, 0, q, rows, :] for q in range(4)], [a[k, 1, q, rows, :] for q in range(4)])
                       for k in range(2)]
            tre, tim = ([], []), ([], [])
            for r in range(4):
                data = jnp.concatenate(
                    [jnp.concatenate([sums_of[k][0][r], sums_of[k][1][r]], axis=1) for k in range(2)], axis=0)
                got = jnp.dot(data, right_ref[r], preferred_element_type=F32).astype(BF16)
                py = 1 if r == 3 else r
                pre, pim = ph[0, py, prow, :], ph[1, py, prow, :]
                turned = []
                for k in range(2):
                    gre, gim = got[k * B:(k + 1) * B, :B], got[k * B:(k + 1) * B, B:]
                    rr, ii, ri, ir = gre * pre, gim * pim, gre * pim, gim * pre
                    nre, nim = (rr - ii, ri + ir) if k == 0 else (rr + ii, ir - ri)
                    turned.append(jnp.concatenate([nre, nim], axis=1))
                back = jnp.dot(jnp.concatenate(turned, axis=0), left_ref[r], preferred_element_type=F32).astype(BF16)
                for k in range(2):
                    tre[k].append(back[k * B:(k + 1) * B, :B])
                    tim[k].append(back[k * B:(k + 1) * B, B:])
            for k in range(2):
                cre, cim = join4(tre[k], tim[k])
                for q in range(4):
                    a[k, 0, q, rows, :] = cre[q]
                    a[k, 1, q, rows, :] = cim[q]
            return carry

        lax.fori_loop(0, 4, along_y, 0, unroll=4)

        for way in range(2):
            pltpu.make_async_copy(
                win.at[0, half_rows(way)], cbuf.at[z, half_rows(way)], crecv.at[z, way]).wait()

        @pl.when(jnp.logical_and(z == 0, jnp.logical_and(section == 0, core == 1)))
        def _():
            section_codes(lambda c: c.start())

        for half in range(2):
            for q in range(4):
                rows = slice(q * B, (q + 1) * B)
                for part in range(2):
                    block = half * 2 + part
                    index = cbuf[z, rows, block * B:(block + 1) * B].astype(jnp.int32)
                    sc[0, block, rows, :] = lookup(cos_levels, index).astype(BF16)
                    sc[1, block, rows, :] = lookup(sin_levels, index).astype(BF16)
            for kind in range(2):
                tre, tim = [], []
                for r in range(4):
                    data = jnp.concatenate([wide(a, kind, 0, half, r), wide(a, kind, 1, half, r)], axis=0)
                    got = jnp.dot(right_ref[r], data, preferred_element_type=F32).astype(BF16)
                    tre.append(got[:B])
                    tim.append(got[B:])
                xre, xim = join4(tre, tim)
                for q in range(4):
                    rows = slice(q * B, (q + 1) * B)
                    for part in range(2):
                        block = half * 2 + part
                        cols = slice(part * B, (part + 1) * B)
                        cre, cim = sc[0, block, rows, :], sc[1, block, rows, :]
                        gre, gim = xre[q][:, cols], xim[q][:, cols]
                        rr, ii, ri, ir = gre * cre, gim * cim, gre * cim, gim * cre
                        nre, nim = (rr - ii, ri + ir) if kind == 0 else (rr + ii, ir - ri)
                        u[new, kind, 0, block, rows, :] = nre
                        u[new, kind, 1, block, rows, :] = nim
        return carry

    lax.fori_loop(0, steps, step, 0)

    for q in range(2):
        for j in range(2):
            for s in range(4):
                for k in range(2):
                    for p in range(2):
                        pad[q, j, s, k, p, 0:8, :] = jnp.zeros((8, B), F32)
                        pad[q, j, s, k, p, 280:288, :] = jnp.zeros((8, B), F32)
    hand_plane(1)

    def gather_plane(q):
        for j in range(2):
            for k in range(2):
                for p in range(2):
                    pad[q, j, 0, k, p, 8:280, :] = u[q, k, p, 2 * core + j, window(j, own[j]), :].astype(F32)
        for n in range(3):
            for j in range(2):
                hand(q, j, n).wait_recv()
                for k in range(2):
                    for p in range(2):
                        pad[q, j, n + 1, k, p, 8:280, :] = raw[q, j, n, k, p].astype(F32)

    def weight(d, j):
        return (1, 8, 4, 2)[(d - j) % 4]

    flip_1 = [[(own[d] + bits(v, 0)[d]) % 2 for d in range(2)] for v in range(4)]
    slot_1 = [[sum(flip_1[v][d] * weight(d, j) for d in range(2)) for j in range(2)] for v in range(4)]

    def produce(q, g):
        def body(n, carry):
            theirs = bits(0, n)
            flip_2 = [(own[d] + theirs[d]) % 2 for d in (2, 3)]
            slot_2 = [sum(flip_2[d - 2] * weight(d, j) for d in (2, 3)) for j in range(2)]
            for v in range(4):
                for j in range(2):
                    row = pl.multiple_of(n * second_stride + v * first_stride + own[j] * 16, 16)
                    slot = slot_2[j] + slot_1[v][j]
                    for l in range(PER):
                        h = g * PER + l - LAG
                        total = None
                        for s in range(4):
                            for p in range(2):
                                left = pad[q, j, s, 0, p, pl.ds(row + (8 - h), 16), :]
                                right = pad[q, j, s, 1, p, pl.ds(row + (8 + h), 16), :]
                                term = left * right
                                total = term if total is None else total + term
                        buf[q, g, j, slot, l] = total.astype(BF16)
            return carry
        lax.fori_loop(0, 4, body, 0)

    recv = (None, r1, r2, r3)

    def copy(q, g, j, t):
        half = 16 >> t
        return pltpu.make_async_remote_copy(
            src_ref=buf.at[q, g, j, pl.ds(half, half)], dst_ref=recv[t].at[q, g, j],
            send_sem=ssem.at[q, g, j, t - 1], recv_sem=rsem.at[q, g, j, t - 1],
            device_id=(depth, near[(j + t) % 4]), device_id_type=MESH)

    def last(q, g, j, slot, who, place):
        part = 2 * core + j
        return pltpu.make_async_remote_copy(
            src_ref=buf.at[q, g, j, slot], dst_ref=(fa, fb)[place].at[g, part],
            send_sem=fsend.at[q, g, j, slot], recv_sem=frecv.at[g, part, place],
            device_id=who, device_id_type=MESH)

    def sends_last(q, g, j, act):
        owner = first_plane + q

        @pl.when(own[j] == yh)
        def _():
            act(last(q, g, j, 1, (owner, near[j]), 0))

        @pl.when(jnp.logical_and(own[j] == yh, core != q))
        def _():
            act(last(q, g, j, 0, sibling, 1))

        @pl.when(own[j] != yh)
        def _():
            act(last(q, g, j, 0, (owner, far), 0))
            act(last(q, g, j, 1, (owner, far_near[j]), 1))

    def arrive(q, g, j, t):
        copy(q, g, j, t).wait_recv()
        half = 16 >> t

        def body(n, carry):
            for k in (half - 1 - 2 * n, half - 2 - 2 * n):
                buf[q, g, j, k] = buf[q, g, j, k] + recv[t][q, g, j, k]
            return carry
        lax.fori_loop(0, half // 2, body, 0, unroll=True)
        if t < 3:
            copy(q, g, j, t + 1).start()
        else:
            sends_last(q, g, j, lambda c: c.start())

    def came(g, i, place):
        pltpu.make_async_remote_copy(
            src_ref=buf.at[0, g, 0, 0], dst_ref=(fa, fb)[place].at[g, i],
            send_sem=fsend.at[0, g, 0, 0], recv_sem=frecv.at[g, i, place],
            device_id=sibling, device_id_type=MESH).wait_recv()

    def finish(g, i):
        came(g, i, 0)
        put = (slice(g * PER, (g + 1) * PER), slice(None), slice(i * B, (i + 1) * B))
        kept = jnp.logical_and(at_home[i], core == i // 2)

        @pl.when(kept)
        def _():
            out[put] = (buf[core, g, i % 2, 0].astype(F32) + fa[g, i].astype(F32)) * factor

        @pl.when(jnp.logical_not(kept))
        def _():
            came(g, i, 1)
            out[put] = (fa[g, i].astype(F32) + fb[g, i].astype(F32)) * factor

    events = [(q, g) for q in range(2) for g in range(GROUPS)]
    for e, (q, g) in enumerate(events):
        if g == 0:
            gather_plane(q)
        produce(q, g)
        for j in range(2):
            copy(q, g, j, 1).start()
    for t in (1, 2, 3):
        for event in events:
            for j in range(2):
                arrive(*event, j, t)
    for g in range(GROUPS):
        for i in range(4):
            finish(g, i)
    for q in range(2):
        for j in range(2):
            for n in range(3):
                hand(q, j, n).wait_send()
            for g in range(GROUPS):
                for t in (1, 2, 3):
                    copy(q, g, j, t).wait_send()
                sends_last(q, g, j, lambda c: c.wait_send())
    for way in range(2):
        codes_to(2, way, sibling).wait_send()
    mean_to(2, sibling).wait_send()

    @pl.when(section == 0)
    def _():
        section_codes(lambda c: c.wait_send())
        for s in range(2):
            mean_to(s, beside[0][s]).wait_send()


def migrate(src, rec, model, table, anchors, right, left, factor):
    vmem = pl.BlockSpec(memory_space=pltpu.VMEM)
    hbm = pl.BlockSpec(memory_space=pltpu.HBM)
    smem = pl.BlockSpec(memory_space=pltpu.SMEM)
    dma = pltpu.SemaphoreType.DMA
    strip = (PER, 16, B)
    return pl.pallas_call(
        functools.partial(migrate_kernel, factor),
        out_shape=jax.ShapeDtypeStruct((LAGS, 16, N), F32),
        in_specs=[hbm, hbm, hbm, smem, smem, hbm, hbm],
        out_specs=vmem,
        scratch_shapes=[
            pltpu.VMEM((4, 2 * B, 2 * B), BF16),
            pltpu.VMEM((4, 2 * B, 2 * B), BF16),
            dma((2,)),
            pltpu.VMEM((2, 2, N, N), jnp.int32),
            pltpu.VMEM((2, N, N), BF16),
            pltpu.VMEM((2, 8, B), F32),
            dma((2, 2)),
            pltpu.VMEM((3, 2, 2, 4, N, B), BF16),
            pltpu.VMEM((2, 2, 4, N, B), BF16),
            pltpu.VMEM((4, N, N), BF16),
            pltpu.VMEM((4, 8, B), F32),
            pltpu.VMEM((2, 3, 3 * B, B), BF16),
            pltpu.VMEM((2, 4, N, B), BF16),
            pltpu.VMEM((2, 2, 3, 2, 2, 272, B), BF16),
            pltpu.VMEM((2, 2, 4, 2, 2, 288, B), F32),
            pltpu.VMEM((2, GROUPS, 2, 16) + strip, BF16),
            pltpu.VMEM((2, GROUPS, 2, 8) + strip, BF16),
            pltpu.VMEM((2, GROUPS, 2, 4) + strip, BF16),
            pltpu.VMEM((2, GROUPS, 2, 2) + strip, BF16),
            pltpu.VMEM((GROUPS, 4) + strip, BF16),
            pltpu.VMEM((GROUPS, 4) + strip, BF16),
            dma((2, 4)), dma((3, 2)), dma((4, 2)), dma((3,)), dma((4,)),
            dma((2, 2, 3)), dma((2, 2, 3)),
            dma((2, GROUPS, 2, 3)), dma((2, GROUPS, 2, 3)), dma((2, GROUPS, 2, 2)), dma((GROUPS, 4, 2)),
        ],
        compiler_params=pltpu.CompilerParams(
            collective_id=1, has_side_effects=True, vmem_limit_bytes=62 * 1024 * 1024),
        name="migrate",
    )(src, rec, model, table, anchors, right, left)


def shards(source_top, receiver_top, slowness_codes, slowness_table, anchors):
    right, left = butterfly_matrices()
    right = jnp.asarray(right, BF16)
    left = jnp.asarray(left, BF16)
    image = migrate(
        source_top, receiver_top, slowness_codes, slowness_table, anchors, right, left, 1.0 / math.sqrt(128.0))
    return image[None]


def solution(mesh):
    return jax.shard_map(
        shards,
        mesh=mesh,
        in_specs=(
            P(None, "freq", None, None, None),
            P(None, "freq", None, None, None),
            P("depth", None, None),
            P(),
            P(),
        ),
        out_specs=P("depth", None, "freq", None),
        check_vma=False,
    )
```
